128 devices in a mesh: row: 16 (over x, y), col: 8 (over z, core).
Axes of the slice: x: 4, y: 4, z: 4, core: 2. Of those that a mesh axis runs over, the one named last changes fastest.
Arguments:
- states: bfloat16 [128, 2, 8, 5376], P(None, None, None, 'row'), may hold values from -6 to 6
- subject_pos: int32 [128, 2], replicated, may hold values from 0 to 7
- gate_weight: bfloat16 [5376, 8, 2688], P('row', 'col'), may hold values from -0.078125 to 0.078125
- up_weight: bfloat16 [5376, 8, 2688], P('row', 'col'), may hold values from -0.078125 to 0.078125
- down_weight: bfloat16 [16, 8, 168, 5376], P('row', 'col'), may hold values from -0.0390625 to 0.0390625
- covariance: float32 [21504, 8, 2688], P('row', 'col'), as said below
- targets: float32 [5376, 128], P(('row', 'col')), may hold values from -24 to 24
Outputs:
- update: bfloat16 [16, 8, 168, 5376], P('row', 'col')
The draws below stay inside these ranges and needn't reach their ends.
Inputs may be any that keep to these rules, and one draw needn't show every extreme that they name: `covariance`: read as an 21504 x 21504 matrix (entry (i, b, a * 168 + j) in column a * 8 * 168 + b * 168 + j), it is symmetric and positive definite.
All inputs are finite; a program needn't handle non-finite values.
Results may differ from the reference program's by a relative error of at most 0.0016.
Values sent between devices are 32-bit elements; how exact they have to be, the bound alone decides.
A program may use at most 128 MiB of HBM per device.

```python
import math
import jax
import jax.numpy as jnp
from jax import lax

D = 5376
FF = 21504
EDITS = 128
PREF = 2
SEQ = 8
ITERS = 2
PIECE = 168
N_ROW = 16
N_COL = 8


def draw_covariance(key, part):
    first = jax.random.fold_in(key, 11)
    second = jax.random.fold_in(key, 23)
    noise = jax.random.normal(first, (FF, FF), jnp.float32)
    diagonal = jnp.exp(jax.random.uniform(second, (FF,), jnp.float32, math.log(1.2), math.log(4.0)))
    spread = 0.4 / math.sqrt(2.0 * FF)
    matrix = (noise + noise.T) * spread
    places = jnp.arange(FF)
    matrix = matrix.at[places, places].add(diagonal)
    stored = matrix.reshape(FF, N_ROW, N_COL, PIECE).transpose(0, 2, 1, 3)
    return stored.reshape(FF, N_COL, N_ROW * PIECE)


def with_ends(entries, rng, least, high):
    longest = entries.shape.index(max(entries.shape))
    spots = []
    for shift in (0, 1):
        where = [jax.random.randint(jax.random.fold_in(rng, axis), (), 0, length) for axis, length in enumerate(entries.shape)]
        where[longest] = (where[longest] + shift) % entries.shape[longest]
        spots.append(tuple(where))
    return entries.at[spots[0]].set(least).at[spots[1]].set(high)


def block_levels(key, extent, pieces, low, high):
    level, own = 1.0, jax.random.fold_in(key, 6)
    for dim, parts in pieces:
        draws = jnp.exp(jax.random.uniform(jax.random.fold_in(own, dim), (parts,), jnp.float32, low / len(pieces), high / len(pieces)))
        level = level * jnp.repeat(draws, extent[dim] // parts).reshape([-1 if axis == dim else 1 for axis in range(len(extent))])
    return level


def centred(key, shape, deviation, most, shards=(), dtype=jnp.bfloat16):
    result = deviation * jax.random.normal(key, shape, jnp.float32)
    if shards:
        result = result * block_levels(key, shape, shards, -0.22, 0.18)
    return jnp.clip(result, -most, most).astype(dtype)


def setup_inputs(seed: int = 0) -> dict:
    seeds = jax.random.split(jax.random.key(seed), 8)
    return {
        "states": centred(seeds[0], (EDITS, PREF, SEQ, D), 1.0, 6.0, ((3, 16),)),
        "subject_pos": with_ends(jax.random.randint(seeds[1], (EDITS, PREF), 0, SEQ), jax.random.fold_in(seeds[1], 1), 0, SEQ - 1).astype(jnp.int32),
        "gate_weight": centred(seeds[2], (D, N_COL, N_ROW * PIECE), D ** -0.5, 0.078125, ((0, 16), (1, 8))),
        "up_weight": centred(seeds[3], (D, N_COL, N_ROW * PIECE), D ** -0.5, 0.078125, ((0, 16), (1, 8))),
        "down_weight": centred(seeds[4], (N_ROW, N_COL, PIECE, D), FF ** -0.5, 0.0390625, ((0, 16), (1, 8))),
        "covariance": draw_covariance(jax.random.fold_in(seeds[7], 71), 0),
        "targets": centred(seeds[6], (D, EDITS), 4.0, 24.0, ((0, 128),), jnp.float32),
    }


def high_dot(left, right):
    return jnp.dot(left.astype(jnp.float32), right.astype(jnp.float32), precision=lax.Precision.HIGHEST, preferred_element_type=jnp.float32)

def small_solve(matrix, right):
    factor = jnp.linalg.cholesky(matrix)
    return jax.scipy.linalg.cho_solve((factor, True), right)

def symmetric(matrix):
    return 0.5 * (matrix + matrix.T)

def hidden_order(stored, leading):
    return stored.reshape(leading, N_COL, N_ROW, PIECE).transpose(0, 2, 1, 3).reshape(leading, FF)

def reference(states, subject_pos, gate_weight, up_weight, down_weight, covariance, targets):
    index = subject_pos.astype(jnp.int32)[:, :, None, None]
    chosen = jnp.take_along_axis(states, index, axis=2)[:, :, 0, :]
    token_rows = chosen.reshape(EDITS * PREF, D)
    gate = jnp.dot(token_rows.astype(jnp.float32), hidden_order(gate_weight, D).astype(jnp.float32), preferred_element_type=jnp.float32)
    up_value = jnp.dot(token_rows.astype(jnp.float32), hidden_order(up_weight, D).astype(jnp.float32), preferred_element_type=jnp.float32)
    hidden = jax.nn.silu(gate) * up_value
    keys = lax.optimization_barrier(jnp.mean(hidden.reshape(EDITS, PREF, FF), axis=1)).T
    keys_half = keys.astype(jnp.bfloat16)
    current = jnp.dot(down_weight.reshape(FF, D).T.astype(jnp.float32), keys_half.astype(jnp.float32), preferred_element_type=jnp.float32)
    residual_t = targets - current
    matrix = hidden_order(covariance, FF)
    basis = 4.0 / math.sqrt(FF) * keys
    solution = jnp.zeros_like(basis)
    resid = basis
    direction = basis
    norm_now = symmetric(high_dot(resid.T, resid))
    for step in range(ITERS):
        image = high_dot(matrix, direction) + high_dot(basis, high_dot(basis.T, direction))
        curvature = symmetric(high_dot(direction.T, image))
        alpha = small_solve(curvature, norm_now)
        solution = solution + high_dot(direction, alpha)
        resid = resid - high_dot(image, alpha)
        if step + 1 < ITERS:
            norm_next = symmetric(high_dot(resid.T, resid))
            beta = small_solve(norm_now, norm_next)
            direction = resid + high_dot(direction, beta)
            norm_now = norm_next
    update = high_dot(solution, residual_t.T)
    return update.reshape(N_ROW, N_COL, PIECE, D).astype(jnp.bfloat16)
```

```python
import math

import jax
import jax.numpy as jnp
from jax import lax
from jax.experimental import pallas as pl
from jax.experimental.pallas import tpu as pltpu
from jax.sharding import PartitionSpec as P

FF = 21504
D = 5376
PIECE = 168
E = 128
F32 = jnp.float32
BF16 = jnp.bfloat16
HI = lax.Precision.HIGHEST
N_SEM = 112
COV_ROWS = 112
COV_STEPS = 1344 // COV_ROWS
LINES = COV_ROWS * 21


def dot(left, right):
    return lax.dot_general(left, right, (((1,), (0,)), ((), ())), precision=HI, preferred_element_type=F32)


def dot_t(left, right):
    return lax.dot_general(left, right, (((0,), (0,)), ((), ())), precision=HI, preferred_element_type=F32)


def dot_b(left, right):
    return lax.dot_general(left, right, (((1,), (0,)), ((), ())), preferred_element_type=F32)


def dot_tb(left, right):
    return lax.dot_general(left, right, (((0,), (0,)), ((), ())), preferred_element_type=F32)


def halves(value):
    high = value.astype(BF16)
    return high, (value - high.astype(F32)).astype(BF16)


def sym(matrix):
    return 0.5 * (matrix + matrix.T)


def sweep_panel(matrix):
    lane = lax.broadcasted_iota(jnp.int32, (E, E), 1)
    sub = lax.broadcasted_iota(jnp.int32, (E, E), 0)
    lane1 = lax.broadcasted_iota(jnp.int32, (1, E), 1)
    for j in range(8):
        column = matrix[:, j : j + 1]
        row = matrix[j : j + 1, :]
        inv = 1.0 / matrix[j : j + 1, j : j + 1]
        row = jnp.where(lane1 == j, inv, row * inv)
        rest = jnp.where(lane == j, 0.0, matrix) - column * row
        matrix = jnp.where(sub == j, row, rest)
    matrix = jnp.concatenate([matrix[8:], matrix[:8]], axis=0)
    return pltpu.roll(matrix, E - 8, 1)


def sweep_some(count, *matrices):
    return lax.fori_loop(0, count, lambda _, ms: tuple(sweep_panel(m) for m in ms), matrices)


def kernel(
    states_h, pos, gw_h, uw_h, dw_h, cov_h, tgt,
    out,
    states, gw, uw, dw, cbuf, flat, gate, up, ra1, rb1, rc1, ra2, rb2, rc2,
    chi, clo, piece, bc, wc, bhl, whl, vv, vk, va, vb, vc, wr,
    part, rk, pa, pb, pc, xr, yr, res, tp, m0, n12, n3, send, recv, local,
):
    a = lax.axis_index("row")
    b = lax.axis_index("col")
    x, y = a // 4, a % 4
    z, k = b // 2, b % 2

    def dev_x(d):
        return {"row": ((x + d) % 4) * 4 + y}

    def dev_y(d):
        return {"row": x * 4 + (y + d) % 4}

    def dev_z(d):
        return {"col": ((z + d) % 4) * 2 + k}

    dev_k = {"col": z * 2 + 1 - k}
    sent = []

    def cp(src, dst, sem, dev):
        copy = pltpu.make_async_remote_copy(
            src_ref=src, dst_ref=dst, send_sem=send.at[sem], recv_sem=recv.at[sem],
            device_id=dev, device_id_type=pl.DeviceIdType.MESH,
        )
        copy.start()
        sent.append(copy)
        return copy

    loads = [
        pltpu.make_async_copy(src, dst, local.at[i])
        for i, (src, dst) in enumerate(((states_h, states), (gw_h, gw), (uw_h, uw), (dw_h, dw)))
    ]
    for load in loads:
        load.start()

    def cov_load(step, slot):
        return pltpu.make_async_copy(
            cov_h.at[pl.ds(pl.multiple_of(step * LINES, 8), LINES)], cbuf.at[slot], local.at[4 + slot]
        )

    cov_load(0, 0).start()

    barrier = pltpu.get_barrier_semaphore()
    peers = [dev(d) for dev in (dev_x, dev_y, dev_z) for d in (1, 2, 3)] + [dev_k]
    for peer in peers:
        pl.semaphore_signal(barrier, inc=1, device_id=peer, device_id_type=pl.DeviceIdType.MESH)
    pl.semaphore_wait(barrier, len(peers))

    def ring_start(data, ra, rb, me, dev, sem):
        m1, m2, m3 = (me + 1) % 4, (me + 2) % 4, (me + 3) % 4
        return [
            cp(data(0, m2), ra(0), sem, dev(1)),
            cp(data(1, m2), ra(1), sem + 1, dev(3)),
            cp(data(0, m3), rb(0), sem + 2, dev(3)),
            cp(data(1, m1), rb(1), sem + 3, dev(1)),
        ]

    def ring_middle(copies, data, ra, rc, me, dev, sem):
        m1, m3 = (me + 1) % 4, (me + 3) % 4
        copies[0].wait_recv()
        data(0, m1)[...] += ra(0)[...]
        c0 = cp(data(0, m1), rc(0), sem + 4, dev(1))
        copies[1].wait_recv()
        data(1, m3)[...] += ra(1)[...]
        c1 = cp(data(1, m3), rc(1), sem + 5, dev(3))
        return [copies[2], copies[3], c0, c1]

    def ring_end(copies, data, rb, rc, me):
        for copy in copies:
            copy.wait_recv()
        for h in (0, 1):
            data(h, me)[...] += rb(h)[...] + rc(h)[...]

    loads[0].wait()
    tokens = []
    for p in (0, 1):
        where = pos[p : p + 1, :]
        chosen = jnp.zeros((336, E), F32)
        for s in range(8):
            chosen = jnp.where(where == s, states[p, s].astype(F32), chosen)
        tokens.append(chosen.astype(BF16))
    tokens = jnp.concatenate(tokens, axis=1)

    def project(weight, target, by_y):
        def chunk(j, carry):
            at = pl.multiple_of(j * 384, 128)
            flat[pl.ds(at, 384), :] = dot_tb(weight[:, pl.ds(at, 384)], tokens)
            return carry

        lax.fori_loop(0, 7, chunk, 0)

        def place(i, carry):
            px, py = i // 4, i % 4
            first, second = (py, px) if by_y else (px, py)
            at = pl.multiple_of(i * PIECE, 8)
            for p in (0, 1):
                target[p, first, second] = flat[pl.ds(at, PIECE), p * E : (p + 1) * E]
            return carry

        lax.fori_loop(0, 16, place, 0)

    def gate_data(h, t):
        return gate.at[h, t]

    def up_data(h, t):
        return up.at[h, t]

    def gate_data2(h, t):
        return gate.at[h, x, t]

    def up_data2(h, t):
        return up.at[h, y, t]

    def buf(ref, which):
        return lambda h: ref.at[which, h]

    loads[1].wait()
    project(gw, gate, False)
    g1 = ring_start(gate_data, buf(ra1, 0), buf(rb1, 0), x, dev_x, 0)
    loads[2].wait()
    project(uw, up, True)
    u1 = ring_start(up_data, buf(ra1, 1), buf(rb1, 1), y, dev_y, 6)

    def cov_step(step, carry):
        slot = step % 2

        @pl.when(step + 1 < COV_STEPS)
        def _():
            cov_load(step + 1, 1 - slot).start()

        cov_load(step, slot).wait()
        rows = pl.ds(pl.multiple_of(step * COV_ROWS, 16), COV_ROWS)
        for t in range(21):
            high, low = halves(cbuf[slot, pl.ds(t, COV_ROWS, stride=21), :])
            chi[rows, t * E : (t + 1) * E] = high
            clo[rows, t * E : (t + 1) * E] = low
        return carry

    lax.fori_loop(0, COV_STEPS // 2, cov_step, 0)
    g1 = ring_middle(g1, gate_data, buf(ra1, 0), buf(rc1, 0), x, dev_x, 0)
    u1 = ring_middle(u1, up_data, buf(ra1, 1), buf(rc1, 1), y, dev_y, 6)
    lax.fori_loop(COV_STEPS // 2, COV_STEPS, cov_step, 0)
    ring_end(g1, gate_data, buf(rb1, 0), buf(rc1, 0), x)
    g2 = ring_start(gate_data2, buf(ra2, 0), buf(rb2, 0), y, dev_y, 12)
    ring_end(u1, up_data, buf(rb1, 1), buf(rc1, 1), y)
    u2 = ring_start(up_data2, buf(ra2, 1), buf(rb2, 1), x, dev_x, 18)
    g2 = ring_middle(g2, gate_data2, buf(ra2, 0), buf(rc2, 0), y, dev_y, 12)
    u2 = ring_middle(u2, up_data2, buf(ra2, 1), buf(rc2, 1), x, dev_x, 18)
    ring_end(g2, gate_data2, buf(rb2, 0), buf(rc2, 0), y)
    ring_end(u2, up_data2, buf(rb2, 1), buf(rc2, 1), x)

    keys = jnp.zeros((PIECE, E), F32)
    for p in (0, 1):
        v = gate[p, x, y]
        keys = keys + v / (1.0 + jnp.exp(-v)) * up[p, y, x]
    keys = keys * 0.5
    keys_half = keys.astype(BF16)
    piece[0] = 4.0 / math.sqrt(FF) * keys
    top, low = pl.ds(0, 88), pl.ds(88, 80)

    def gather_start(field, own, sem):
        field[x, y] = piece[own]
        return [cp(field.at[x, y, top], field.at[x, y, top], sem + d - 1, dev_x(d)) for d in (1, 2, 3)] + [
            cp(field.at[x, y, low], field.at[x, y, low], sem + 2 + d, dev_y(d)) for d in (1, 2, 3)
        ]

    def gather_middle(copies, field, sem):
        for copy in copies[:3]:
            copy.wait_recv()
        mine = field.at[:, y, top]
        out_y = [cp(mine, mine, sem + 6, dev_y(1)), cp(mine, mine, sem + 7, dev_y(3))]
        for copy in copies[3:]:
            copy.wait_recv()
        mine = field.at[x, :, low]
        out_x = [cp(mine, mine, sem + 8, dev_x(1)), cp(mine, mine, sem + 9, dev_x(3))]
        return out_y + out_x

    def gather_forward(copies, field, sem):
        y1, y3, x1, x3 = (y + 1) % 4, (y + 3) % 4, (x + 1) % 4, (x + 3) % 4
        copies[0].wait_recv()
        part0 = field.at[:, y3, pl.ds(0, 48)]
        f0 = cp(part0, part0, sem + 10, dev_y(1))
        copies[1].wait_recv()
        part1 = field.at[:, y1, pl.ds(48, 40)]
        f1 = cp(part1, part1, sem + 11, dev_y(3))
        copies[2].wait_recv()
        part2 = field.at[x3, :, pl.ds(88, 40)]
        f2 = cp(part2, part2, sem + 12, dev_x(1))
        copies[3].wait_recv()
        part3 = field.at[x1, :, pl.ds(128, 40)]
        f3 = cp(part3, part3, sem + 13, dev_x(3))
        return [f0, f1, f2, f3]

    def split_field(field, target):
        def body(i, carry):
            rows = pl.ds(pl.multiple_of(i * 336, 16), 336)
            high, rest = halves(field[i // 2, pl.ds((i % 2) * 2, 2)].reshape(336, E))
            target[rows, :E] = high
            target[rows, E:] = rest
            return carry

        lax.fori_loop(0, 8, body, 0)

    def gram(left, right):
        def body(i, total):
            rows = pl.ds(pl.multiple_of(i * 336, 16), 336)
            return total + dot_tb(left[rows, :], right[rows, :])

        total = lax.fori_loop(0, 8, body, jnp.zeros((2 * E, 2 * E), F32))
        return (total[:E, :E] + total[E:, E:]) + (total[:E, E:] + total[E:, :E])

    def cov_times(i, target):
        rows = pl.ds(pl.multiple_of(i * 336, 16), 336)
        both = dot_b(chi[rows, :], target[...])
        return both[:, :E] + (both[:, E:] + dot_b(clo[rows, :], target[:, :E]))

    bg = gather_start(bc, 0, 24)

    loads[3].wait()
    tp[...] = jnp.zeros_like(tp)
    tp[0:42, :] = tgt[...]
    first = (a * 8 + b) * 42

    def current(j, carry):
        at = pl.multiple_of(j * 384, 128)
        value = dot_tb(keys_half, dw[:, pl.ds(at, 384)])
        place = lax.broadcasted_iota(jnp.int32, (48, 384), 1) + j * 384 - first
        mark = jnp.where(place == lax.broadcasted_iota(jnp.int32, (48, 384), 0), 1.0, 0.0)
        value = dot_t(tp[...], mark) - value
        for i in range(3):
            part[j * 3 + i] = value[:, i * E : (i + 1) * E]
        return carry

    lax.fori_loop(0, 14, current, 0)
    for i in range(42, 48):
        part[i] = jnp.zeros((E, E), F32)
    real = pl.ds(0, 42)

    def half_of(kk):
        return pl.ds(pl.multiple_of(kk * 64, 8), 64)

    p1 = cp(part.at[real, half_of(1 - k)], rk, 52, dev_k)
    bg = gather_middle(bg, bc, 24)

    def part_data(h, t):
        return part.at[real, pl.ds(pl.multiple_of(k * 64 + t * 16 + h * 8, 8), 8)]

    p1.wait_recv()

    def add_half(i, carry):
        part[i, half_of(k), :] += rk[i]
        return carry

    lax.fori_loop(0, 42, add_half, 0)
    bf = gather_forward(bg, bc, 24)
    pz = ring_start(part_data, lambda h: pa.at[h], lambda h: pb.at[h], z, dev_z, 53)
    for copy in bf:
        copy.wait_recv()
    split_field(bc, bhl)
    m0[0] = gram(bhl, bhl)
    mk = cp(m0.at[0], m0.at[1], 59, dev_k)

    def first_image(i, carry):
        value = cov_times(i, bhl)
        vv[i, 0] = value[:PIECE]
        vv[i, 1] = value[PIECE:]
        return carry

    lax.fori_loop(0, 4, first_image, 0)
    v1 = cp(vv.at[:, 1 - k], vk, 60, dev_k)
    pz = ring_middle(pz, part_data, lambda h: pa.at[h], lambda h: pc.at[h], z, dev_z, 53)
    v1.wait_recv()
    vv[:, k] += vk[...]

    def image_data(h, t):
        return vv.at[t, k, top if h == 0 else low]

    def image_buf(ref):
        return lambda h: ref.at[h, pl.ds(0, 88 if h == 0 else 80)]

    vz = ring_start(image_data, image_buf(va), image_buf(vb), z, dev_z, 61)
    mk.wait_recv()
    m0[2] = m0[0] + m0[1]
    vz = ring_middle(vz, image_data, image_buf(va), image_buf(vc), z, dev_z, 61)
    mz = [cp(m0.at[2], m0.at[2 + d], 66 + d, dev_z(d)) for d in (1, 2, 3)]
    ring_end(vz, image_data, image_buf(vb), image_buf(vc), z)
    piece[1] = vv[z, k]
    wg = gather_start(wc, 1, 38)
    wr[z, k] = piece[1]
    wz = [cp(wr.at[z, k], wr.at[z, k], 69 + d, dev_z(d)) for d in (1, 2, 3)]
    ring_end(pz, part_data, lambda h: pb.at[h], lambda h: pc.at[h], z)
    wg = gather_middle(wg, wc, 38)
    wf = gather_forward(wg, wc, 38)
    own_rows = pl.ds(pl.multiple_of(k * 64 + z * 16, 8), 16)

    def twelve(t):
        return pl.ds(t * 12, 12)

    px = [cp(part.at[twelve((x + d) % 4), own_rows], xr.at[d - 1], 72 + d, dev_x(d)) for d in (1, 2, 3)]
    for copy in wz:
        copy.wait_recv()
    wk = cp(wr.at[:, k], wr.at[:, k], 76, dev_k)
    for copy in mz:
        copy.wait_recv()
    gram0 = sym((m0[2] + m0[3]) + (m0[4] + m0[5]))
    for copy in wf:
        copy.wait_recv()
    split_field(wc, whl)
    n12[0, 0] = gram(bhl, whl)
    n12[0, 1] = gram(whl, whl)
    nk = cp(n12.at[0], n12.at[1], 77, dev_k)
    wk.wait_recv()

    def second_image(i, total):
        value = cov_times(i, whl)
        return total + dot_t(wr[i].reshape(336, E), value)

    n3[0] = lax.fori_loop(0, 4, second_image, jnp.zeros((E, E), F32))
    n3k = cp(n3.at[0], n3.at[1], 78, dev_k)
    nk.wait_recv()
    n12[2] = n12[0] + n12[1]
    nz = [cp(n12.at[2], n12.at[2 + d], 78 + d, dev_z(d)) for d in (1, 2, 3)]
    n3k.wait_recv()
    n3[2] = n3[0] + n3[1]
    n3z = [cp(n3.at[2], n3.at[2 + d], 81 + d, dev_z(d)) for d in (1, 2, 3)]

    for copy in px:
        copy.wait_recv()
    part[twelve(x), own_rows] += (xr[0] + xr[1]) + xr[2]

    def three(t):
        return pl.ds(x * 12 + t * 3, 3)

    py = [cp(part.at[three((y + d) % 4), own_rows], yr.at[d - 1], 84 + d, dev_y(d)) for d in (1, 2, 3)]
    for copy in nz:
        copy.wait_recv()
    both = (n12[2] + n12[3]) + (n12[4] + n12[5])
    n1, n2 = sym(both[0]), both[1]
    square = dot(gram0, gram0)
    m1 = sym(n1 + square)
    n1m0 = dot(n1, gram0)
    m2 = sym(n2 + n1m0 + n1m0.T + dot(square, gram0))
    n2m0 = dot(n2, gram0)
    m3_rest = sym(n2m0 + n2m0.T + dot(gram0, n1m0) + dot(m1, m1))
    for copy in n3z:
        copy.wait_recv()
    n3[6] = (n3[2] + n3[3]) + (n3[4] + n3[5])
    n3y = [cp(n3.at[6], n3.at[6 + d], 87 + d, dev_y(d)) for d in (1, 2, 3)]
    for copy in py:
        copy.wait_recv()
    res[three(y), own_rows] = part[three(y), own_rows] + ((yr[0] + yr[1]) + yr[2])
    mine = res.at[three(y), own_rows]
    ry = [cp(mine, mine, 90 + d, dev_y(d)) for d in (1, 2, 3)]
    inv0, inv1 = sweep_some(4, gram0, m1)
    for copy in n3y:
        copy.wait_recv()
    n3[10] = (n3[6] + n3[7]) + (n3[8] + n3[9])
    n3x = [cp(n3.at[10], n3.at[10 + d], 93 + d, dev_x(d)) for d in (1, 2, 3)]
    for copy in ry:
        copy.wait_recv()
    mine_x = res.at[twelve(x), own_rows]
    rx = [cp(mine_x, mine_x, 96 + d, dev_x(d)) for d in (1, 2, 3)]
    inv0, inv1 = sweep_some(6, inv0, inv1)
    for copy in rx:
        copy.wait_recv()
    mine_z = res.at[real, own_rows]
    rz = [cp(mine_z, mine_z, 100, dev_z(1)), cp(mine_z, mine_z, 101, dev_z(3))]
    inv0, inv1 = sweep_some(6, inv0, inv1)

    def rows_of(zz, h):
        return pl.ds(pl.multiple_of(k * 64 + zz * 16 + h * 8, 8), 8)

    rz[0].wait_recv()
    fwd0 = res.at[real, rows_of((z + 3) % 4, 0)]
    rf0 = cp(fwd0, fwd0, 102, dev_z(1))
    rz[1].wait_recv()
    fwd1 = res.at[real, rows_of((z + 1) % 4, 1)]
    rf1 = cp(fwd1, fwd1, 103, dev_z(3))
    alpha0 = dot(inv1, gram0)
    norm1 = sym(dot_t(alpha0, dot(m2, alpha0)) - gram0)
    beta = dot(inv0, norm1)
    eye = jnp.where(
        lax.broadcasted_iota(jnp.int32, (E, E), 0) == lax.broadcasted_iota(jnp.int32, (E, E), 1), 1.0, 0.0
    )
    c1 = eye + beta
    cross = dot_t(c1, dot(m2, alpha0))
    curv_rest = dot_t(c1, dot(m1, c1)) - cross - cross.T
    for copy in n3x:
        copy.wait_recv()
    m3 = m3_rest + sym((n3[10] + n3[11]) + (n3[12] + n3[13]))
    curvature = sym(curv_rest + dot_t(alpha0, dot(m3, alpha0)))
    (inv2,) = sweep_some(16, curvature)
    rf0.wait_recv()
    rf1.wait_recv()
    half = res.at[real, half_of(k)]
    rkk = cp(half, half, 104, dev_k)
    alpha1 = dot(inv2, norm1)
    on_w = -dot(alpha0, alpha1)
    m0[3] = dot(c1, alpha1)
    m0[4] = dot(gram0, on_w)
    on_b = alpha0 + (m0[3] + m0[4])
    fh, fl = halves(jnp.concatenate([piece[0], piece[1]], axis=1))
    ch, cl = halves(jnp.concatenate([on_b, on_w], axis=0))
    found = dot_b(fh, ch) + (dot_b(fh, cl) + dot_b(fl, ch))
    xh, xl = halves(found)
    xhh = jnp.concatenate([xh, xh], axis=1)
    rkk.wait_recv()

    def update(j, carry):
        right = jnp.concatenate([res[j * 2], res[j * 2 + 1]], axis=1)
        rh, rl = halves(right)
        value = dot_b(xhh, jnp.concatenate([rh, rl], axis=0)) + dot_b(xl, rh)
        out[:, pl.ds(pl.multiple_of(j * 256, 128), 256)] = value.astype(BF16)
        return carry

    lax.fori_loop(0, 21, update, 0)
    for copy in sent:
        copy.wait_send()


def body(states, subject_pos, gate_weight, up_weight, down_weight, covariance, targets):
    vmem = pl.BlockSpec(memory_space=pltpu.VMEM)
    anyw = pl.BlockSpec(memory_space=pl.ANY)
    small = lambda *dims: pltpu.VMEM(dims, F32)
    update = pl.pallas_call(
        kernel,
        out_shape=jax.ShapeDtypeStruct((PIECE, D), BF16),
        in_specs=[anyw, vmem, anyw, anyw, anyw, anyw, vmem],
        out_specs=vmem,
        scratch_shapes=[
            pltpu.VMEM((2, 8, 336, E), BF16),
            pltpu.VMEM((336, 2688), BF16),
            pltpu.VMEM((336, 2688), BF16),
            pltpu.VMEM((PIECE, D), BF16),
            small(2, LINES, E),
            small(2688, 2 * E),
            small(2, 4, 4, PIECE, E),
            small(2, 4, 4, PIECE, E),
            small(2, 2, 4, PIECE, E),
            small(2, 2, 4, PIECE, E),
            small(2, 2, 4, PIECE, E),
            small(2, 2, PIECE, E),
            small(2, 2, PIECE, E),
            small(2, 2, PIECE, E),
            pltpu.VMEM((1344, 2688), BF16),
            pltpu.VMEM((1344, 2688), BF16),
            small(2, PIECE, E),
            small(4, 4, PIECE, E),
            small(4, 4, PIECE, E),
            pltpu.VMEM((2688, 2 * E), BF16),
            pltpu.VMEM((2688, 2 * E), BF16),
            small(4, 2, PIECE, E),
            small(4, PIECE, E),
            small(2, 88, E),
            small(2, 88, E),
            small(2, 88, E),
            small(4, 2, PIECE, E),
            small(48, E, E),
            small(42, 64, E),
            small(2, 42, 8, E),
            small(2, 42, 8, E),
            small(2, 42, 8, E),
            small(3, 12, 16, E),
            small(3, 3, 16, E),
            small(48, E, E),
            small(48, E),
            small(6, E, E),
            small(6, 2, E, E),
            small(14, E, E),
            pltpu.SemaphoreType.DMA((N_SEM,)),
            pltpu.SemaphoreType.DMA((N_SEM,)),
            pltpu.SemaphoreType.DMA((6,)),
        ],
        compiler_params=pltpu.CompilerParams(
            collective_id=0, has_side_effects=True, vmem_limit_bytes=60 * 1024 * 1024
        ),
        name="edit",
    )(
        jnp.transpose(states, (1, 2, 3, 0)),
        subject_pos.T,
        gate_weight.reshape(336, 2688),
        up_weight.reshape(336, 2688),
        down_weight.reshape(PIECE, D),
        covariance.reshape(1344 * 21, E),
        targets,
    )
    return update.reshape(1, 1, PIECE, D)


def solution(mesh):
    return jax.shard_map(
        body,
        mesh=mesh,
        in_specs=(
            P(None, None, None, "row"),
            P(),
            P("row", "col", None),
            P("row", "col", None),
            P("row", "col", None, None),
            P("row", "col", None),
            P(("row", "col"), None),
        ),
        out_specs=P("row", "col", None, None),
        check_vma=False,
    )
```

```python
import math

import jax
import jax.numpy as jnp
from jax import lax
from jax.experimental import pallas as pl
from jax.experimental.pallas import tpu as pltpu
from jax.sharding import PartitionSpec as P

FF = 21504
D = 5376
PIECE = 168
E = 128
F32 = jnp.float32
BF16 = jnp.bfloat16
HI = lax.Precision.HIGHEST
N_SEM = 132
COV_ROWS = 112
COV_STEPS = 1344 // COV_ROWS
LINES = COV_ROWS * 21


def dot(left, right):
    return lax.dot_general(left, right, (((1,), (0,)), ((), ())), precision=HI, preferred_element_type=F32)


def dot_t(left, right):
    return lax.dot_general(left, right, (((0,), (0,)), ((), ())), precision=HI, preferred_element_type=F32)


def dot_b(left, right):
    return lax.dot_general(left, right, (((1,), (0,)), ((), ())), preferred_element_type=F32)


def dot_tb(left, right):
    return lax.dot_general(left, right, (((0,), (0,)), ((), ())), preferred_element_type=F32)


def halves(value):
    high = value.astype(BF16)
    return high, (value - high.astype(F32)).astype(BF16)


def sym(matrix):
    return 0.5 * (matrix + matrix.T)


def sweep_panel(matrix):
    lane = lax.broadcasted_iota(jnp.int32, (E, E), 1)
    sub = lax.broadcasted_iota(jnp.int32, (E, E), 0)
    lane1 = lax.broadcasted_iota(jnp.int32, (1, E), 1)
    for j in range(8):
        column = matrix[:, j : j + 1]
        row = matrix[j : j + 1, :]
        inv = 1.0 / matrix[j : j + 1, j : j + 1]
        row = jnp.where(lane1 == j, inv, row * inv)
        rest = jnp.where(lane == j, 0.0, matrix) - column * row
        matrix = jnp.where(sub == j, row, rest)
    matrix = jnp.concatenate([matrix[8:], matrix[:8]], axis=0)
    return pltpu.roll(matrix, E - 8, 1)


def sweep_some(count, *matrices):
    return lax.fori_loop(0, count, lambda _, ms: tuple(sweep_panel(m) for m in ms), matrices)


def kernel(
    states_h, pos, gw_h, uw_h, dw_h, cov_h, tgt,
    out,
    states, gw, uw, dw, cbuf, flat, gate, up, ra1, rb1, rc1, ra2, rb2, rc2,
    chi, clo, piece, bc, wc, bhl, whl, vv, vk, va, vb, vc, wr,
    part, rk, pa, pb, pc, xr, yr, res, tp, m0, n12, n3, mc, nc, mc2, mzr, nzr, n3r, gsum, tmp, send, recv, local,
):
    a = lax.axis_index("row")
    b = lax.axis_index("col")
    x, y = a // 4, a % 4
    z, k = b // 2, b % 2

    def dev_x(d):
        return {"row": ((x + d) % 4) * 4 + y}

    def dev_y(d):
        return {"row": x * 4 + (y + d) % 4}

    def dev_z(d):
        return {"col": ((z + d) % 4) * 2 + k}

    dev_k = {"col": z * 2 + 1 - k}
    sent = []

    def cp(src, dst, dev):
        sem = len(sent)
        copy = pltpu.make_async_remote_copy(
            src_ref=src, dst_ref=dst, send_sem=send.at[sem], recv_sem=recv.at[sem],
            device_id=dev, device_id_type=pl.DeviceIdType.MESH,
        )
        copy.start()
        sent.append(copy)
        return copy

    loads = [
        pltpu.make_async_copy(src, dst, local.at[i])
        for i, (src, dst) in enumerate(((states_h, states), (gw_h, gw), (uw_h, uw), (dw_h, dw)))
    ]
    for load in loads:
        load.start()

    def cov_load(step, slot):
        return pltpu.make_async_copy(
            cov_h.at[pl.ds(pl.multiple_of(step * LINES, 8), LINES)], cbuf.at[slot], local.at[4 + slot]
        )

    cov_load(0, 0).start()

    barrier = pltpu.get_barrier_semaphore()
    peers = [dev(d) for dev in (dev_x, dev_y, dev_z) for d in (1, 2, 3)] + [dev_k]
    for peer in peers:
        pl.semaphore_signal(barrier, inc=1, device_id=peer, device_id_type=pl.DeviceIdType.MESH)
    pl.semaphore_wait(barrier, len(peers))

    def ring_start(data, ra, rb, me, dev):
        m1, m2, m3 = (me + 1) % 4, (me + 2) % 4, (me + 3) % 4
        return [
            cp(data(0, m2), ra(0), dev(1)),
            cp(data(1, m2), ra(1), dev(3)),
            cp(data(0, m3), rb(0), dev(3)),
            cp(data(1, m1), rb(1), dev(1)),
        ]

    def ring_middle(copies, data, ra, rc, me, dev):
        m1, m3 = (me + 1) % 4, (me + 3) % 4
        copies[0].wait_recv()
        data(0, m1)[...] += ra(0)[...]
        c0 = cp(data(0, m1), rc(0), dev(1))
        copies[1].wait_recv()
        data(1, m3)[...] += ra(1)[...]
        c1 = cp(data(1, m3), rc(1), dev(3))
        return [copies[2], copies[3], c0, c1]

    def ring_end(copies, data, rb, rc, me):
        for copy in copies:
            copy.wait_recv()
        for h in (0, 1):
            data(h, me)[...] += rb(h)[...] + rc(h)[...]

    def to_three(src, dst, dev):
        return [cp(src(d), dst(d), dev(d)) for d in (1, 2, 3)]

    def wait_all(copies):
        for copy in copies:
            copy.wait_recv()

    loads[0].wait()
    tokens = []
    for p in (0, 1):
        where = pos[p : p + 1, :]
        chosen = jnp.zeros((336, E), F32)
        for s in range(8):
            chosen = jnp.where(where == s, states[p, s].astype(F32), chosen)
        tokens.append(chosen.astype(BF16))
    tokens = jnp.concatenate(tokens, axis=1)

    def project(weight, target, by_y):
        def chunk(j, carry):
            at = pl.multiple_of(j * 384, 128)
            flat[pl.ds(at, 384), :] = dot_tb(weight[:, pl.ds(at, 384)], tokens)
            return carry

        lax.fori_loop(0, 7, chunk, 0)

        def place(i, carry):
            px, py = i // 4, i % 4
            first, second = (py, px) if by_y else (px, py)
            at = pl.multiple_of(i * PIECE, 8)
            for p in (0, 1):
                target[p, first, second] = flat[pl.ds(at, PIECE), p * E : (p + 1) * E]
            return carry

        lax.fori_loop(0, 16, place, 0)

    def gate_data(h, t):
        return gate.at[h, t]

    def up_data(h, t):
        return up.at[h, t]

    def gate_data2(h, t):
        return gate.at[h, x, t]

    def up_data2(h, t):
        return up.at[h, y, t]

    def buf(ref, which):
        return lambda h: ref.at[which, h]

    loads[1].wait()
    project(gw, gate, False)
    g1 = ring_start(gate_data, buf(ra1, 0), buf(rb1, 0), x, dev_x)
    loads[2].wait()
    project(uw, up, True)
    u1 = ring_start(up_data, buf(ra1, 1), buf(rb1, 1), y, dev_y)

    def cov_step(step, carry):
        slot = step % 2

        @pl.when(step + 1 < COV_STEPS)
        def _():
            cov_load(step + 1, 1 - slot).start()

        cov_load(step, slot).wait()
        rows = pl.ds(pl.multiple_of(step * COV_ROWS, 16), COV_ROWS)
        for t in range(21):
            high, low = halves(cbuf[slot, pl.ds(t, COV_ROWS, stride=21), :])
            chi[rows, t * E : (t + 1) * E] = high
            clo[rows, t * E : (t + 1) * E] = low
        return carry

    lax.fori_loop(0, COV_STEPS // 2, cov_step, 0)
    g1 = ring_middle(g1, gate_data, buf(ra1, 0), buf(rc1, 0), x, dev_x)
    u1 = ring_middle(u1, up_data, buf(ra1, 1), buf(rc1, 1), y, dev_y)
    lax.fori_loop(COV_STEPS // 2, COV_STEPS, cov_step, 0)
    ring_end(g1, gate_data, buf(rb1, 0), buf(rc1, 0), x)
    g2 = ring_start(gate_data2, buf(ra2, 0), buf(rb2, 0), y, dev_y)
    ring_end(u1, up_data, buf(rb1, 1), buf(rc1, 1), y)
    u2 = ring_start(up_data2, buf(ra2, 1), buf(rb2, 1), x, dev_x)
    g2 = ring_middle(g2, gate_data2, buf(ra2, 0), buf(rc2, 0), y, dev_y)
    u2 = ring_middle(u2, up_data2, buf(ra2, 1), buf(rc2, 1), x, dev_x)
    ring_end(g2, gate_data2, buf(rb2, 0), buf(rc2, 0), y)
    ring_end(u2, up_data2, buf(rb2, 1), buf(rc2, 1), x)

    keys = jnp.zeros((PIECE, E), F32)
    for p in (0, 1):
        v = gate[p, x, y]
        keys = keys + v / (1.0 + jnp.exp(-v)) * up[p, y, x]
    keys = keys * 0.5
    keys_half = keys.astype(BF16)
    piece[0] = 4.0 / math.sqrt(FF) * keys
    top, low = pl.ds(0, 88), pl.ds(88, 80)

    def gather_start(field, own):
        field[x, y] = piece[own]
        at, ab = field.at[x, y, top], field.at[x, y, low]
        return to_three(lambda d: at, lambda d: at, dev_x) + to_three(lambda d: ab, lambda d: ab, dev_y)

    def gather_middle(copies, field):
        wait_all(copies[:3])
        mine = field.at[:, y, top]
        out_y = [cp(mine, mine, dev_y(1)), cp(mine, mine, dev_y(3))]
        wait_all(copies[3:])
        mine = field.at[x, :, low]
        return out_y + [cp(mine, mine, dev_x(1)), cp(mine, mine, dev_x(3))]

    def gather_forward(copies, field):
        parts = (
            (field.at[:, (y + 3) % 4, pl.ds(0, 48)], dev_y(1)),
            (field.at[:, (y + 1) % 4, pl.ds(48, 40)], dev_y(3)),
            (field.at[(x + 3) % 4, :, pl.ds(88, 40)], dev_x(1)),
            (field.at[(x + 1) % 4, :, pl.ds(128, 40)], dev_x(3)),
        )
        sends = []
        for copy, (block, dev) in zip(copies, parts):
            copy.wait_recv()
            sends.append(cp(block, block, dev))
        return sends

    def split_field(field, target):
        def body(i, carry):
            rows = pl.ds(pl.multiple_of(i * 336, 16), 336)
            high, rest = halves(field[i // 2, pl.ds((i % 2) * 2, 2)].reshape(336, E))
            target[rows, :E] = high
            target[rows, E:] = rest
            return carry

        lax.fori_loop(0, 8, body, 0)

    def gram(left, right):
        def body(i, total):
            rows = pl.ds(pl.multiple_of(i * 336, 16), 336)
            return total + dot_tb(left[rows, :], right[rows, :])

        total = lax.fori_loop(0, 8, body, jnp.zeros((2 * E, 2 * E), F32))
        return (total[:E, :E] + total[E:, E:]) + (total[:E, E:] + total[E:, :E])

    def cov_times(i, target):
        rows = pl.ds(pl.multiple_of(i * 336, 16), 336)
        both = dot_b(chi[rows, :], target[...])
        return both[:, :E] + (both[:, E:] + dot_b(clo[rows, :], target[:, :E]))

    bg = gather_start(bc, 0)

    loads[3].wait()
    tp[...] = jnp.zeros_like(tp)
    tp[0:42, :] = tgt[...]
    first = (a * 8 + b) * 42
    t_high, t_rest = tp[...].astype(BF16), tp[...] - tp[...].astype(BF16).astype(F32)
    t_mid, t_low = halves(t_rest)
    t_all = jnp.concatenate([t_high, t_mid, t_low], axis=0)
    minus = -keys_half

    def current(j, carry):
        at = pl.multiple_of(j * 384, 128)
        place = lax.broadcasted_iota(jnp.int32, (48, 384), 1) + j * 384 - first
        mark = jnp.where(place == lax.broadcasted_iota(jnp.int32, (48, 384), 0), 1.0, 0.0).astype(BF16)
        value = dot_tb(minus, dw[:, pl.ds(at, 384)]) + dot_tb(t_all, jnp.concatenate([mark, mark, mark], axis=0))
        for i in range(3):
            part[j * 3 + i] = value[:, i * E : (i + 1) * E]
        return carry

    lax.fori_loop(0, 14, current, 0)
    for i in range(42, 48):
        part[i] = jnp.zeros((E, E), F32)
    real = pl.ds(0, 42)

    def half_of(kk):
        return pl.ds(pl.multiple_of(kk * 64, 8), 64)

    def rows_of(zz, h):
        return pl.ds(pl.multiple_of(k * 64 + zz * 16 + h * 8, 8), 8)

    def part_data(h, t):
        return part.at[real, rows_of(t, h)]

    def at_half(ref):
        return lambda h: ref.at[h]

    p1 = cp(part.at[real, half_of(1 - k)], rk, dev_k)
    bg = gather_middle(bg, bc)
    p1.wait_recv()

    def add_half(i, carry):
        part[i, half_of(k), :] += rk[i]
        return carry

    lax.fori_loop(0, 42, add_half, 0)
    pz = ring_start(part_data, at_half(pa), at_half(pb), z, dev_z)
    bf = gather_forward(bg, bc)
    wait_all(bf)
    split_field(bc, bhl)

    def halve(ref, i, value):
        ref[i, 0] = value[:64]
        ref[i, 1] = value[64:]

    def cores_start(ref, n, got):
        return cp(ref.at[pl.ds(0, n), 1 - k], got.at[pl.ds(0, n)], dev_k)

    def cores_end(copy, ref, n, got):
        copy.wait_recv()
        ref[pl.ds(0, n), k] += got[pl.ds(0, n)]

    def axis_start(ref, n, got, dev):
        return to_three(lambda d: ref.at[pl.ds(0, n), k], lambda d: got.at[d - 1, pl.ds(0, n)], dev)

    def axis_end(copies, ref, n, got, target):
        wait_all(copies)
        target[pl.ds(0, n), k] = ref[pl.ds(0, n), k] + ((got[0, pl.ds(0, n)] + got[1, pl.ds(0, n)]) + got[2, pl.ds(0, n)])

    def cores_share(ref):
        return cp(ref.at[:, k], ref.at[:, k], dev_k)

    def first_image(i, carry):
        value = cov_times(i, bhl)
        vv[i, 0] = value[:PIECE]
        vv[i, 1] = value[PIECE:]
        return carry

    lax.fori_loop(0, 4, first_image, 0)
    v1 = cp(vv.at[:, 1 - k], vk, dev_k)
    halve(m0, 0, gram(bhl, bhl))
    mk = cores_start(m0, 1, mc)
    v1.wait_recv()
    vv[:, k] += vk[...]

    def image_data(h, t):
        return vv.at[t, k, top if h == 0 else low]

    def image_buf(ref):
        return lambda h: ref.at[h, pl.ds(0, 88 if h == 0 else 80)]

    vz = ring_start(image_data, image_buf(va), image_buf(vb), z, dev_z)
    pz = ring_middle(pz, part_data, at_half(pa), at_half(pc), z, dev_z)
    vz = ring_middle(vz, image_data, image_buf(va), image_buf(vc), z, dev_z)
    cores_end(mk, m0, 1, mc)
    ring_end(vz, image_data, image_buf(vb), image_buf(vc), z)
    piece[1] = vv[z, k]
    wg = gather_start(wc, 1)
    wr[z, k] = piece[1]
    wz = to_three(lambda d: wr.at[z, k], lambda d: wr.at[z, k], dev_z)
    mz = axis_start(m0, 1, mzr, dev_z)
    ring_end(pz, part_data, at_half(pb), at_half(pc), z)

    def twelve(t):
        return pl.ds(t * 12, 12)

    def three(t, u):
        return pl.ds(t * 12 + u * 3, 3)

    up_rows, down_rows = rows_of(z, 0), rows_of(z, 1)
    wg = gather_middle(wg, wc)
    px = to_three(lambda d: part.at[twelve((x + d) % 4), up_rows], lambda d: xr.at[0, d - 1], dev_x)
    px += to_three(lambda d: part.at[twelve((y + d) % 4), down_rows], lambda d: xr.at[1, d - 1], dev_y)
    wait_all(wz)
    wk = cp(wr.at[:, k], wr.at[:, k], dev_k)
    axis_end(mz, m0, 1, mzr, gsum)
    wf = gather_forward(wg, wc)
    wait_all(px)
    part[twelve(x), up_rows] += (xr[0, 0] + xr[0, 1]) + xr[0, 2]
    part[twelve(y), down_rows] += (xr[1, 0] + xr[1, 1]) + xr[1, 2]
    py = to_three(lambda d: part.at[three(x, (y + d) % 4), up_rows], lambda d: yr.at[0, d - 1], dev_y)
    py += to_three(lambda d: part.at[three(y, (x + d) % 4), down_rows], lambda d: yr.at[1, d - 1], dev_x)
    wait_all(wf)
    split_field(wc, whl)
    halve(n12, 0, gram(bhl, whl))
    halve(n12, 1, gram(whl, whl))
    nk = cores_start(n12, 2, nc)
    wait_all(py)
    res[three(x, y), up_rows] = part[three(x, y), up_rows] + ((yr[0, 0] + yr[0, 1]) + yr[0, 2])
    res[three(y, x), down_rows] = part[three(y, x), down_rows] + ((yr[1, 0] + yr[1, 1]) + yr[1, 2])
    own_a, own_b = res.at[three(x, y), up_rows], res.at[three(y, x), down_rows]
    ry = to_three(lambda d: own_a, lambda d: own_a, dev_y) + to_three(lambda d: own_b, lambda d: own_b, dev_x)
    wk.wait_recv()

    def second_image(i, total):
        value = cov_times(i, whl)
        return total + dot_t(wr[i].reshape(336, E), value)

    total = lax.fori_loop(0, 2, second_image, jnp.zeros((E, E), F32))
    cores_end(nk, n12, 2, nc)
    nz = axis_start(n12, 2, nzr, dev_z)
    wait_all(ry)
    own_a, own_b = res.at[twelve(x), up_rows], res.at[twelve(y), down_rows]
    rx = to_three(lambda d: own_a, lambda d: own_a, dev_x) + to_three(lambda d: own_b, lambda d: own_b, dev_y)
    total = lax.fori_loop(2, 4, second_image, total)
    halve(n3, 0, total)
    n3k = cores_start(n3, 1, mc2)
    axis_end(nz, n12, 2, nzr, gsum.at[pl.ds(1, 2)])
    gs = cores_share(gsum)
    wait_all(rx)
    own_z = res.at[real, pl.ds(pl.multiple_of(k * 64 + z * 16, 8), 16)]
    rz = [cp(own_z, own_z, dev_z(1)), cp(own_z, own_z, dev_z(3))]
    cores_end(n3k, n3, 1, mc2)
    n3y = axis_start(n3, 1, n3r.at[0], dev_y)
    gs.wait_recv()

    def whole(ref, i):
        return jnp.concatenate([ref[i, 0], ref[i, 1]], axis=0)

    gram0, n1, n2 = sym(whole(gsum, 0)), sym(whole(gsum, 1)), sym(whole(gsum, 2))
    square = dot(gram0, gram0)
    m1 = sym(n1 + square)
    axis_end(n3y, n3, 1, n3r.at[0], n3.at[pl.ds(1, 1)])
    n3x = axis_start(n3.at[pl.ds(1, 1)], 1, n3r.at[1], dev_x)
    inv0, inv1 = sweep_some(5, gram0, m1)
    axis_end(n3x, n3.at[pl.ds(1, 1)], 1, n3r.at[1], n3.at[pl.ds(2, 1)])
    n3z = axis_start(n3.at[pl.ds(2, 1)], 1, n3r.at[2], dev_z)
    inv0, inv1 = sweep_some(6, inv0, inv1)
    rz[0].wait_recv()
    fwd0 = res.at[real, rows_of((z + 3) % 4, 0)]
    rf0 = cp(fwd0, fwd0, dev_z(1))
    rz[1].wait_recv()
    fwd1 = res.at[real, rows_of((z + 1) % 4, 1)]
    rf1 = cp(fwd1, fwd1, dev_z(3))
    axis_end(n3z, n3.at[pl.ds(2, 1)], 1, n3r.at[2], n3.at[pl.ds(3, 1)])
    n3s = cores_share(n3.at[pl.ds(3, 1)])
    inv0, inv1 = sweep_some(5, inv0, inv1)
    n1m0 = dot(n1, gram0)
    m2 = sym(n2 + n1m0 + n1m0.T + dot(square, gram0))
    n2m0 = dot(n2, gram0)
    m3_rest = sym(n2m0 + n2m0.T + dot(gram0, n1m0) + dot(m1, m1))
    alpha0 = dot(inv1, gram0)
    norm1 = sym(dot_t(alpha0, dot(m2, alpha0)) - gram0)
    beta = dot(inv0, norm1)
    eye = jnp.where(
        lax.broadcasted_iota(jnp.int32, (E, E), 0) == lax.broadcasted_iota(jnp.int32, (E, E), 1), 1.0, 0.0
    )
    c1 = eye + beta
    cross = dot_t(c1, dot(m2, alpha0))
    curv_rest = dot_t(c1, dot(m1, c1)) - cross - cross.T
    n3s.wait_recv()
    m3 = m3_rest + sym(whole(n3, 3))
    curvature = sym(curv_rest + dot_t(alpha0, dot(m3, alpha0)))
    wait_all([rf0, rf1])
    half = res.at[real, half_of(k)]
    rkk = cp(half, half, dev_k)
    (inv2,) = sweep_some(16, curvature)
    alpha1 = dot(inv2, norm1)
    on_w = -dot(alpha0, alpha1)
    tmp[0] = dot(c1, alpha1)
    tmp[1] = dot(gram0, on_w)
    on_b = alpha0 + (tmp[0] + tmp[1])
    fh, fl = halves(jnp.concatenate([piece[0], piece[1]], axis=1))
    ch, cl = halves(jnp.concatenate([on_b, on_w], axis=0))
    found = dot_b(fh, ch) + (dot_b(fh, cl) + dot_b(fl, ch))
    xh, xl = halves(found)
    xhh = jnp.concatenate([xh, xh], axis=1)
    rkk.wait_recv()

    def update(j, carry):
        right = jnp.concatenate([res[j * 2], res[j * 2 + 1]], axis=1)
        rh, rl = halves(right)
        value = dot_b(xhh, jnp.concatenate([rh, rl], axis=0)) + dot_b(xl, rh)
        out[:, pl.ds(pl.multiple_of(j * 256, 128), 256)] = value.astype(BF16)
        return carry

    lax.fori_loop(0, 21, update, 0)
    for copy in sent:
        copy.wait_send()


def body(states, subject_pos, gate_weight, up_weight, down_weight, covariance, targets):
    vmem = pl.BlockSpec(memory_space=pltpu.VMEM)
    anyw = pl.BlockSpec(memory_space=pl.ANY)
    small = lambda *dims: pltpu.VMEM(dims, F32)
    update = pl.pallas_call(
        kernel,
        out_shape=jax.ShapeDtypeStruct((PIECE, D), BF16),
        in_specs=[anyw, vmem, anyw, anyw, anyw, anyw, vmem],
        out_specs=vmem,
        scratch_shapes=[
            pltpu.VMEM((2, 8, 336, E), BF16),
            pltpu.VMEM((336, 2688), BF16),
            pltpu.VMEM((336, 2688), BF16),
            pltpu.VMEM((PIECE, D), BF16),
            small(2, LINES, E),
            small(2688, 2 * E),
            small(2, 4, 4, PIECE, E),
            small(2, 4, 4, PIECE, E),
            small(2, 2, 4, PIECE, E),
            small(2, 2, 4, PIECE, E),
            small(2, 2, 4, PIECE, E),
            small(2, 2, PIECE, E),
            small(2, 2, PIECE, E),
            small(2, 2, PIECE, E),
            pltpu.VMEM((1344, 2688), BF16),
            pltpu.VMEM((1344, 2688), BF16),
            small(2, PIECE, E),
            small(4, 4, PIECE, E),
            small(4, 4, PIECE, E),
            pltpu.VMEM((2688, 2 * E), BF16),
            pltpu.VMEM((2688, 2 * E), BF16),
            small(4, 2, PIECE, E),
            small(4, PIECE, E),
            small(2, 88, E),
            small(2, 88, E),
            small(2, 88, E),
            small(4, 2, PIECE, E),
            small(48, E, E),
            small(42, 64, E),
            small(2, 42, 8, E),
            small(2, 42, 8, E),
            small(2, 42, 8, E),
            small(2, 3, 12, 8, E),
            small(2, 3, 3, 8, E),
            small(48, E, E),
            small(48, E),
            small(1, 2, 64, E),
            small(2, 2, 64, E),
            small(4, 2, 64, E),
            small(1, 64, E),
            small(2, 64, E),
            small(1, 64, E),
            small(3, 1, 64, E),
            small(3, 2, 64, E),
            small(3, 3, 1, 64, E),
            small(3, 2, 64, E),
            small(2, E, E),
            pltpu.SemaphoreType.DMA((N_SEM,)),
            pltpu.SemaphoreType.DMA((N_SEM,)),
            pltpu.SemaphoreType.DMA((6,)),
        ],
        compiler_params=pltpu.CompilerParams(
            collective_id=0, has_side_effects=True, vmem_limit_bytes=60 * 1024 * 1024
        ),
        name="edit",
    )(
        jnp.transpose(states, (1, 2, 3, 0)),
        subject_pos.T,
        gate_weight.reshape(336, 2688),
        up_weight.reshape(336, 2688),
        down_weight.reshape(PIECE, D),
        covariance.reshape(1344 * 21, E),
        targets,
    )
    return update.reshape(1, 1, PIECE, D)


def solution(mesh):
    return jax.shard_map(
        body,
        mesh=mesh,
        in_specs=(
            P(None, None, None, "row"),
            P(),
            P("row", "col", None),
            P("row", "col", None),
            P("row", "col", None, None),
            P("row", "col", None),
            P(("row", "col"), None),
        ),
        out_specs=P("row", "col", None, None),
        check_vma=False,
    )
```

```python
import math

import jax
import jax.numpy as jnp
from jax import lax
from jax.experimental import pallas as pl
from jax.experimental.pallas import tpu as pltpu
from jax.sharding import PartitionSpec as P

FF = 21504
D = 5376
PIECE = 168
E = 128
F32 = jnp.float32
BF16 = jnp.bfloat16
HI = lax.Precision.HIGHEST
N_SEM = 180
COV_ROWS = 112
COV_STEPS = 1344 // COV_ROWS
LINES = COV_ROWS * 21


def dot(left, right):
    return lax.dot_general(left, right, (((1,), (0,)), ((), ())), precision=HI, preferred_element_type=F32)


def dot_t(left, right):
    return lax.dot_general(left, right, (((0,), (0,)), ((), ())), precision=HI, preferred_element_type=F32)


def dot_b(left, right):
    return lax.dot_general(left, right, (((1,), (0,)), ((), ())), preferred_element_type=F32)


def dot_tb(left, right):
    return lax.dot_general(left, right, (((0,), (0,)), ((), ())), preferred_element_type=F32)


def halves(value):
    high = value.astype(BF16)
    return high, (value - high.astype(F32)).astype(BF16)


def sym(matrix):
    return 0.5 * (matrix + matrix.T)


def sweep_panel(matrix):
    lane = lax.broadcasted_iota(jnp.int32, (E, E), 1)
    sub = lax.broadcasted_iota(jnp.int32, (E, E), 0)
    lane1 = lax.broadcasted_iota(jnp.int32, (1, E), 1)
    for j in range(8):
        column = matrix[:, j : j + 1]
        row = matrix[j : j + 1, :]
        inv = 1.0 / matrix[j : j + 1, j : j + 1]
        row = jnp.where(lane1 == j, inv, row * inv)
        rest = jnp.where(lane == j, 0.0, matrix) - column * row
        matrix = jnp.where(sub == j, row, rest)
    matrix = jnp.concatenate([matrix[8:], matrix[:8]], axis=0)
    return pltpu.roll(matrix, E - 8, 1)


def sweep_some(count, *matrices):
    return lax.fori_loop(0, count, lambda _, ms: tuple(sweep_panel(m) for m in ms), matrices)


def kernel(
    states_h, pos, gw_h, uw_h, dw_h, cov_h, tgt,
    out,
    states, gw, uw, dw, cbuf, gate, up, ra1, rb1, rc1, ra2,
    chi, clo, piece, bc, wc, bhl, whl, vv, vk, va, wr,
    part, rk, pa, xr, res, tp, m0, n12, n3, mc, nc, mc2, mzr, nzr, n3r, gsum, tmp, send, recv, local,
):
    a = lax.axis_index("row")
    b = lax.axis_index("col")
    x, y = a // 4, a % 4
    z, k = b // 2, b % 2

    def dev_x(d):
        return {"row": ((x + d) % 4) * 4 + y}

    def dev_y(d):
        return {"row": x * 4 + (y + d) % 4}

    def dev_z(d):
        return {"col": ((z + d) % 4) * 2 + k}

    others = [(i, j) for i in range(4) for j in range(4) if i + j > 0]

    def dev_xy(i, j):
        return {"row": ((x + i) % 4) * 4 + (y + j) % 4}

    dev_k = {"col": z * 2 + 1 - k}
    sent = []

    def cp(src, dst, dev):
        sem = len(sent)
        copy = pltpu.make_async_remote_copy(
            src_ref=src, dst_ref=dst, send_sem=send.at[sem], recv_sem=recv.at[sem],
            device_id=dev, device_id_type=pl.DeviceIdType.MESH,
        )
        copy.start()
        sent.append(copy)
        return copy

    loads = [
        pltpu.make_async_copy(src, dst, local.at[i])
        for i, (src, dst) in enumerate(((states_h, states), (gw_h, gw), (uw_h, uw), (dw_h, dw)))
    ]
    for load in loads:
        load.start()

    def cov_load(step, slot):
        return pltpu.make_async_copy(
            cov_h.at[pl.ds(pl.multiple_of(step * LINES, 8), LINES)], cbuf.at[slot], local.at[4 + slot]
        )

    cov_load(0, 0).start()

    barrier = pltpu.get_barrier_semaphore()
    peers = [dev_z(d) for d in (1, 2, 3)] + [dev_k]
    peers += [dev_xy(i, j) for i, j in others]
    for peer in peers:
        pl.semaphore_signal(barrier, inc=1, device_id=peer, device_id_type=pl.DeviceIdType.MESH)
    pl.semaphore_wait(barrier, len(peers))

    def ring_far(data, ra, me, dev):
        m2 = (me + 2) % 4
        return [cp(data(0, m2), ra(0), dev(1)), cp(data(1, m2), ra(1), dev(3))]

    def ring_near(data, rb, me, dev):
        return [cp(data(0, (me + 3) % 4), rb(0), dev(3)), cp(data(1, (me + 1) % 4), rb(1), dev(1))]

    def ring_middle(copies, data, ra, rc, me, dev):
        m1, m3 = (me + 1) % 4, (me + 3) % 4
        copies[0].wait_recv()
        data(0, m1)[...] += ra(0)[...]
        c0 = cp(data(0, m1), rc(0), dev(1))
        copies[1].wait_recv()
        data(1, m3)[...] += ra(1)[...]
        c1 = cp(data(1, m3), rc(1), dev(3))
        return [c0, c1]

    def ring_end(copies, data, rb, rc, me):
        for copy in copies:
            copy.wait_recv()
        for h in (0, 1):
            data(h, me)[...] += rb(h)[...] + rc(h)[...]

    def to_three(src, dst, dev):
        return [cp(src(d), dst(d), dev(d)) for d in (1, 2, 3)]

    def wait_all(copies):
        for copy in copies:
            copy.wait_recv()

    loads[0].wait()
    tokens = []
    for p in (0, 1):
        where = pos[p : p + 1, :]
        chosen = jnp.zeros((336, E), F32)
        for s in range(8):
            chosen = jnp.where(where == s, states[p, s].astype(F32), chosen)
        tokens.append(chosen.astype(BF16))
    tokens = jnp.concatenate(tokens, axis=1)

    def project(weight, target, by_y):
        for j in range(7):
            value = dot_tb(weight[:, j * 384 : (j + 1) * 384], tokens)
            row = j * 384
            while row < (j + 1) * 384:
                block, off = row // PIECE, row % PIECE
                size = min(PIECE - off, (j + 1) * 384 - row)
                first, second = (block % 4, block // 4) if by_y else (block // 4, block % 4)
                lines = value[row - j * 384 : row - j * 384 + size]
                target[0, first, second, off : off + size] = lines[:, :E]
                target[1, first, second, off : off + size] = lines[:, E:]
                row += size

    def gate_data(h, t):
        return gate.at[h, t]

    def up_data(h, t):
        return up.at[h, t]

    def buf(ref, which):
        return lambda h: ref.at[which, h]

    def cov_step(step, carry):
        slot = step % 2

        @pl.when(step + 1 < COV_STEPS)
        def _():
            cov_load(step + 1, 1 - slot).start()

        cov_load(step, slot).wait()
        rows = pl.ds(pl.multiple_of(step * COV_ROWS, 16), COV_ROWS)
        for t in range(21):
            high, low = halves(cbuf[slot, pl.ds(t, COV_ROWS, stride=21), :])
            chi[rows, t * E : (t + 1) * E] = high
            clo[rows, t * E : (t + 1) * E] = low
        return carry

    loads[1].wait()
    project(gw, gate, False)
    g_far = ring_far(gate_data, buf(ra1, 0), x, dev_x)
    loads[2].wait()
    project(uw, up, True)
    u_far = ring_far(up_data, buf(ra1, 1), y, dev_y)
    g_near = ring_near(gate_data, buf(rb1, 0), x, dev_x)
    lax.fori_loop(0, 3, cov_step, 0)
    u_near = ring_near(up_data, buf(rb1, 1), y, dev_y)
    lax.fori_loop(3, 6, cov_step, 0)
    g_near += ring_middle(g_far, gate_data, buf(ra1, 0), buf(rc1, 0), x, dev_x)
    lax.fori_loop(6, 8, cov_step, 0)
    u_near += ring_middle(u_far, up_data, buf(ra1, 1), buf(rc1, 1), y, dev_y)
    lax.fori_loop(8, COV_STEPS, cov_step, 0)
    ring_end(g_near, gate_data, buf(rb1, 0), buf(rc1, 0), x)
    g2 = to_three(lambda d: gate.at[:, x, (y + d) % 4], lambda d: ra2.at[0, d - 1], dev_y)
    ring_end(u_near, up_data, buf(rb1, 1), buf(rc1, 1), y)
    u2 = to_three(lambda d: up.at[:, y, (x + d) % 4], lambda d: ra2.at[1, d - 1], dev_x)
    wait_all(g2)
    wait_all(u2)

    keys = jnp.zeros((PIECE, E), F32)
    for p in (0, 1):
        v = gate[p, x, y] + ((ra2[0, 0, p] + ra2[0, 1, p]) + ra2[0, 2, p])
        u = up[p, y, x] + ((ra2[1, 0, p] + ra2[1, 1, p]) + ra2[1, 2, p])
        keys = keys + v / (1.0 + jnp.exp(-v)) * u
    keys = keys * 0.5
    keys_half = keys.astype(BF16)
    piece[0] = 4.0 / math.sqrt(FF) * keys
    top, low = pl.ds(0, 88), pl.ds(88, 80)

    def gather_start(field, own):
        field[x, y] = piece[own]
        at, ab = field.at[x, y, top], field.at[x, y, low]
        first = [cp(at, at, dev_x(d)) for d in (1, 3, 2)] + [cp(ab, ab, dev_y(d)) for d in (1, 3, 2)]
        return first, [cp(ab, ab, dev_x(d)) for d in (1, 3, 2)] + [cp(at, at, dev_y(d)) for d in (1, 3, 2)]

    def gather_next(copies, field):
        first, rest = copies
        rest = list(rest)
        for i, d in enumerate((3, 1, 2)):
            first[i].wait_recv()
            at = field.at[(x + d) % 4, y, top]
            rest += to_three(lambda e: at, lambda e: at, dev_y)
            first[i + 3].wait_recv()
            ab = field.at[x, (y + d) % 4, low]
            rest += to_three(lambda e: ab, lambda e: ab, dev_x)
        return rest

    def split_field(field, target):
        def body(i, carry):
            rows = pl.ds(pl.multiple_of(i * 336, 16), 336)
            high, rest = halves(field[i // 2, pl.ds((i % 2) * 2, 2)].reshape(336, E))
            target[rows, :E] = high
            target[rows, E:] = rest
            return carry

        lax.fori_loop(0, 8, body, 0)

    def gram(left, right):
        def body(i, total):
            rows = pl.ds(pl.multiple_of(i * 336, 16), 336)
            return total + dot_tb(left[rows, :], right[rows, :])

        total = lax.fori_loop(0, 8, body, jnp.zeros((2 * E, 2 * E), F32))
        return (total[:E, :E] + total[E:, E:]) + (total[:E, E:] + total[E:, :E])

    def cov_times(i, target):
        rows = pl.ds(pl.multiple_of(i * 336, 16), 336)
        both = dot_b(chi[rows, :], target[...])
        return both[:, :E] + (both[:, E:] + dot_b(clo[rows, :], target[:, :E]))

    bg = gather_start(bc, 0)

    loads[3].wait()
    tp[...] = jnp.zeros_like(tp)
    tp[0:42, :] = tgt[...]
    first = (a * 8 + b) * 42
    t_high, t_rest = tp[...].astype(BF16), tp[...] - tp[...].astype(BF16).astype(F32)
    t_mid, t_low = halves(t_rest)
    t_all = jnp.concatenate([t_high, t_mid, t_low], axis=0)
    minus = -keys_half

    def current(j, carry):
        at = pl.multiple_of(j * 384, 128)
        place = lax.broadcasted_iota(jnp.int32, (48, 384), 1) + j * 384 - first
        mark = jnp.where(place == lax.broadcasted_iota(jnp.int32, (48, 384), 0), 1.0, 0.0).astype(BF16)
        value = dot_tb(minus, dw[:, pl.ds(at, 384)]) + dot_tb(t_all, jnp.concatenate([mark, mark, mark], axis=0))
        for i in range(3):
            part[j * 3 + i] = value[:, i * E : (i + 1) * E]
        return carry

    lax.fori_loop(0, 14, current, 0)
    for i in range(42, 48):
        part[i] = jnp.zeros((E, E), F32)
    real = pl.ds(0, 42)

    def half_of(kk):
        return pl.ds(pl.multiple_of(kk * 64, 8), 64)

    def rows_of(zz):
        return pl.ds(pl.multiple_of(k * 64 + zz * 16, 8), 16)

    p1 = cp(part.at[real, half_of(1 - k)], rk, dev_k)
    bg = gather_next(bg, bc)
    p1.wait_recv()

    def add_half(i, carry):
        part[i, half_of(k), :] += rk[i]
        return carry

    lax.fori_loop(0, 42, add_half, 0)
    own_rows = rows_of(z)
    pz = to_three(lambda d: part.at[real, rows_of((z + d) % 4)], lambda d: pa.at[d - 1], dev_z)
    wait_all(bg)
    split_field(bc, bhl)

    def halve(ref, i, value):
        ref[i, 0] = value[:64]
        ref[i, 1] = value[64:]

    def cores_start(ref, n, got):
        return cp(ref.at[pl.ds(0, n), 1 - k], got.at[pl.ds(0, n)], dev_k)

    def cores_end(copy, ref, n, got):
        copy.wait_recv()
        ref[pl.ds(0, n), k] += got[pl.ds(0, n)]

    def axis_start(ref, n, got, dev):
        return to_three(lambda d: ref.at[pl.ds(0, n), k], lambda d: got.at[d - 1, pl.ds(0, n)], dev)

    def axis_end(copies, ref, n, got, target):
        wait_all(copies)
        target[pl.ds(0, n), k] = ref[pl.ds(0, n), k] + ((got[0, pl.ds(0, n)] + got[1, pl.ds(0, n)]) + got[2, pl.ds(0, n)])

    def cores_share(ref):
        return cp(ref.at[:, k], ref.at[:, k], dev_k)

    def first_image(i, carry):
        value = cov_times(i, bhl)
        vv[i, 0] = value[:PIECE]
        vv[i, 1] = value[PIECE:]
        return carry

    lax.fori_loop(0, 4, first_image, 0)
    v1 = cp(vv.at[:, 1 - k], vk, dev_k)
    halve(m0, 0, gram(bhl, bhl))
    mk = cores_start(m0, 1, mc)
    v1.wait_recv()
    vv[:, k] += vk[...]

    vz = to_three(lambda d: vv.at[(z + d) % 4, k], lambda d: va.at[d - 1], dev_z)
    cores_end(mk, m0, 1, mc)
    wait_all(vz)
    piece[1] = vv[z, k] + ((va[0] + va[1]) + va[2])
    wg = gather_start(wc, 1)
    wr[z, k] = piece[1]
    wz = to_three(lambda d: wr.at[z, k], lambda d: wr.at[z, k], dev_z)
    mz = axis_start(m0, 1, mzr, dev_z)
    wg = gather_next(wg, wc)

    def three(xx, yy):
        return pl.ds(xx * 12 + yy * 3, 3)

    wait_all(pz)
    part[real, own_rows] += (pa[0] + pa[1]) + pa[2]
    px = [
        cp(part.at[three((x + i) % 4, (y + j) % 4), own_rows], xr.at[n], dev_xy(i, j))
        for n, (i, j) in enumerate(others)
    ]
    wait_all(wz)
    wk = cp(wr.at[:, k], wr.at[:, k], dev_k)
    axis_end(mz, m0, 1, mzr, gsum)
    wait_all(wg)
    split_field(wc, whl)
    wk.wait_recv()

    def second_image(i, total):
        value = cov_times(i, whl)
        return total + dot_t(wr[i].reshape(336, E), value)

    total = lax.fori_loop(0, 4, second_image, jnp.zeros((E, E), F32))
    halve(n3, 0, total)
    n3k = cores_start(n3, 1, mc2)
    wait_all(px)
    mine = part[three(x, y), own_rows]
    for n in range(15):
        mine = mine + xr[n]
    res[three(x, y), own_rows] = mine
    own = res.at[three(x, y), own_rows]
    rx = [cp(own, own, dev_xy(i, j)) for i, j in others]
    cores_end(n3k, n3, 1, mc2)
    n3z = axis_start(n3, 1, n3r.at[0], dev_z)
    halve(n12, 0, gram(bhl, whl))
    halve(n12, 1, gram(whl, whl))
    nk = cores_start(n12, 2, nc)
    axis_end(n3z, n3, 1, n3r.at[0], n3.at[pl.ds(1, 1)])
    n3y = axis_start(n3.at[pl.ds(1, 1)], 1, n3r.at[1], dev_y)
    cores_end(nk, n12, 2, nc)
    nz = axis_start(n12, 2, nzr, dev_z)
    wait_all(rx)
    own_z = res.at[real, own_rows]
    rz = to_three(lambda d: own_z, lambda d: own_z, dev_z)
    axis_end(n3y, n3.at[pl.ds(1, 1)], 1, n3r.at[1], n3.at[pl.ds(2, 1)])
    n3x = axis_start(n3.at[pl.ds(2, 1)], 1, n3r.at[2], dev_x)
    axis_end(nz, n12, 2, nzr, gsum.at[pl.ds(1, 2)])
    gs = cores_share(gsum)
    gs.wait_recv()

    def whole(ref, i):
        return jnp.concatenate([ref[i, 0], ref[i, 1]], axis=0)

    gram0, n1, n2 = sym(whole(gsum, 0)), sym(whole(gsum, 1)), sym(whole(gsum, 2))
    square = dot(gram0, gram0)
    m1 = sym(n1 + square)
    inv0, inv1 = sweep_some(5, gram0, m1)
    axis_end(n3x, n3.at[pl.ds(2, 1)], 1, n3r.at[2], n3.at[pl.ds(3, 1)])
    n3s = cores_share(n3.at[pl.ds(3, 1)])
    inv0, inv1 = sweep_some(11, inv0, inv1)
    n1m0 = dot(n1, gram0)
    m2 = sym(n2 + n1m0 + n1m0.T + dot(square, gram0))
    n2m0 = dot(n2, gram0)
    m3_rest = sym(n2m0 + n2m0.T + dot(gram0, n1m0) + dot(m1, m1))
    alpha0 = dot(inv1, gram0)
    norm1 = sym(dot_t(alpha0, dot(m2, alpha0)) - gram0)
    beta = dot(inv0, norm1)
    eye = jnp.where(
        lax.broadcasted_iota(jnp.int32, (E, E), 0) == lax.broadcasted_iota(jnp.int32, (E, E), 1), 1.0, 0.0
    )
    c1 = eye + beta
    cross = dot_t(c1, dot(m2, alpha0))
    curv_rest = dot_t(c1, dot(m1, c1)) - cross - cross.T
    n3s.wait_recv()
    m3 = m3_rest + sym(whole(n3, 3))
    curvature = sym(curv_rest + dot_t(alpha0, dot(m3, alpha0)))
    wait_all(rz)
    half = res.at[real, half_of(k)]
    rkk = cp(half, half, dev_k)
    (inv2,) = sweep_some(16, curvature)
    alpha1 = dot(inv2, norm1)
    on_w = -dot(alpha0, alpha1)
    tmp[0] = dot(c1, alpha1)
    tmp[1] = dot(gram0, on_w)
    on_b = alpha0 + (tmp[0] + tmp[1])
    fh, fl = halves(jnp.concatenate([piece[0], piece[1]], axis=1))
    ch, cl = halves(jnp.concatenate([on_b, on_w], axis=0))
    found = dot_b(fh, ch) + (dot_b(fh, cl) + dot_b(fl, ch))
    xh, xl = halves(found)
    xhh = jnp.concatenate([xh, xh], axis=1)
    rkk.wait_recv()

    def update(j, carry):
        right = jnp.concatenate([res[j * 2], res[j * 2 + 1]], axis=1)
        rh, rl = halves(right)
        value = dot_b(xhh, jnp.concatenate([rh, rl], axis=0)) + dot_b(xl, rh)
        out[:, pl.ds(pl.multiple_of(j * 256, 128), 256)] = value.astype(BF16)
        return carry

    lax.fori_loop(0, 21, update, 0)
    for copy in sent:
        copy.wait_send()


def body(states, subject_pos, gate_weight, up_weight, down_weight, covariance, targets):
    vmem = pl.BlockSpec(memory_space=pltpu.VMEM)
    anyw = pl.BlockSpec(memory_space=pl.ANY)
    small = lambda *dims: pltpu.VMEM(dims, F32)
    update = pl.pallas_call(
        kernel,
        out_shape=jax.ShapeDtypeStruct((PIECE, D), BF16),
        in_specs=[anyw, vmem, anyw, anyw, anyw, anyw, vmem],
        out_specs=vmem,
        scratch_shapes=[
            pltpu.VMEM((2, 8, 336, E), BF16),
            pltpu.VMEM((336, 2688), BF16),
            pltpu.VMEM((336, 2688), BF16),
            pltpu.VMEM((PIECE, D), BF16),
            small(2, LINES, E),
            small(2, 4, 4, PIECE, E),
            small(2, 4, 4, PIECE, E),
            small(2, 2, 4, PIECE, E),
            small(2, 2, 4, PIECE, E),
            small(2, 2, 4, PIECE, E),
            small(2, 3, 2, PIECE, E),
            pltpu.VMEM((1344, 2688), BF16),
            pltpu.VMEM((1344, 2688), BF16),
            small(2, PIECE, E),
            small(4, 4, PIECE, E),
            small(4, 4, PIECE, E),
            pltpu.VMEM((2688, 2 * E), BF16),
            pltpu.VMEM((2688, 2 * E), BF16),
            small(4, 2, PIECE, E),
            small(4, PIECE, E),
            small(3, PIECE, E),
            small(4, 2, PIECE, E),
            small(48, E, E),
            small(42, 64, E),
            small(3, 42, 16, E),
            small(15, 3, 16, E),
            small(48, E, E),
            small(48, E),
            small(1, 2, 64, E),
            small(2, 2, 64, E),
            small(4, 2, 64, E),
            small(1, 64, E),
            small(2, 64, E),
            small(1, 64, E),
            small(3, 1, 64, E),
            small(3, 2, 64, E),
            small(3, 3, 1, 64, E),
            small(3, 2, 64, E),
            small(2, E, E),
            pltpu.SemaphoreType.DMA((N_SEM,)),
            pltpu.SemaphoreType.DMA((N_SEM,)),
            pltpu.SemaphoreType.DMA((6,)),
        ],
        compiler_params=pltpu.CompilerParams(
            collective_id=0, has_side_effects=True, vmem_limit_bytes=60 * 1024 * 1024
        ),
        name="edit",
    )(
        jnp.transpose(states, (1, 2, 3, 0)),
        subject_pos.T,
        gate_weight.reshape(336, 2688),
        up_weight.reshape(336, 2688),
        down_weight.reshape(PIECE, D),
        covariance.reshape(1344 * 21, E),
        targets,
    )
    return update.reshape(1, 1, PIECE, D)


def solution(mesh):
    return jax.shard_map(
        body,
        mesh=mesh,
        in_specs=(
            P(None, None, None, "row"),
            P(),
            P("row", "col", None),
            P("row", "col", None),
            P("row", "col", None, None),
            P("row", "col", None),
            P(("row", "col"), None),
        ),
        out_specs=P("row", "col", None, None),
        check_vma=False,
    )
```

```python
import math

import jax
import jax.numpy as jnp
from jax import lax
from jax.experimental import pallas as pl
from jax.experimental.pallas import tpu as pltpu
from jax.sharding import PartitionSpec as P

FF = 21504
D = 5376
PIECE = 168
E = 128
F32 = jnp.float32
BF16 = jnp.bfloat16
HI = lax.Precision.HIGHEST
N_SEM = 180
COV_ROWS = 112
COV_STEPS = 1344 // COV_ROWS
LINES = COV_ROWS * 21


def dot(left, right):
    return lax.dot_general(left, right, (((1,), (0,)), ((), ())), precision=HI, preferred_element_type=F32)


def dot_t(left, right):
    return lax.dot_general(left, right, (((0,), (0,)), ((), ())), precision=HI, preferred_element_type=F32)


def dot_b(left, right):
    return lax.dot_general(left, right, (((1,), (0,)), ((), ())), preferred_element_type=F32)


def dot_tb(left, right):
    return lax.dot_general(left, right, (((0,), (0,)), ((), ())), preferred_element_type=F32)


def halves(value):
    high = value.astype(BF16)
    return high, (value - high.astype(F32)).astype(BF16)


def sym(matrix):
    return 0.5 * (matrix + matrix.T)


def sweep_panel(matrix):
    lane8 = lax.broadcasted_iota(jnp.int32, (8, E), 1)
    sub8 = lax.broadcasted_iota(jnp.int32, (8, E), 0)
    lane = lax.broadcasted_iota(jnp.int32, (E - 8, E), 1)
    lane1 = lax.broadcasted_iota(jnp.int32, (1, E), 1)
    top, rest = matrix[:8], matrix[8:]
    for base in (0, 4):
        tops = [jnp.broadcast_to(top[:, base + j : base + j + 1], (8, E)) for j in range(4)]
        rests = [jnp.broadcast_to(rest[:, base + j : base + j + 1], (E - 8, E)) for j in range(4)]
        for j in range(4):
            r = base + j
            inv = 1.0 / tops[j][r : r + 1, :]
            row = jnp.where(lane1 == r, inv, top[r : r + 1, :] * inv)
            rest = jnp.where(lane == r, 0.0, rest) - rests[j] * row
            top = jnp.where(sub8 == r, row, jnp.where(lane8 == r, 0.0, top) - tops[j] * row)
            for m in range(j + 1, 4):
                factor = tops[m][r : r + 1, :] * inv
                rests[m] = rests[m] - rests[j] * factor
                tops[m] = jnp.where(sub8 == r, factor, tops[m] - tops[j] * factor)
    return pltpu.roll(jnp.concatenate([rest, top], axis=0), E - 8, 1)


def sweep_some(count, *matrices):
    return lax.fori_loop(0, count, lambda _, ms: tuple(sweep_panel(m) for m in ms), matrices)


def kernel(
    states_h, pos, gw_h, uw_h, dw_h, cov_h, tgt,
    out,
    states, gw, uw, dw, cbuf, gate, up, ra1, rb1, rc1, ra2,
    chi, clo, piece, bc, wc, bhl, whl, vv, vk, va, wr,
    part, rk, pa, xr, res, tp, m0, n12, n3, mc, nc, mc2, mzr, nzr, n3r, gsum, tmp, send, recv, local,
):
    a = lax.axis_index("row")
    b = lax.axis_index("col")
    x, y = a // 4, a % 4
    z, k = b // 2, b % 2

    def dev_x(d):
        return {"row": ((x + d) % 4) * 4 + y}

    def dev_y(d):
        return {"row": x * 4 + (y + d) % 4}

    def dev_z(d):
        return {"col": ((z + d) % 4) * 2 + k}

    others = [(i, j) for i in range(4) for j in range(4) if i + j > 0]

    def dev_xy(i, j):
        return {"row": ((x + i) % 4) * 4 + (y + j) % 4}

    dev_k = {"col": z * 2 + 1 - k}
    sent = []

    def cp(src, dst, dev):
        sem = len(sent)
        copy = pltpu.make_async_remote_copy(
            src_ref=src, dst_ref=dst, send_sem=send.at[sem], recv_sem=recv.at[sem],
            device_id=dev, device_id_type=pl.DeviceIdType.MESH,
        )
        copy.start()
        sent.append(copy)
        return copy

    loads = [
        pltpu.make_async_copy(src, dst, local.at[i])
        for i, (src, dst) in enumerate(((states_h, states), (gw_h, gw), (uw_h, uw), (dw_h, dw)))
    ]
    for load in loads:
        load.start()

    def cov_load(step, slot):
        return pltpu.make_async_copy(
            cov_h.at[pl.ds(pl.multiple_of(step * LINES, 8), LINES)], cbuf.at[slot], local.at[4 + slot]
        )

    cov_load(0, 0).start()

    barrier = pltpu.get_barrier_semaphore()
    peers = [dev_z(d) for d in (1, 2, 3)] + [dev_k]
    peers += [dev_xy(i, j) for i, j in others]
    for peer in peers:
        pl.semaphore_signal(barrier, inc=1, device_id=peer, device_id_type=pl.DeviceIdType.MESH)
    pl.semaphore_wait(barrier, len(peers))

    def ring_far(data, ra, me, dev):
        m2 = (me + 2) % 4
        return [cp(data(0, m2), ra(0), dev(1)), cp(data(1, m2), ra(1), dev(3))]

    def ring_near(data, rb, me, dev):
        return [cp(data(0, (me + 3) % 4), rb(0), dev(3)), cp(data(1, (me + 1) % 4), rb(1), dev(1))]

    def ring_middle(copies, data, ra, rc, me, dev):
        m1, m3 = (me + 1) % 4, (me + 3) % 4
        copies[0].wait_recv()
        data(0, m1)[...] += ra(0)[...]
        c0 = cp(data(0, m1), rc(0), dev(1))
        copies[1].wait_recv()
        data(1, m3)[...] += ra(1)[...]
        c1 = cp(data(1, m3), rc(1), dev(3))
        return [c0, c1]

    def ring_end(copies, data, rb, rc, me):
        for copy in copies:
            copy.wait_recv()
        for h in (0, 1):
            data(h, me)[...] += rb(h)[...] + rc(h)[...]

    def to_three(src, dst, dev):
        return [cp(src(d), dst(d), dev(d)) for d in (1, 2, 3)]

    def wait_all(copies):
        for copy in copies:
            copy.wait_recv()

    loads[0].wait()
    tokens = []
    for p in (0, 1):
        where = pos[p : p + 1, :]
        chosen = jnp.zeros((336, E), F32)
        for s in range(8):
            chosen = jnp.where(where == s, states[p, s].astype(F32), chosen)
        tokens.append(chosen.astype(BF16))
    tokens = jnp.concatenate(tokens, axis=1)

    def project(weight, target, by_y):
        for j in range(7):
            value = dot_tb(weight[:, j * 384 : (j + 1) * 384], tokens)
            row = j * 384
            while row < (j + 1) * 384:
                block, off = row // PIECE, row % PIECE
                size = min(PIECE - off, (j + 1) * 384 - row)
                first, second = (block % 4, block // 4) if by_y else (block // 4, block % 4)
                lines = value[row - j * 384 : row - j * 384 + size]
                target[0, first, second, off : off + size] = lines[:, :E]
                target[1, first, second, off : off + size] = lines[:, E:]
                row += size

    def gate_data(h, t):
        return gate.at[h, t]

    def up_data(h, t):
        return up.at[h, t]

    def buf(ref, which):
        return lambda h: ref.at[which, h]

    def cov_step(step, carry):
        slot = step % 2

        @pl.when(step + 1 < COV_STEPS)
        def _():
            cov_load(step + 1, 1 - slot).start()

        cov_load(step, slot).wait()
        rows = pl.ds(pl.multiple_of(step * COV_ROWS, 16), COV_ROWS)
        for t in range(21):
            high, low = halves(cbuf[slot, pl.ds(t, COV_ROWS, stride=21), :])
            chi[rows, t * E : (t + 1) * E] = high
            clo[rows, t * E : (t + 1) * E] = low
        return carry

    loads[1].wait()
    project(gw, gate, False)
    g_far = ring_far(gate_data, buf(ra1, 0), x, dev_x)
    loads[2].wait()
    project(uw, up, True)
    u_far = ring_far(up_data, buf(ra1, 1), y, dev_y)
    g_near = ring_near(gate_data, buf(rb1, 0), x, dev_x)
    lax.fori_loop(0, 3, cov_step, 0)
    u_near = ring_near(up_data, buf(rb1, 1), y, dev_y)
    lax.fori_loop(3, 6, cov_step, 0)
    g_near += ring_middle(g_far, gate_data, buf(ra1, 0), buf(rc1, 0), x, dev_x)
    lax.fori_loop(6, 8, cov_step, 0)
    u_near += ring_middle(u_far, up_data, buf(ra1, 1), buf(rc1, 1), y, dev_y)
    lax.fori_loop(8, COV_STEPS, cov_step, 0)
    ring_end(g_near, gate_data, buf(rb1, 0), buf(rc1, 0), x)
    g2 = to_three(lambda d: gate.at[:, x, (y + d) % 4], lambda d: ra2.at[0, d - 1], dev_y)
    ring_end(u_near, up_data, buf(rb1, 1), buf(rc1, 1), y)
    u2 = to_three(lambda d: up.at[:, y, (x + d) % 4], lambda d: ra2.at[1, d - 1], dev_x)
    wait_all(g2)
    wait_all(u2)

    keys = jnp.zeros((PIECE, E), F32)
    for p in (0, 1):
        v = gate[p, x, y] + ((ra2[0, 0, p] + ra2[0, 1, p]) + ra2[0, 2, p])
        u = up[p, y, x] + ((ra2[1, 0, p] + ra2[1, 1, p]) + ra2[1, 2, p])
        keys = keys + v / (1.0 + jnp.exp(-v)) * u
    keys = keys * 0.5
    keys_half = keys.astype(BF16)
    piece[0] = 4.0 / math.sqrt(FF) * keys
    top, low = pl.ds(0, 88), pl.ds(88, 80)

    def gather_start(field, own):
        field[x, y] = piece[own]
        at, ab = field.at[x, y, top], field.at[x, y, low]
        first = [cp(at, at, dev_x(d)) for d in (1, 3, 2)] + [cp(ab, ab, dev_y(d)) for d in (1, 3, 2)]
        return first, [cp(ab, ab, dev_x(d)) for d in (1, 3, 2)] + [cp(at, at, dev_y(d)) for d in (1, 3, 2)]

    def gather_next(copies, field):
        first, rest = copies
        rest = list(rest)
        for i, d in enumerate((3, 1, 2)):
            first[i].wait_recv()
            at = field.at[(x + d) % 4, y, top]
            rest += to_three(lambda e: at, lambda e: at, dev_y)
            first[i + 3].wait_recv()
            ab = field.at[x, (y + d) % 4, low]
            rest += to_three(lambda e: ab, lambda e: ab, dev_x)
        return rest

    def split_field(field, target):
        def body(i, carry):
            rows = pl.ds(pl.multiple_of(i * 336, 16), 336)
            high, rest = halves(field[i // 2, pl.ds((i % 2) * 2, 2)].reshape(336, E))
            target[rows, :E] = high
            target[rows, E:] = rest
            return carry

        lax.fori_loop(0, 8, body, 0)

    def gram(left, right):
        def body(i, total):
            rows = pl.ds(pl.multiple_of(i * 336, 16), 336)
            return total + dot_tb(left[rows, :], right[rows, :])

        total = lax.fori_loop(0, 8, body, jnp.zeros((2 * E, 2 * E), F32))
        return (total[:E, :E] + total[E:, E:]) + (total[:E, E:] + total[E:, :E])

    def cov_times(i, target):
        rows = pl.ds(pl.multiple_of(i * 336, 16), 336)
        both = dot_b(chi[rows, :], target[...])
        return both[:, :E] + (both[:, E:] + dot_b(clo[rows, :], target[:, :E]))

    bg = gather_start(bc, 0)

    loads[3].wait()
    tp[...] = jnp.zeros_like(tp)
    tp[0:42, :] = tgt[...]
    first = (a * 8 + b) * 42
    t_high, t_rest = tp[...].astype(BF16), tp[...] - tp[...].astype(BF16).astype(F32)
    t_mid, t_low = halves(t_rest)
    t_all = jnp.concatenate([t_high, t_mid, t_low], axis=0)
    minus = -keys_half

    def current(j, carry):
        at = pl.multiple_of(j * 384, 128)
        place = lax.broadcasted_iota(jnp.int32, (48, 384), 1) + j * 384 - first
        mark = jnp.where(place == lax.broadcasted_iota(jnp.int32, (48, 384), 0), 1.0, 0.0).astype(BF16)
        value = dot_tb(minus, dw[:, pl.ds(at, 384)]) + dot_tb(t_all, jnp.concatenate([mark, mark, mark], axis=0))
        for i in range(3):
            part[j * 3 + i] = value[:, i * E : (i + 1) * E]
        return carry

    lax.fori_loop(0, 14, current, 0)
    for i in range(42, 48):
        part[i] = jnp.zeros((E, E), F32)
    real = pl.ds(0, 42)

    def half_of(kk):
        return pl.ds(pl.multiple_of(kk * 64, 8), 64)

    def rows_of(zz):
        return pl.ds(pl.multiple_of(k * 64 + zz * 16, 8), 16)

    p1 = cp(part.at[real, half_of(1 - k)], rk, dev_k)
    bg = gather_next(bg, bc)
    p1.wait_recv()

    def add_half(i, carry):
        part[i, half_of(k), :] += rk[i]
        return carry

    lax.fori_loop(0, 42, add_half, 0)
    own_rows = rows_of(z)
    pz = to_three(lambda d: part.at[real, rows_of((z + d) % 4)], lambda d: pa.at[d - 1], dev_z)
    wait_all(bg)
    split_field(bc, bhl)

    def halve(ref, i, value):
        ref[i, 0] = value[:64]
        ref[i, 1] = value[64:]

    def cores_start(ref, n, got):
        return cp(ref.at[pl.ds(0, n), 1 - k], got.at[pl.ds(0, n)], dev_k)

    def cores_end(copy, ref, n, got):
        copy.wait_recv()
        ref[pl.ds(0, n), k] += got[pl.ds(0, n)]

    def axis_start(ref, n, got, dev):
        return to_three(lambda d: ref.at[pl.ds(0, n), k], lambda d: got.at[d - 1, pl.ds(0, n)], dev)

    def axis_end(copies, ref, n, got, target):
        wait_all(copies)
        target[pl.ds(0, n), k] = ref[pl.ds(0, n), k] + ((got[0, pl.ds(0, n)] + got[1, pl.ds(0, n)]) + got[2, pl.ds(0, n)])

    def cores_share(ref):
        return cp(ref.at[:, k], ref.at[:, k], dev_k)

    def first_image(i, carry):
        value = cov_times(i, bhl)
        vv[i, 0] = value[:PIECE]
        vv[i, 1] = value[PIECE:]
        return carry

    lax.fori_loop(0, 4, first_image, 0)
    v1 = cp(vv.at[:, 1 - k], vk, dev_k)
    halve(m0, 0, gram(bhl, bhl))
    mk = cores_start(m0, 1, mc)
    v1.wait_recv()
    vv[:, k] += vk[...]

    vz = to_three(lambda d: vv.at[(z + d) % 4, k], lambda d: va.at[d - 1], dev_z)
    cores_end(mk, m0, 1, mc)
    wait_all(vz)
    piece[1] = vv[z, k] + ((va[0] + va[1]) + va[2])
    wg = gather_start(wc, 1)
    wr[z, k] = piece[1]
    wz = to_three(lambda d: wr.at[z, k], lambda d: wr.at[z, k], dev_z)
    mz = axis_start(m0, 1, mzr, dev_z)
    wg = gather_next(wg, wc)

    def three(xx, yy):
        return pl.ds(xx * 12 + yy * 3, 3)

    wait_all(pz)
    part[real, own_rows] += (pa[0] + pa[1]) + pa[2]
    px = [
        cp(part.at[three((x + i) % 4, (y + j) % 4), own_rows], xr.at[n], dev_xy(i, j))
        for n, (i, j) in enumerate(others)
    ]
    wait_all(wz)
    wk = cp(wr.at[:, k], wr.at[:, k], dev_k)
    axis_end(mz, m0, 1, mzr, gsum)
    wait_all(wg)
    split_field(wc, whl)
    halve(n12, 0, gram(bhl, whl))
    first_n = n12.at[pl.ds(0, 1)]
    nk = cores_start(first_n, 1, nc.at[pl.ds(0, 1)])
    wk.wait_recv()

    def second_image(i, total):
        value = cov_times(i, whl)
        return total + dot_t(wr[i].reshape(336, E), value)

    total = lax.fori_loop(0, 2, second_image, jnp.zeros((E, E), F32))
    cores_end(nk, first_n, 1, nc.at[pl.ds(0, 1)])
    nz = axis_start(first_n, 1, nzr.at[0], dev_z)
    total = lax.fori_loop(2, 4, second_image, total)
    halve(n3, 0, total)
    n3k = cores_start(n3, 1, mc2)
    wait_all(px)
    mine = part[three(x, y), own_rows]
    for n in range(15):
        mine = mine + xr[n]
    res[three(x, y), own_rows] = mine
    own = res.at[three(x, y), own_rows]
    cores_end(n3k, n3, 1, mc2)
    n3z = axis_start(n3, 1, n3r.at[0], dev_z)
    axis_end(nz, first_n, 1, nzr.at[0], gsum.at[pl.ds(1, 1)])
    gs = cores_share(gsum.at[pl.ds(0, 2)])
    rx = [cp(own, own, dev_xy(i, j)) for i, j in others]
    halve(n12, 1, gram(whl, whl))
    second_n = n12.at[pl.ds(1, 1)]
    nk = cores_start(second_n, 1, nc.at[pl.ds(1, 1)])
    gs.wait_recv()

    def whole(ref, i):
        return jnp.concatenate([ref[i, 0], ref[i, 1]], axis=0)

    gram0, n1 = sym(whole(gsum, 0)), sym(whole(gsum, 1))
    g11 = sym(n1 + dot(gram0, gram0))
    (inv1,) = sweep_some(2, g11)
    axis_end(n3z, n3, 1, n3r.at[0], n3.at[pl.ds(1, 1)])
    n3y = axis_start(n3.at[pl.ds(1, 1)], 1, n3r.at[1], dev_y)
    cores_end(nk, second_n, 1, nc.at[pl.ds(1, 1)])
    nz = axis_start(second_n, 1, nzr.at[1], dev_z)
    (inv1,) = sweep_some(6, inv1)
    axis_end(n3y, n3.at[pl.ds(1, 1)], 1, n3r.at[1], n3.at[pl.ds(2, 1)])
    n3x = axis_start(n3.at[pl.ds(2, 1)], 1, n3r.at[2], dev_x)
    axis_end(nz, second_n, 1, nzr.at[1], gsum.at[pl.ds(2, 1)])
    gs = cores_share(gsum.at[pl.ds(2, 1)])
    wait_all(rx)
    own_z = res.at[real, own_rows]
    rz = to_three(lambda d: own_z, lambda d: own_z, dev_z)
    (inv1,) = sweep_some(8, inv1)
    axis_end(n3x, n3.at[pl.ds(2, 1)], 1, n3r.at[2], n3.at[pl.ds(3, 1)])
    n3s = cores_share(n3.at[pl.ds(3, 1)])
    gs.wait_recv()
    g12 = sym(whole(gsum, 2)) + dot(gram0, n1)
    solved = dot(inv1, jnp.concatenate([g12, gram0], axis=1))
    taken = dot_t(g12, solved)
    g22 = dot(n1, n1)
    n3s.wait_recv()
    schur = sym(sym(whole(n3, 3)) + g22 - taken[:, :E])
    right2 = n1 - taken[:, E:]
    wait_all(rz)
    half = res.at[real, half_of(k)]
    rkk = cp(half, half, dev_k)
    (inv2,) = sweep_some(16, schur)
    on_w = dot(inv2, right2)
    tmp[0] = dot(solved[:, :E], on_w)
    on_b = solved[:, E:] - tmp[0]
    fh, fl = halves(jnp.concatenate([piece[0], piece[1]], axis=1))
    ch, cl = halves(jnp.concatenate([on_b, on_w], axis=0))
    found = dot_b(fh, ch) + (dot_b(fh, cl) + dot_b(fl, ch))
    xh, xl = halves(found)
    xhh = jnp.concatenate([xh, xh], axis=1)
    rkk.wait_recv()

    def update(j, carry):
        right = jnp.concatenate([res[j * 2], res[j * 2 + 1]], axis=1)
        rh, rl = halves(right)
        value = dot_b(xhh, jnp.concatenate([rh, rl], axis=0)) + dot_b(xl, rh)
        out[:, pl.ds(pl.multiple_of(j * 256, 128), 256)] = value.astype(BF16)
        return carry

    lax.fori_loop(0, 21, update, 0, unroll=3)
    for copy in sent:
        copy.wait_send()


def body(states, subject_pos, gate_weight, up_weight, down_weight, covariance, targets):
    vmem = pl.BlockSpec(memory_space=pltpu.VMEM)
    anyw = pl.BlockSpec(memory_space=pl.ANY)
    small = lambda *dims: pltpu.VMEM(dims, F32)
    update = pl.pallas_call(
        kernel,
        out_shape=jax.ShapeDtypeStruct((PIECE, D), BF16),
        in_specs=[anyw, vmem, anyw, anyw, anyw, anyw, vmem],
        out_specs=vmem,
        scratch_shapes=[
            pltpu.VMEM((2, 8, 336, E), BF16),
            pltpu.VMEM((336, 2688), BF16),
            pltpu.VMEM((336, 2688), BF16),
            pltpu.VMEM((PIECE, D), BF16),
            small(2, LINES, E),
            small(2, 4, 4, PIECE, E),
            small(2, 4, 4, PIECE, E),
            small(2, 2, 4, PIECE, E),
            small(2, 2, 4, PIECE, E),
            small(2, 2, 4, PIECE, E),
            small(2, 3, 2, PIECE, E),
            pltpu.VMEM((1344, 2688), BF16),
            pltpu.VMEM((1344, 2688), BF16),
            small(2, PIECE, E),
            small(4, 4, PIECE, E),
            small(4, 4, PIECE, E),
            pltpu.VMEM((2688, 2 * E), BF16),
            pltpu.VMEM((2688, 2 * E), BF16),
            small(4, 2, PIECE, E),
            small(4, PIECE, E),
            small(3, PIECE, E),
            small(4, 2, PIECE, E),
            small(48, E, E),
            small(42, 64, E),
            small(3, 42, 16, E),
            small(15, 3, 16, E),
            small(48, E, E),
            small(48, E),
            small(1, 2, 64, E),
            small(2, 2, 64, E),
            small(4, 2, 64, E),
            small(1, 64, E),
            small(2, 64, E),
            small(1, 64, E),
            small(3, 1, 64, E),
            small(2, 3, 1, 64, E),
            small(3, 3, 1, 64, E),
            small(3, 2, 64, E),
            small(1, E, E),
            pltpu.SemaphoreType.DMA((N_SEM,)),
            pltpu.SemaphoreType.DMA((N_SEM,)),
            pltpu.SemaphoreType.DMA((6,)),
        ],
        compiler_params=pltpu.CompilerParams(
            collective_id=0, has_side_effects=True, vmem_limit_bytes=60 * 1024 * 1024
        ),
        name="edit",
    )(
        jnp.transpose(states, (1, 2, 3, 0)),
        subject_pos.T,
        gate_weight.reshape(336, 2688),
        up_weight.reshape(336, 2688),
        down_weight.reshape(PIECE, D),
        covariance.reshape(1344 * 21, E),
        targets,
    )
    return update.reshape(1, 1, PIECE, D)


def solution(mesh):
    return jax.shard_map(
        body,
        mesh=mesh,
        in_specs=(
            P(None, None, None, "row"),
            P(),
            P("row", "col", None),
            P("row", "col", None),
            P("row", "col", None, None),
            P("row", "col", None),
            P(("row", "col"), None),
        ),
        out_specs=P("row", "col", None, None),
        check_vma=False,
    )
```

```python
import math

import jax
import jax.numpy as jnp
from jax import lax
from jax.experimental import pallas as pl
from jax.experimental.pallas import tpu as pltpu
from jax.sharding import PartitionSpec as P

FF = 21504
D = 5376
PIECE = 168
E = 128
F32 = jnp.float32
BF16 = jnp.bfloat16
HI = lax.Precision.HIGHEST
N_SEM = 180
COV_ROWS = 112
COV_STEPS = 1344 // COV_ROWS
LINES = COV_ROWS * 21


def dot(left, right):
    return lax.dot_general(left, right, (((1,), (0,)), ((), ())), precision=HI, preferred_element_type=F32)


def dot_t(left, right):
    return lax.dot_general(left, right, (((0,), (0,)), ((), ())), precision=HI, preferred_element_type=F32)


def dot_b(left, right):
    return lax.dot_general(left, right, (((1,), (0,)), ((), ())), preferred_element_type=F32)


def dot_tb(left, right):
    return lax.dot_general(left, right, (((0,), (0,)), ((), ())), preferred_element_type=F32)


def halves(value):
    high = value.astype(BF16)
    return high, (value - high.astype(F32)).astype(BF16)


def sym(matrix):
    return 0.5 * (matrix + matrix.T)


def sweep_panel(matrix):
    lane8 = lax.broadcasted_iota(jnp.int32, (8, E), 1)
    sub8 = lax.broadcasted_iota(jnp.int32, (8, E), 0)
    lane = lax.broadcasted_iota(jnp.int32, (E - 8, E), 1)
    lane1 = lax.broadcasted_iota(jnp.int32, (1, E), 1)
    top, rest = matrix[:8], matrix[8:]
    for base in (0, 4):
        tops = [jnp.broadcast_to(top[:, base + j : base + j + 1], (8, E)) for j in range(4)]
        rests = [jnp.broadcast_to(rest[:, base + j : base + j + 1], (E - 8, E)) for j in range(4)]
        for j in range(4):
            r = base + j
            inv = 1.0 / tops[j][r : r + 1, :]
            row = jnp.where(lane1 == r, inv, top[r : r + 1, :] * inv)
            rest = jnp.where(lane == r, 0.0, rest) - rests[j] * row
            top = jnp.where(sub8 == r, row, jnp.where(lane8 == r, 0.0, top) - tops[j] * row)
            for m in range(j + 1, 4):
                factor = tops[m][r : r + 1, :] * inv
                rests[m] = rests[m] - rests[j] * factor
                tops[m] = jnp.where(sub8 == r, factor, tops[m] - tops[j] * factor)
    return pltpu.roll(jnp.concatenate([rest, top], axis=0), E - 8, 1)


def sweep_some(count, *matrices):
    return lax.fori_loop(0, count, lambda _, ms: tuple(sweep_panel(m) for m in ms), matrices)


def kernel(
    states_h, pos, gw_h, uw_h, dw_h, cov_h, tgt,
    out,
    states, gw, uw, dw, cbuf, gate, up, ra1, rb1, rc1, ra2,
    chi, clo, piece, bc, wc, bhl, whl, vv, vk, va, wr,
    part, rk, pa, xr, res, tp, m0, n12, n3, mc, nc, mc2, mzr, nzr, n3r, gsum, tmp, send, recv, local,
):
    a = lax.axis_index("row")
    b = lax.axis_index("col")
    x, y = a // 4, a % 4
    z, k = b // 2, b % 2

    def dev_x(d):
        return {"row": ((x + d) % 4) * 4 + y}

    def dev_y(d):
        return {"row": x * 4 + (y + d) % 4}

    def dev_z(d):
        return {"col": ((z + d) % 4) * 2 + k}

    others = [(i, j) for i in range(4) for j in range(4) if i + j > 0]

    def dev_xy(i, j):
        return {"row": ((x + i) % 4) * 4 + (y + j) % 4}

    dev_k = {"col": z * 2 + 1 - k}
    sent = []

    def cp(src, dst, dev):
        sem = len(sent)
        copy = pltpu.make_async_remote_copy(
            src_ref=src, dst_ref=dst, send_sem=send.at[sem], recv_sem=recv.at[sem],
            device_id=dev, device_id_type=pl.DeviceIdType.MESH,
        )
        copy.start()
        sent.append(copy)
        return copy

    loads = [
        pltpu.make_async_copy(src, dst, local.at[i])
        for i, (src, dst) in enumerate(((states_h, states), (gw_h, gw), (uw_h, uw), (dw_h, dw)))
    ]
    for load in loads:
        load.start()

    def cov_load(step, slot):
        return pltpu.make_async_copy(
            cov_h.at[pl.ds(pl.multiple_of(step * LINES, 8), LINES)], cbuf.at[slot], local.at[4 + slot]
        )

    cov_load(0, 0).start()

    barrier = pltpu.get_barrier_semaphore()
    peers = [dev_z(d) for d in (1, 2, 3)] + [dev_k]
    peers += [dev_xy(i, j) for i, j in others]
    for peer in peers:
        pl.semaphore_signal(barrier, inc=1, device_id=peer, device_id_type=pl.DeviceIdType.MESH)

    def ring_far(data, ra, me, dev):
        m2 = (me + 2) % 4
        return [cp(data(0, m2), ra(0), dev(1)), cp(data(1, m2), ra(1), dev(3))]

    def ring_near(data, rb, me, dev):
        return [cp(data(0, (me + 3) % 4), rb(0), dev(3)), cp(data(1, (me + 1) % 4), rb(1), dev(1))]

    def ring_middle(copies, data, ra, rc, me, dev):
        m1, m3 = (me + 1) % 4, (me + 3) % 4
        copies[0].wait_recv()
        data(0, m1)[...] += ra(0)[...]
        c0 = cp(data(0, m1), rc(0), dev(1))
        copies[1].wait_recv()
        data(1, m3)[...] += ra(1)[...]
        c1 = cp(data(1, m3), rc(1), dev(3))
        return [c0, c1]

    def ring_end(copies, data, rb, rc, me):
        for copy in copies:
            copy.wait_recv()
        for h in (0, 1):
            data(h, me)[...] += rb(h)[...] + rc(h)[...]

    def to_three(src, dst, dev):
        return [cp(src(d), dst(d), dev(d)) for d in (1, 2, 3)]

    def wait_all(copies):
        for copy in copies:
            copy.wait_recv()

    loads[0].wait()
    tokens = []
    for p in (0, 1):
        where = pos[p : p + 1, :]
        chosen = jnp.zeros((336, E), F32)
        for s in range(8):
            chosen = jnp.where(where == s, states[p, s].astype(F32), chosen)
        tokens.append(chosen.astype(BF16))
    tokens = jnp.concatenate(tokens, axis=1)

    def project(weight, target, by_y):
        for j in range(7):
            value = dot_tb(weight[:, j * 384 : (j + 1) * 384], tokens)
            row = j * 384
            while row < (j + 1) * 384:
                block, off = row // PIECE, row % PIECE
                size = min(PIECE - off, (j + 1) * 384 - row)
                first, second = (block % 4, block // 4) if by_y else (block // 4, block % 4)
                lines = value[row - j * 384 : row - j * 384 + size]
                target[0, first, second, off : off + size] = lines[:, :E]
                target[1, first, second, off : off + size] = lines[:, E:]
                row += size

    def gate_data(h, t):
        return gate.at[h, t]

    def up_data(h, t):
        return up.at[h, t]

    def buf(ref, which):
        return lambda h: ref.at[which, h]

    def cov_step(step, carry):
        slot = step % 2

        @pl.when(step + 1 < COV_STEPS)
        def _():
            cov_load(step + 1, 1 - slot).start()

        cov_load(step, slot).wait()
        rows = pl.ds(pl.multiple_of(step * COV_ROWS, 16), COV_ROWS)
        for t in range(21):
            high, low = halves(cbuf[slot, pl.ds(t, COV_ROWS, stride=21), :])
            chi[rows, t * E : (t + 1) * E] = high
            clo[rows, t * E : (t + 1) * E] = low
        return carry

    loads[1].wait()
    project(gw, gate, False)
    pl.semaphore_wait(barrier, len(peers))
    g_far = ring_far(gate_data, buf(ra1, 0), x, dev_x)
    loads[2].wait()
    project(uw, up, True)
    u_far = ring_far(up_data, buf(ra1, 1), y, dev_y)
    lax.fori_loop(0, 6, cov_step, 0)
    g_near = ring_near(gate_data, buf(rb1, 0), x, dev_x)
    lax.fori_loop(6, 7, cov_step, 0)
    u_near = ring_near(up_data, buf(rb1, 1), y, dev_y)
    lax.fori_loop(7, 10, cov_step, 0)
    g_near += ring_middle(g_far, gate_data, buf(ra1, 0), buf(rc1, 0), x, dev_x)
    u_near += ring_middle(u_far, up_data, buf(ra1, 1), buf(rc1, 1), y, dev_y)
    lax.fori_loop(10, COV_STEPS, cov_step, 0)
    ring_end(g_near, gate_data, buf(rb1, 0), buf(rc1, 0), x)
    g2 = to_three(lambda d: gate.at[:, x, (y + d) % 4], lambda d: ra2.at[0, d - 1], dev_y)
    ring_end(u_near, up_data, buf(rb1, 1), buf(rc1, 1), y)
    u2 = to_three(lambda d: up.at[:, y, (x + d) % 4], lambda d: ra2.at[1, d - 1], dev_x)
    wait_all(g2)
    wait_all(u2)

    keys = jnp.zeros((PIECE, E), F32)
    for p in (0, 1):
        v = gate[p, x, y] + ((ra2[0, 0, p] + ra2[0, 1, p]) + ra2[0, 2, p])
        u = up[p, y, x] + ((ra2[1, 0, p] + ra2[1, 1, p]) + ra2[1, 2, p])
        keys = keys + v / (1.0 + jnp.exp(-v)) * u
    keys = keys * 0.5
    keys_half = keys.astype(BF16)
    piece[0] = 4.0 / math.sqrt(FF) * keys
    top, low = pl.ds(0, 88), pl.ds(88, 80)

    def gather_start(field, own):
        field[x, y] = piece[own]
        at, ab = field.at[x, y, top], field.at[x, y, low]
        first = [cp(at, at, dev_x(d)) for d in (1, 3, 2)] + [cp(ab, ab, dev_y(d)) for d in (1, 3, 2)]
        return first, [cp(ab, ab, dev_x(d)) for d in (1, 3, 2)] + [cp(at, at, dev_y(d)) for d in (1, 3, 2)]

    def gather_next(copies, field):
        first, rest = copies
        rest = list(rest)
        for i, d in enumerate((3, 1, 2)):
            first[i].wait_recv()
            at = field.at[(x + d) % 4, y, top]
            rest += to_three(lambda e: at, lambda e: at, dev_y)
            first[i + 3].wait_recv()
            ab = field.at[x, (y + d) % 4, low]
            rest += to_three(lambda e: ab, lambda e: ab, dev_x)
        return rest

    def split_field(field, target):
        def body(i, carry):
            rows = pl.ds(pl.multiple_of(i * 336, 16), 336)
            high, rest = halves(field[i // 2, pl.ds((i % 2) * 2, 2)].reshape(336, E))
            target[rows, :E] = high
            target[rows, E:] = rest
            return carry

        lax.fori_loop(0, 8, body, 0)

    def gram(left, right):
        def body(i, total):
            rows = pl.ds(pl.multiple_of(i * 336, 16), 336)
            return total + dot_tb(left[rows, :], right[rows, :])

        total = lax.fori_loop(0, 8, body, jnp.zeros((2 * E, 2 * E), F32))
        return (total[:E, :E] + total[E:, E:]) + (total[:E, E:] + total[E:, :E])

    def cov_times(i, target):
        rows = pl.ds(pl.multiple_of(i * 336, 16), 336)
        both = dot_b(chi[rows, :], target[...])
        return both[:, :E] + (both[:, E:] + dot_b(clo[rows, :], target[:, :E]))

    bg = gather_start(bc, 0)

    loads[3].wait()
    tp[...] = jnp.zeros_like(tp)
    tp[0:42, :] = tgt[...]
    first = (a * 8 + b) * 42
    t_high, t_rest = tp[...].astype(BF16), tp[...] - tp[...].astype(BF16).astype(F32)
    t_mid, t_low = halves(t_rest)
    t_all = jnp.concatenate([t_high, t_mid, t_low], axis=0)
    minus = -keys_half

    def current(j, carry):
        at = pl.multiple_of(j * 384, 128)
        place = lax.broadcasted_iota(jnp.int32, (48, 384), 1) + j * 384 - first
        mark = jnp.where(place == lax.broadcasted_iota(jnp.int32, (48, 384), 0), 1.0, 0.0).astype(BF16)
        value = dot_tb(minus, dw[:, pl.ds(at, 384)]) + dot_tb(t_all, jnp.concatenate([mark, mark, mark], axis=0))
        for i in range(3):
            part[j * 3 + i] = value[:, i * E : (i + 1) * E]
        return carry

    lax.fori_loop(0, 14, current, 0)
    for i in range(42, 48):
        part[i] = jnp.zeros((E, E), F32)
    real = pl.ds(0, 42)

    def half_of(kk):
        return pl.ds(pl.multiple_of(kk * 64, 8), 64)

    def rows_of(zz):
        return pl.ds(pl.multiple_of(k * 64 + zz * 16, 8), 16)

    p1 = cp(part.at[real, half_of(1 - k)], rk, dev_k)
    bg = gather_next(bg, bc)
    p1.wait_recv()

    def add_half(i, carry):
        part[i, half_of(k), :] += rk[i]
        return carry

    lax.fori_loop(0, 42, add_half, 0)
    own_rows = rows_of(z)
    pz = to_three(lambda d: part.at[real, rows_of((z + d) % 4)], lambda d: pa.at[d - 1], dev_z)
    wait_all(bg)
    split_field(bc, bhl)

    def halve(ref, i, value):
        ref[i, 0] = value[:64]
        ref[i, 1] = value[64:]

    def cores_start(ref, n, got):
        return cp(ref.at[pl.ds(0, n), 1 - k], got.at[pl.ds(0, n)], dev_k)

    def cores_end(copy, ref, n, got):
        copy.wait_recv()
        ref[pl.ds(0, n), k] += got[pl.ds(0, n)]

    def axis_start(ref, n, got, dev):
        return to_three(lambda d: ref.at[pl.ds(0, n), k], lambda d: got.at[d - 1, pl.ds(0, n)], dev)

    def axis_end(copies, ref, n, got, target):
        wait_all(copies)
        target[pl.ds(0, n), k] = ref[pl.ds(0, n), k] + ((got[0, pl.ds(0, n)] + got[1, pl.ds(0, n)]) + got[2, pl.ds(0, n)])

    def cores_share(ref):
        return cp(ref.at[:, k], ref.at[:, k], dev_k)

    def first_image(i, carry):
        value = cov_times(i, bhl)
        vv[i, 0] = value[:PIECE]
        vv[i, 1] = value[PIECE:]
        return carry

    lax.fori_loop(0, 4, first_image, 0)
    v1 = cp(vv.at[:, 1 - k], vk, dev_k)
    v1.wait_recv()
    vv[:, k] += vk[...]
    vz = to_three(lambda d: vv.at[(z + d) % 4, k], lambda d: va.at[d - 1], dev_z)
    halve(m0, 0, gram(bhl, bhl))
    mk = cores_start(m0, 1, mc)

    def three(xx, yy):
        return pl.ds(xx * 12 + yy * 3, 3)

    wait_all(pz)
    part[real, own_rows] += (pa[0] + pa[1]) + pa[2]
    px = [
        cp(part.at[three((x + i) % 4, (y + j) % 4), own_rows], xr.at[n], dev_xy(i, j))
        for n, (i, j) in enumerate(others)
    ]
    wait_all(vz)
    piece[1] = vv[z, k] + ((va[0] + va[1]) + va[2])
    wg = gather_start(wc, 1)
    wr[z, k] = piece[1]
    wz = to_three(lambda d: wr.at[z, k], lambda d: wr.at[z, k], dev_z)
    cores_end(mk, m0, 1, mc)
    mz = axis_start(m0, 1, mzr, dev_z)
    wg = gather_next(wg, wc)
    wait_all(px)
    mine = part[three(x, y), own_rows]
    for n in range(15):
        mine = mine + xr[n]
    res[three(x, y), own_rows] = mine
    own = res.at[three(x, y), own_rows]
    rx = [cp(own, own, dev_xy(i, j)) for i, j in others]
    wait_all(wz)
    wk = cp(wr.at[:, k], wr.at[:, k], dev_k)
    axis_end(mz, m0, 1, mzr, gsum)
    wait_all(wg)
    split_field(wc, whl)
    halve(n12, 0, gram(bhl, whl))
    first_n = n12.at[pl.ds(0, 1)]
    nk = cores_start(first_n, 1, nc.at[pl.ds(0, 1)])
    wk.wait_recv()

    def second_image(i, total):
        value = cov_times(i, whl)
        return total + dot_t(wr[i].reshape(336, E), value)

    total = lax.fori_loop(0, 2, second_image, jnp.zeros((E, E), F32))
    cores_end(nk, first_n, 1, nc.at[pl.ds(0, 1)])
    nz = axis_start(first_n, 1, nzr.at[0], dev_z)
    wait_all(rx)
    own_z = res.at[real, own_rows]
    rz = to_three(lambda d: own_z, lambda d: own_z, dev_z)
    total = lax.fori_loop(2, 4, second_image, total)
    halve(n3, 0, total)
    n3k = cores_start(n3, 1, mc2)
    cores_end(n3k, n3, 1, mc2)
    n3z = axis_start(n3, 1, n3r.at[0], dev_z)
    axis_end(nz, first_n, 1, nzr.at[0], gsum.at[pl.ds(1, 1)])
    gs = cores_share(gsum.at[pl.ds(0, 2)])
    halve(n12, 1, gram(whl, whl))
    second_n = n12.at[pl.ds(1, 1)]
    nk = cores_start(second_n, 1, nc.at[pl.ds(1, 1)])
    gs.wait_recv()

    def whole(ref, i):
        return jnp.concatenate([ref[i, 0], ref[i, 1]], axis=0)

    gram0, n1 = sym(whole(gsum, 0)), sym(whole(gsum, 1))
    g11 = sym(n1 + dot(gram0, gram0))
    (inv1,) = sweep_some(2, g11)
    axis_end(n3z, n3, 1, n3r.at[0], n3.at[pl.ds(1, 1)])
    n3y = axis_start(n3.at[pl.ds(1, 1)], 1, n3r.at[1], dev_y)
    cores_end(nk, second_n, 1, nc.at[pl.ds(1, 1)])
    nz = axis_start(second_n, 1, nzr.at[1], dev_z)
    (inv1,) = sweep_some(6, inv1)
    axis_end(n3y, n3.at[pl.ds(1, 1)], 1, n3r.at[1], n3.at[pl.ds(2, 1)])
    n3x = axis_start(n3.at[pl.ds(2, 1)], 1, n3r.at[2], dev_x)
    axis_end(nz, second_n, 1, nzr.at[1], gsum.at[pl.ds(2, 1)])
    gs = cores_share(gsum.at[pl.ds(2, 1)])
    (inv1,) = sweep_some(8, inv1)
    axis_end(n3x, n3.at[pl.ds(2, 1)], 1, n3r.at[2], n3.at[pl.ds(3, 1)])
    n3s = cores_share(n3.at[pl.ds(3, 1)])
    gs.wait_recv()
    g12 = sym(whole(gsum, 2)) + dot(gram0, n1)
    solved = dot(inv1, jnp.concatenate([g12, gram0], axis=1))
    taken = dot_t(g12, solved)
    g22 = dot(n1, n1)
    n3s.wait_recv()
    schur = sym(sym(whole(n3, 3)) + g22 - taken[:, :E])
    right2 = n1 - taken[:, E:]
    wait_all(rz)
    half = res.at[real, half_of(k)]
    rkk = cp(half, half, dev_k)
    (inv2,) = sweep_some(16, schur)
    on_w = dot(inv2, right2)
    tmp[0] = dot(solved[:, :E], on_w)
    on_b = solved[:, E:] - tmp[0]
    fh, fl = halves(jnp.concatenate([piece[0], piece[1]], axis=1))
    ch, cl = halves(jnp.concatenate([on_b, on_w], axis=0))
    found = dot_b(fh, ch) + (dot_b(fh, cl) + dot_b(fl, ch))
    xh, xl = halves(found)
    xhh = jnp.concatenate([xh, xh], axis=1)
    rkk.wait_recv()

    def update(j, carry):
        right = jnp.concatenate([res[j * 2], res[j * 2 + 1]], axis=1)
        rh, rl = halves(right)
        value = dot_b(xhh, jnp.concatenate([rh, rl], axis=0)) + dot_b(xl, rh)
        out[:, pl.ds(pl.multiple_of(j * 256, 128), 256)] = value.astype(BF16)
        return carry

    lax.fori_loop(0, 21, update, 0, unroll=3)
    for copy in sent:
        copy.wait_send()


def body(states, subject_pos, gate_weight, up_weight, down_weight, covariance, targets):
    vmem = pl.BlockSpec(memory_space=pltpu.VMEM)
    anyw = pl.BlockSpec(memory_space=pl.ANY)
    small = lambda *dims: pltpu.VMEM(dims, F32)
    update = pl.pallas_call(
        kernel,
        out_shape=jax.ShapeDtypeStruct((PIECE, D), BF16),
        in_specs=[anyw, vmem, anyw, anyw, anyw, anyw, vmem],
        out_specs=vmem,
        scratch_shapes=[
            pltpu.VMEM((2, 8, 336, E), BF16),
            pltpu.VMEM((336, 2688), BF16),
            pltpu.VMEM((336, 2688), BF16),
            pltpu.VMEM((PIECE, D), BF16),
            small(2, LINES, E),
            small(2, 4, 4, PIECE, E),
            small(2, 4, 4, PIECE, E),
            small(2, 2, 4, PIECE, E),
            small(2, 2, 4, PIECE, E),
            small(2, 2, 4, PIECE, E),
            small(2, 3, 2, PIECE, E),
            pltpu.VMEM((1344, 2688), BF16),
            pltpu.VMEM((1344, 2688), BF16),
            small(2, PIECE, E),
            small(4, 4, PIECE, E),
            small(4, 4, PIECE, E),
            pltpu.VMEM((2688, 2 * E), BF16),
            pltpu.VMEM((2688, 2 * E), BF16),
            small(4, 2, PIECE, E),
            small(4, PIECE, E),
            small(3, PIECE, E),
            small(4, 2, PIECE, E),
            small(48, E, E),
            small(42, 64, E),
            small(3, 42, 16, E),
            small(15, 3, 16, E),
            small(48, E, E),
            small(48, E),
            small(1, 2, 64, E),
            small(2, 2, 64, E),
            small(4, 2, 64, E),
            small(1, 64, E),
            small(2, 64, E),
            small(1, 64, E),
            small(3, 1, 64, E),
            small(2, 3, 1, 64, E),
            small(3, 3, 1, 64, E),
            small(3, 2, 64, E),
            small(1, E, E),
            pltpu.SemaphoreType.DMA((N_SEM,)),
            pltpu.SemaphoreType.DMA((N_SEM,)),
            pltpu.SemaphoreType.DMA((6,)),
        ],
        compiler_params=pltpu.CompilerParams(
            collective_id=0, has_side_effects=True, vmem_limit_bytes=60 * 1024 * 1024
        ),
        name="edit",
    )(
        jnp.transpose(states, (1, 2, 3, 0)),
        subject_pos.T,
        gate_weight.reshape(336, 2688),
        up_weight.reshape(336, 2688),
        down_weight.reshape(PIECE, D),
        covariance.reshape(1344 * 21, E),
        targets,
    )
    return update.reshape(1, 1, PIECE, D)


def solution(mesh):
    return jax.shard_map(
        body,
        mesh=mesh,
        in_specs=(
            P(None, None, None, "row"),
            P(),
            P("row", "col", None),
            P("row", "col", None),
            P("row", "col", None, None),
            P("row", "col", None),
            P(("row", "col"), None),
        ),
        out_specs=P("row", "col", None, None),
        check_vma=False,
    )
```

```python
import math

import jax
import jax.numpy as jnp
from jax import lax
from jax.experimental import pallas as pl
from jax.experimental.pallas import tpu as pltpu
from jax.sharding import PartitionSpec as P

FF = 21504
D = 5376
PIECE = 168
E = 128
F32 = jnp.float32
BF16 = jnp.bfloat16
HI = lax.Precision.HIGHEST
N_SEM = 180
COV_ROWS = 112
COV_STEPS = 1344 // COV_ROWS
LINES = COV_ROWS * 21


def dot(left, right):
    return lax.dot_general(left, right, (((1,), (0,)), ((), ())), precision=HI, preferred_element_type=F32)


def dot_t(left, right):
    return lax.dot_general(left, right, (((0,), (0,)), ((), ())), precision=HI, preferred_element_type=F32)


def dot_b(left, right):
    return lax.dot_general(left, right, (((1,), (0,)), ((), ())), preferred_element_type=F32)


def dot_tb(left, right):
    return lax.dot_general(left, right, (((0,), (0,)), ((), ())), preferred_element_type=F32)


def halves(value):
    high = value.astype(BF16)
    return high, (value - high.astype(F32)).astype(BF16)


def sym(matrix):
    return 0.5 * (matrix + matrix.T)


def sweep_panel(matrix):
    lane8 = lax.broadcasted_iota(jnp.int32, (8, E), 1)
    sub8 = lax.broadcasted_iota(jnp.int32, (8, E), 0)
    lane = lax.broadcasted_iota(jnp.int32, (E - 8, E), 1)
    lane1 = lax.broadcasted_iota(jnp.int32, (1, E), 1)
    top, rest = matrix[:8], matrix[8:]
    for base in (0, 4):
        tops = [jnp.broadcast_to(top[:, base + j : base + j + 1], (8, E)) for j in range(4)]
        rests = [jnp.broadcast_to(rest[:, base + j : base + j + 1], (E - 8, E)) for j in range(4)]
        for j in range(4):
            r = base + j
            inv = 1.0 / tops[j][r : r + 1, :]
            row = jnp.where(lane1 == r, inv, top[r : r + 1, :] * inv)
            rest = jnp.where(lane == r, 0.0, rest) - rests[j] * row
            top = jnp.where(sub8 == r, row, jnp.where(lane8 == r, 0.0, top) - tops[j] * row)
            for m in range(j + 1, 4):
                factor = tops[m][r : r + 1, :] * inv
                rests[m] = rests[m] - rests[j] * factor
                tops[m] = jnp.where(sub8 == r, factor, tops[m] - tops[j] * factor)
    return pltpu.roll(jnp.concatenate([rest, top], axis=0), E - 8, 1)


def sweep_some(count, *matrices):
    return lax.fori_loop(0, count, lambda _, ms: tuple(sweep_panel(m) for m in ms), matrices)


def kernel(
    states_h, pos, gw_h, uw_h, dw_h, cov_h, tgt,
    out,
    states, gw, uw, dw, cbuf, gate, up, ra1, rb1, rc1, ra2,
    chi, clo, piece, bc, wc, bhl, whl, vv, vk, va, wr,
    part, rk, xr, yr, zr, res, tp, m0, n12, n3, mc, nc, mc2, mzr, nzr, n3r, gsum, tmp, send, recv, local,
):
    a = lax.axis_index("row")
    b = lax.axis_index("col")
    x, y = a // 4, a % 4
    z, k = b // 2, b % 2

    def dev_x(d):
        return {"row": ((x + d) % 4) * 4 + y}

    def dev_y(d):
        return {"row": x * 4 + (y + d) % 4}

    def dev_z(d):
        return {"col": ((z + d) % 4) * 2 + k}

    dev_k = {"col": z * 2 + 1 - k}
    sent = []

    def cp(src, dst, dev):
        sem = len(sent)
        copy = pltpu.make_async_remote_copy(
            src_ref=src, dst_ref=dst, send_sem=send.at[sem], recv_sem=recv.at[sem],
            device_id=dev, device_id_type=pl.DeviceIdType.MESH,
        )
        copy.start()
        sent.append(copy)
        return copy

    loads = [
        pltpu.make_async_copy(src, dst, local.at[i])
        for i, (src, dst) in enumerate(((states_h, states), (gw_h, gw), (uw_h, uw), (dw_h, dw)))
    ]
    for load in loads:
        load.start()

    def cov_load(step, slot):
        return pltpu.make_async_copy(
            cov_h.at[pl.ds(pl.multiple_of(step * LINES, 8), LINES)], cbuf.at[slot], local.at[4 + slot]
        )

    cov_load(0, 0).start()

    barrier = pltpu.get_barrier_semaphore()
    peers = [dev(d) for dev in (dev_x, dev_y, dev_z) for d in (1, 2, 3)] + [dev_k]
    for peer in peers:
        pl.semaphore_signal(barrier, inc=1, device_id=peer, device_id_type=pl.DeviceIdType.MESH)

    def ring_far(data, ra, me, dev):
        m2 = (me + 2) % 4
        return [cp(data(0, m2), ra(0), dev(1)), cp(data(1, m2), ra(1), dev(3))]

    def ring_near(data, rb, me, dev):
        return [cp(data(0, (me + 3) % 4), rb(0), dev(3)), cp(data(1, (me + 1) % 4), rb(1), dev(1))]

    def ring_middle(copies, data, ra, rc, me, dev):
        m1, m3 = (me + 1) % 4, (me + 3) % 4
        copies[0].wait_recv()
        data(0, m1)[...] += ra(0)[...]
        c0 = cp(data(0, m1), rc(0), dev(1))
        copies[1].wait_recv()
        data(1, m3)[...] += ra(1)[...]
        c1 = cp(data(1, m3), rc(1), dev(3))
        return [c0, c1]

    def ring_end(copies, data, rb, rc, me):
        for copy in copies:
            copy.wait_recv()
        for h in (0, 1):
            data(h, me)[...] += rb(h)[...] + rc(h)[...]

    def to_three(src, dst, dev):
        return [cp(src(d), dst(d), dev(d)) for d in (1, 2, 3)]

    def wait_all(copies):
        for copy in copies:
            copy.wait_recv()

    loads[0].wait()
    tokens = []
    for p in (0, 1):
        where = pos[p : p + 1, :]
        chosen = jnp.zeros((336, E), F32)
        for s in range(8):
            chosen = jnp.where(where == s, states[p, s].astype(F32), chosen)
        tokens.append(chosen.astype(BF16))
    tokens = jnp.concatenate(tokens, axis=1)

    def project(weight, target, by_y):
        for j in range(7):
            value = dot_tb(weight[:, j * 384 : (j + 1) * 384], tokens)
            row = j * 384
            while row < (j + 1) * 384:
                block, off = row // PIECE, row % PIECE
                size = min(PIECE - off, (j + 1) * 384 - row)
                first, second = (block % 4, block // 4) if by_y else (block // 4, block % 4)
                lines = value[row - j * 384 : row - j * 384 + size]
                target[0, first, second, off : off + size] = lines[:, :E]
                target[1, first, second, off : off + size] = lines[:, E:]
                row += size

    def gate_data(h, t):
        return gate.at[h, t]

    def up_data(h, t):
        return up.at[h, t]

    def buf(ref, which):
        return lambda h: ref.at[which, h]

    def cov_step(step, carry):
        slot = step % 2

        @pl.when(step + 1 < COV_STEPS)
        def _():
            cov_load(step + 1, 1 - slot).start()

        cov_load(step, slot).wait()
        rows = pl.ds(pl.multiple_of(step * COV_ROWS, 16), COV_ROWS)
        for t in range(21):
            high, low = halves(cbuf[slot, pl.ds(t, COV_ROWS, stride=21), :])
            chi[rows, t * E : (t + 1) * E] = high
            clo[rows, t * E : (t + 1) * E] = low
        return carry

    loads[1].wait()
    project(gw, gate, False)
    pl.semaphore_wait(barrier, len(peers))
    g_far = ring_far(gate_data, buf(ra1, 0), x, dev_x)
    loads[2].wait()
    project(uw, up, True)
    u_far = ring_far(up_data, buf(ra1, 1), y, dev_y)
    lax.fori_loop(0, 6, cov_step, 0)
    g_near = ring_near(gate_data, buf(rb1, 0), x, dev_x)
    lax.fori_loop(6, 7, cov_step, 0)
    u_near = ring_near(up_data, buf(rb1, 1), y, dev_y)
    lax.fori_loop(7, 10, cov_step, 0)
    g_near += ring_middle(g_far, gate_data, buf(ra1, 0), buf(rc1, 0), x, dev_x)
    u_near += ring_middle(u_far, up_data, buf(ra1, 1), buf(rc1, 1), y, dev_y)
    lax.fori_loop(10, COV_STEPS, cov_step, 0)
    ring_end(g_near, gate_data, buf(rb1, 0), buf(rc1, 0), x)
    g2 = to_three(lambda d: gate.at[:, x, (y + d) % 4], lambda d: ra2.at[0, d - 1], dev_y)
    ring_end(u_near, up_data, buf(rb1, 1), buf(rc1, 1), y)
    u2 = to_three(lambda d: up.at[:, y, (x + d) % 4], lambda d: ra2.at[1, d - 1], dev_x)
    wait_all(g2)
    wait_all(u2)

    keys = jnp.zeros((PIECE, E), F32)
    for p in (0, 1):
        v = gate[p, x, y] + ((ra2[0, 0, p] + ra2[0, 1, p]) + ra2[0, 2, p])
        u = up[p, y, x] + ((ra2[1, 0, p] + ra2[1, 1, p]) + ra2[1, 2, p])
        keys = keys + v / (1.0 + jnp.exp(-v)) * u
    keys = keys * 0.5
    keys_half = keys.astype(BF16)
    piece[0] = 4.0 / math.sqrt(FF) * keys
    top, low = pl.ds(0, 88), pl.ds(88, 80)

    def gather_start(field, own):
        field[x, y] = piece[own]
        at, ab = field.at[x, y, top], field.at[x, y, low]
        first = [cp(at, at, dev_x(d)) for d in (1, 3, 2)] + [cp(ab, ab, dev_y(d)) for d in (1, 3, 2)]
        return first, [cp(ab, ab, dev_x(d)) for d in (1, 3, 2)] + [cp(at, at, dev_y(d)) for d in (1, 3, 2)]

    def gather_next(copies, field):
        first, rest = copies
        rest = list(rest)
        for i, d in enumerate((3, 1, 2)):
            first[i].wait_recv()
            at = field.at[(x + d) % 4, y, top]
            rest += to_three(lambda e: at, lambda e: at, dev_y)
            first[i + 3].wait_recv()
            ab = field.at[x, (y + d) % 4, low]
            rest += to_three(lambda e: ab, lambda e: ab, dev_x)
        return rest

    def split_field(field, target):
        def body(i, carry):
            rows = pl.ds(pl.multiple_of(i * 336, 16), 336)
            high, rest = halves(field[i // 2, pl.ds((i % 2) * 2, 2)].reshape(336, E))
            target[rows, :E] = high
            target[rows, E:] = rest
            return carry

        lax.fori_loop(0, 8, body, 0)

    def gram(left, right):
        def body(i, total):
            rows = pl.ds(pl.multiple_of(i * 336, 16), 336)
            return total + dot_tb(left[rows, :], right[rows, :])

        total = lax.fori_loop(0, 8, body, jnp.zeros((2 * E, 2 * E), F32))
        return (total[:E, :E] + total[E:, E:]) + (total[:E, E:] + total[E:, :E])

    def cov_times(i, target):
        rows = pl.ds(pl.multiple_of(i * 336, 16), 336)
        both = dot_b(chi[rows, :], target[...])
        return both[:, :E] + (both[:, E:] + dot_b(clo[rows, :], target[:, :E]))

    bg = gather_start(bc, 0)

    loads[3].wait()
    tp[...] = jnp.zeros_like(tp)
    tp[0:42, :] = tgt[...]
    first = (a * 8 + b) * 42
    t_high, t_rest = tp[...].astype(BF16), tp[...] - tp[...].astype(BF16).astype(F32)
    t_mid, t_low = halves(t_rest)
    t_all = jnp.concatenate([t_high, t_mid, t_low], axis=0)
    minus = -keys_half

    def current(j, carry):
        at = pl.multiple_of(j * 384, 128)
        place = lax.broadcasted_iota(jnp.int32, (48, 384), 1) + j * 384 - first
        mark = jnp.where(place == lax.broadcasted_iota(jnp.int32, (48, 384), 0), 1.0, 0.0).astype(BF16)
        value = dot_tb(minus, dw[:, pl.ds(at, 384)]) + dot_tb(t_all, jnp.concatenate([mark, mark, mark], axis=0))
        for i in range(3):
            part[j * 3 + i] = value[:, i * E : (i + 1) * E]
        return carry

    lax.fori_loop(0, 14, current, 0)
    for i in range(42, 48):
        part[i] = jnp.zeros((E, E), F32)
    real = pl.ds(0, 42)

    def half_of(kk):
        return pl.ds(pl.multiple_of(kk * 64, 8), 64)

    def rows_h(h):
        return pl.ds(pl.multiple_of(k * 64 + h * 32, 8), 32)

    def rows_z(h):
        return pl.ds(pl.multiple_of(k * 64 + h * 32 + z * 8, 8), 8)

    def rows_to(h, d):
        return pl.ds(pl.multiple_of(k * 64 + h * 32 + ((z + d) % 4) * 8, 8), 8)

    def twelve(t):
        return pl.ds(t * 12, 12)

    def three(t, u):
        return pl.ds(t * 12 + u * 3, 3)

    ways = ((0, x, dev_x, y, dev_y), (1, y, dev_y, x, dev_x))

    p1 = cp(part.at[real, half_of(1 - k)], rk, dev_k)
    bg = gather_next(bg, bc)
    p1.wait_recv()

    def add_half(i, carry):
        part[i, half_of(k), :] += rk[i]
        return carry

    lax.fori_loop(0, 42, add_half, 0)
    px = []
    for h, u, dev_u, _, _ in ways:
        px += to_three(lambda d: part.at[twelve((u + d) % 4), rows_h(h)], lambda d: xr.at[h, d - 1], dev_u)
    wait_all(bg)
    split_field(bc, bhl)

    def halve(ref, i, value):
        ref[i, 0] = value[:64]
        ref[i, 1] = value[64:]

    def cores_start(ref, n, got):
        return cp(ref.at[pl.ds(0, n), 1 - k], got.at[pl.ds(0, n)], dev_k)

    def cores_end(copy, ref, n, got):
        copy.wait_recv()
        ref[pl.ds(0, n), k] += got[pl.ds(0, n)]

    def axis_start(ref, n, got, dev):
        return to_three(lambda d: ref.at[pl.ds(0, n), k], lambda d: got.at[d - 1, pl.ds(0, n)], dev)

    def axis_end(copies, ref, n, got, target):
        wait_all(copies)
        target[pl.ds(0, n), k] = ref[pl.ds(0, n), k] + ((got[0, pl.ds(0, n)] + got[1, pl.ds(0, n)]) + got[2, pl.ds(0, n)])

    def cores_share(ref):
        return cp(ref.at[:, k], ref.at[:, k], dev_k)

    def first_image(i, carry):
        value = cov_times(i, bhl)
        vv[i, 0] = value[:PIECE]
        vv[i, 1] = value[PIECE:]
        return carry

    lax.fori_loop(0, 4, first_image, 0)
    v1 = cp(vv.at[:, 1 - k], vk, dev_k)
    v1.wait_recv()
    vv[:, k] += vk[...]
    vz = to_three(lambda d: vv.at[(z + d) % 4, k], lambda d: va.at[d - 1], dev_z)
    wait_all(px)
    py = []
    for h, u, _, w, dev_w in ways:
        part[twelve(u), rows_h(h)] += (xr[h, 0] + xr[h, 1]) + xr[h, 2]
        py += to_three(lambda d: part.at[three(u, (w + d) % 4), rows_h(h)], lambda d: yr.at[h, d - 1], dev_w)
    halve(m0, 0, gram(bhl, bhl))
    mk = cores_start(m0, 1, mc)
    wait_all(vz)
    piece[1] = vv[z, k] + ((va[0] + va[1]) + va[2])
    wg = gather_start(wc, 1)
    wr[z, k] = piece[1]
    wz = to_three(lambda d: wr.at[z, k], lambda d: wr.at[z, k], dev_z)
    wait_all(py)
    pz = []
    for h, u, _, w, _ in ways:
        part[three(u, w), rows_h(h)] += (yr[h, 0] + yr[h, 1]) + yr[h, 2]
        pz += to_three(lambda d: part.at[three(u, w), rows_to(h, d)], lambda d: zr.at[h, d - 1], dev_z)
    cores_end(mk, m0, 1, mc)
    mz = axis_start(m0, 1, mzr, dev_z)
    wg = gather_next(wg, wc)
    wait_all(pz)
    rz = []
    for h, u, _, w, _ in ways:
        res[three(u, w), rows_z(h)] = part[three(u, w), rows_z(h)] + ((zr[h, 0] + zr[h, 1]) + zr[h, 2])
        mine = res.at[three(u, w), rows_z(h)]
        rz += to_three(lambda d: mine, lambda d: mine, dev_z)
    wait_all(wz)
    wk = cp(wr.at[:, k], wr.at[:, k], dev_k)
    axis_end(mz, m0, 1, mzr, gsum)
    wait_all(rz)
    ry = []
    for h, u, _, w, dev_w in ways:
        block = res.at[three(u, w), rows_h(h)]
        ry += to_three(lambda d: block, lambda d: block, dev_w)
    wait_all(wg)
    split_field(wc, whl)
    halve(n12, 0, gram(bhl, whl))
    first_n = n12.at[pl.ds(0, 1)]
    nk = cores_start(first_n, 1, nc.at[pl.ds(0, 1)])
    wait_all(ry)
    rx = []
    for h, u, dev_u, _, _ in ways:
        lines = res.at[twelve(u), rows_h(h)]
        rx += to_three(lambda d: lines, lambda d: lines, dev_u)
    wk.wait_recv()

    def second_image(i, total):
        value = cov_times(i, whl)
        return total + dot_t(wr[i].reshape(336, E), value)

    total = lax.fori_loop(0, 2, second_image, jnp.zeros((E, E), F32))
    cores_end(nk, first_n, 1, nc.at[pl.ds(0, 1)])
    nz = axis_start(first_n, 1, nzr.at[0], dev_z)
    total = lax.fori_loop(2, 4, second_image, total)
    halve(n3, 0, total)
    n3k = cores_start(n3, 1, mc2)
    cores_end(n3k, n3, 1, mc2)
    n3z = axis_start(n3, 1, n3r.at[0], dev_z)
    axis_end(nz, first_n, 1, nzr.at[0], gsum.at[pl.ds(1, 1)])
    gs = cores_share(gsum.at[pl.ds(0, 2)])
    halve(n12, 1, gram(whl, whl))
    second_n = n12.at[pl.ds(1, 1)]
    nk = cores_start(second_n, 1, nc.at[pl.ds(1, 1)])
    gs.wait_recv()

    def whole(ref, i):
        return jnp.concatenate([ref[i, 0], ref[i, 1]], axis=0)

    gram0, n1 = sym(whole(gsum, 0)), sym(whole(gsum, 1))
    g11 = sym(n1 + dot(gram0, gram0))
    (inv1,) = sweep_some(2, g11)
    axis_end(n3z, n3, 1, n3r.at[0], n3.at[pl.ds(1, 1)])
    n3y = axis_start(n3.at[pl.ds(1, 1)], 1, n3r.at[1], dev_y)
    cores_end(nk, second_n, 1, nc.at[pl.ds(1, 1)])
    nz = axis_start(second_n, 1, nzr.at[1], dev_z)
    (inv1,) = sweep_some(6, inv1)
    axis_end(n3y, n3.at[pl.ds(1, 1)], 1, n3r.at[1], n3.at[pl.ds(2, 1)])
    n3x = axis_start(n3.at[pl.ds(2, 1)], 1, n3r.at[2], dev_x)
    axis_end(nz, second_n, 1, nzr.at[1], gsum.at[pl.ds(2, 1)])
    gs = cores_share(gsum.at[pl.ds(2, 1)])
    wait_all(rx)
    half = res.at[real, half_of(k)]
    rkk = cp(half, half, dev_k)
    (inv1,) = sweep_some(8, inv1)
    axis_end(n3x, n3.at[pl.ds(2, 1)], 1, n3r.at[2], n3.at[pl.ds(3, 1)])
    n3s = cores_share(n3.at[pl.ds(3, 1)])
    gs.wait_recv()
    g12 = sym(whole(gsum, 2)) + dot(gram0, n1)
    solved = dot(inv1, jnp.concatenate([g12, gram0], axis=1))
    taken = dot_t(g12, solved)
    g22 = dot(n1, n1)
    n3s.wait_recv()
    schur = sym(sym(whole(n3, 3)) + g22 - taken[:, :E])
    right2 = n1 - taken[:, E:]
    (inv2,) = sweep_some(16, schur)
    on_w = dot(inv2, right2)
    tmp[0] = dot(solved[:, :E], on_w)
    on_b = solved[:, E:] - tmp[0]
    fh, fl = halves(jnp.concatenate([piece[0], piece[1]], axis=1))
    ch, cl = halves(jnp.concatenate([on_b, on_w], axis=0))
    found = dot_b(fh, ch) + (dot_b(fh, cl) + dot_b(fl, ch))
    xh, xl = halves(found)
    xhh = jnp.concatenate([xh, xh], axis=1)
    rkk.wait_recv()

    def update(j, carry):
        right = jnp.concatenate([res[j * 2], res[j * 2 + 1]], axis=1)
        rh, rl = halves(right)
        value = dot_b(xhh, jnp.concatenate([rh, rl], axis=0)) + dot_b(xl, rh)
        out[:, pl.ds(pl.multiple_of(j * 256, 128), 256)] = value.astype(BF16)
        return carry

    lax.fori_loop(0, 21, update, 0, unroll=3)
    for copy in sent:
        copy.wait_send()


def body(states, subject_pos, gate_weight, up_weight, down_weight, covariance, targets):
    vmem = pl.BlockSpec(memory_space=pltpu.VMEM)
    anyw = pl.BlockSpec(memory_space=pl.ANY)
    small = lambda *dims: pltpu.VMEM(dims, F32)
    update = pl.pallas_call(
        kernel,
        out_shape=jax.ShapeDtypeStruct((PIECE, D), BF16),
        in_specs=[anyw, vmem, anyw, anyw, anyw, anyw, vmem],
        out_specs=vmem,
        scratch_shapes=[
            pltpu.VMEM((2, 8, 336, E), BF16),
            pltpu.VMEM((336, 2688), BF16),
            pltpu.VMEM((336, 2688), BF16),
            pltpu.VMEM((PIECE, D), BF16),
            small(2, LINES, E),
            small(2, 4, 4, PIECE, E),
            small(2, 4, 4, PIECE, E),
            small(2, 2, 4, PIECE, E),
            small(2, 2, 4, PIECE, E),
            small(2, 2, 4, PIECE, E),
            small(2, 3, 2, PIECE, E),
            pltpu.VMEM((1344, 2688), BF16),
            pltpu.VMEM((1344, 2688), BF16),
            small(2, PIECE, E),
            small(4, 4, PIECE, E),
            small(4, 4, PIECE, E),
            pltpu.VMEM((2688, 2 * E), BF16),
            pltpu.VMEM((2688, 2 * E), BF16),
            small(4, 2, PIECE, E),
            small(4, PIECE, E),
            small(3, PIECE, E),
            small(4, 2, PIECE, E),
            small(48, E, E),
            small(42, 64, E),
            small(2, 3, 12, 32, E),
            small(2, 3, 3, 32, E),
            small(2, 3, 3, 8, E),
            small(48, E, E),
            small(48, E),
            small(1, 2, 64, E),
            small(2, 2, 64, E),
            small(4, 2, 64, E),
            small(1, 64, E),
            small(2, 64, E),
            small(1, 64, E),
            small(3, 1, 64, E),
            small(2, 3, 1, 64, E),
            small(3, 3, 1, 64, E),
            small(3, 2, 64, E),
            small(1, E, E),
            pltpu.SemaphoreType.DMA((N_SEM,)),
            pltpu.SemaphoreType.DMA((N_SEM,)),
            pltpu.SemaphoreType.DMA((6,)),
        ],
        compiler_params=pltpu.CompilerParams(
            collective_id=0, has_side_effects=True, vmem_limit_bytes=60 * 1024 * 1024
        ),
        name="edit",
    )(
        jnp.transpose(states, (1, 2, 3, 0)),
        subject_pos.T,
        gate_weight.reshape(336, 2688),
        up_weight.reshape(336, 2688),
        down_weight.reshape(PIECE, D),
        covariance.reshape(1344 * 21, E),
        targets,
    )
    return update.reshape(1, 1, PIECE, D)


def solution(mesh):
    return jax.shard_map(
        body,
        mesh=mesh,
        in_specs=(
            P(None, None, None, "row"),
            P(),
            P("row", "col", None),
            P("row", "col", None),
            P("row", "col", None, None),
            P("row", "col", None),
            P(("row", "col"), None),
        ),
        out_specs=P("row", "col", None, None),
        check_vma=False,
    )
```

```python
import math

import jax
import jax.numpy as jnp
from jax import lax
from jax.experimental import pallas as pl
from jax.experimental.pallas import tpu as pltpu
from jax.sharding import PartitionSpec as P

FF = 21504
D = 5376
PIECE = 168
E = 128
F32 = jnp.float32
BF16 = jnp.bfloat16
HI = lax.Precision.HIGHEST
N_SEM = 220
COV_ROWS = 112
COV_STEPS = 1344 // COV_ROWS
LINES = COV_ROWS * 21


def dot(left, right):
    return lax.dot_general(left, right, (((1,), (0,)), ((), ())), precision=HI, preferred_element_type=F32)


def dot_t(left, right):
    return lax.dot_general(left, right, (((0,), (0,)), ((), ())), precision=HI, preferred_element_type=F32)


def dot_b(left, right):
    return lax.dot_general(left, right, (((1,), (0,)), ((), ())), preferred_element_type=F32)


def dot_tb(left, right):
    return lax.dot_general(left, right, (((0,), (0,)), ((), ())), preferred_element_type=F32)


def halves(value):
    high = value.astype(BF16)
    return high, (value - high.astype(F32)).astype(BF16)


def sym(matrix):
    return 0.5 * (matrix + matrix.T)


def sweep_panel(matrix):
    lane8 = lax.broadcasted_iota(jnp.int32, (8, E), 1)
    sub8 = lax.broadcasted_iota(jnp.int32, (8, E), 0)
    lane = lax.broadcasted_iota(jnp.int32, (E - 8, E), 1)
    lane1 = lax.broadcasted_iota(jnp.int32, (1, E), 1)
    top, rest = matrix[:8], matrix[8:]
    for base in (0, 4):
        tops = [jnp.broadcast_to(top[:, base + j : base + j + 1], (8, E)) for j in range(4)]
        rests = [jnp.broadcast_to(rest[:, base + j : base + j + 1], (E - 8, E)) for j in range(4)]
        for j in range(4):
            r = base + j
            inv = 1.0 / tops[j][r : r + 1, :]
            row = jnp.where(lane1 == r, inv, top[r : r + 1, :] * inv)
            rest = jnp.where(lane == r, 0.0, rest) - rests[j] * row
            top = jnp.where(sub8 == r, row, jnp.where(lane8 == r, 0.0, top) - tops[j] * row)
            for m in range(j + 1, 4):
                factor = tops[m][r : r + 1, :] * inv
                rests[m] = rests[m] - rests[j] * factor
                tops[m] = jnp.where(sub8 == r, factor, tops[m] - tops[j] * factor)
    return pltpu.roll(jnp.concatenate([rest, top], axis=0), E - 8, 1)


def sweep_some(count, *matrices):
    return lax.fori_loop(0, count, lambda _, ms: tuple(sweep_panel(m) for m in ms), matrices)


def kernel(
    states_h, pos, gw_h, uw_h, dw_h, cov_h, tgt,
    out,
    states, gw, uw, dw, cbuf, gate, up, ra1, rb1, rc1, ra2,
    chi, clo, piece, bc, wc, bhl, whl, vv, vk, va, wr,
    part, rk, xr, yr, zr, res, tp, m0, n12, n3, mc, nc, mc2, mzr, nzr, n3r, gsum, tmp, send, recv, local,
):
    a = lax.axis_index("row")
    b = lax.axis_index("col")
    x, y = a // 4, a % 4
    z, k = b // 2, b % 2

    def dev_x(d):
        return {"row": ((x + d) % 4) * 4 + y}

    def dev_y(d):
        return {"row": x * 4 + (y + d) % 4}

    def dev_z(d):
        return {"col": ((z + d) % 4) * 2 + k}

    dev_k = {"col": z * 2 + 1 - k}
    sent = []

    def cp(src, dst, dev):
        sem = len(sent)
        copy = pltpu.make_async_remote_copy(
            src_ref=src, dst_ref=dst, send_sem=send.at[sem], recv_sem=recv.at[sem],
            device_id=dev, device_id_type=pl.DeviceIdType.MESH,
        )
        copy.start()
        sent.append(copy)
        return copy

    loads = [
        pltpu.make_async_copy(src, dst, local.at[i])
        for i, (src, dst) in enumerate(((states_h, states), (gw_h, gw), (uw_h, uw), (dw_h, dw)))
    ]
    for load in loads:
        load.start()

    def cov_load(step, slot):
        return pltpu.make_async_copy(
            cov_h.at[pl.ds(pl.multiple_of(step * LINES, 8), LINES)], cbuf.at[slot], local.at[4 + slot]
        )

    cov_load(0, 0).start()

    barrier = pltpu.get_barrier_semaphore()
    peers = [dev(d) for dev in (dev_x, dev_y, dev_z) for d in (1, 2, 3)] + [dev_k]
    for peer in peers:
        pl.semaphore_signal(barrier, inc=1, device_id=peer, device_id_type=pl.DeviceIdType.MESH)

    def ring_far(data, ra, me, dev):
        m2 = (me + 2) % 4
        return [cp(data(0, m2), ra(0), dev(1)), cp(data(1, m2), ra(1), dev(3))]

    def ring_near(data, rb, me, dev):
        return [cp(data(0, (me + 3) % 4), rb(0), dev(3)), cp(data(1, (me + 1) % 4), rb(1), dev(1))]

    def ring_middle(copies, data, ra, rc, me, dev):
        m1, m3 = (me + 1) % 4, (me + 3) % 4
        copies[0].wait_recv()
        data(0, m1)[...] += ra(0)[...]
        c0 = cp(data(0, m1), rc(0), dev(1))
        copies[1].wait_recv()
        data(1, m3)[...] += ra(1)[...]
        c1 = cp(data(1, m3), rc(1), dev(3))
        return [c0, c1]

    def ring_end(copies, data, rb, rc, me):
        for copy in copies:
            copy.wait_recv()
        for h in (0, 1):
            data(h, me)[...] += rb(h)[...] + rc(h)[...]

    def to_three(src, dst, dev):
        return [cp(src(d), dst(d), dev(d)) for d in (1, 2, 3)]

    def wait_all(copies):
        for copy in copies:
            copy.wait_recv()

    loads[0].wait()
    tokens = []
    for p in (0, 1):
        where = pos[p : p + 1, :]
        chosen = jnp.zeros((336, E), F32)
        for s in range(8):
            chosen = jnp.where(where == s, states[p, s].astype(F32), chosen)
        tokens.append(chosen.astype(BF16))
    tokens = jnp.concatenate(tokens, axis=1)

    def project(weight, target, by_y):
        for j in range(7):
            value = dot_tb(weight[:, j * 384 : (j + 1) * 384], tokens)
            row = j * 384
            while row < (j + 1) * 384:
                block, off = row // PIECE, row % PIECE
                size = min(PIECE - off, (j + 1) * 384 - row)
                first, second = (block % 4, block // 4) if by_y else (block // 4, block % 4)
                lines = value[row - j * 384 : row - j * 384 + size]
                target[0, first, second, off : off + size] = lines[:, :E]
                target[1, first, second, off : off + size] = lines[:, E:]
                row += size

    cuts = (pl.ds(0, 88), pl.ds(88, 80))

    def gate_data(q):
        return lambda h, t: gate.at[h, t, :, cuts[q]]

    def up_data(q):
        return lambda h, t: up.at[h, t, :, cuts[q]]

    def buf(ref, which, q):
        return lambda h: ref.at[which, h, :, cuts[q]]

    def cov_step(step, carry):
        slot = step % 2

        @pl.when(step + 1 < COV_STEPS)
        def _():
            cov_load(step + 1, 1 - slot).start()

        cov_load(step, slot).wait()
        rows = pl.ds(pl.multiple_of(step * COV_ROWS, 16), COV_ROWS)
        for t in range(21):
            high, low = halves(cbuf[slot, pl.ds(t, COV_ROWS, stride=21), :])
            chi[rows, t * E : (t + 1) * E] = high
            clo[rows, t * E : (t + 1) * E] = low
        return carry

    loads[1].wait()
    project(gw, gate, False)
    pl.semaphore_wait(barrier, len(peers))
    g_far = [ring_far(gate_data(q), buf(ra1, 0, q), x, dev_x) for q in (0, 1)]
    loads[2].wait()
    project(uw, up, True)
    u_far = [ring_far(up_data(q), buf(ra1, 1, q), y, dev_y) for q in (0, 1)]

    def near(q):
        g = ring_near(gate_data(q), buf(rb1, 0, q), x, dev_x)
        return g, ring_near(up_data(q), buf(rb1, 1, q), y, dev_y)

    def middle(q):
        g = ring_middle(g_far[q], gate_data(q), buf(ra1, 0, q), buf(rc1, 0, q), x, dev_x)
        return g, ring_middle(u_far[q], up_data(q), buf(ra1, 1, q), buf(rc1, 1, q), y, dev_y)

    def second(q, g, u):
        ring_end(g, gate_data(q), buf(rb1, 0, q), buf(rc1, 0, q), x)
        g2 = to_three(
            lambda d: gate.at[:, x, (y + d) % 4, cuts[q]], lambda d: ra2.at[0, d - 1, :, cuts[q]], dev_y
        )
        ring_end(u, up_data(q), buf(rb1, 1, q), buf(rc1, 1, q), y)
        return g2 + to_three(
            lambda d: up.at[:, y, (x + d) % 4, cuts[q]], lambda d: ra2.at[1, d - 1, :, cuts[q]], dev_x
        )

    lax.fori_loop(0, 5, cov_step, 0)
    gn0, un0 = near(0)
    lax.fori_loop(5, 8, cov_step, 0)
    gc0, uc0 = middle(0)
    gn1, un1 = near(1)
    gc1, uc1 = middle(1)
    lax.fori_loop(8, COV_STEPS, cov_step, 0)
    parts = second(0, gn0 + gc0, un0 + uc0)
    parts += second(1, gn1 + gc1, un1 + uc1)
    wait_all(parts)

    keys = jnp.zeros((PIECE, E), F32)
    for p in (0, 1):
        v = gate[p, x, y] + ((ra2[0, 0, p] + ra2[0, 1, p]) + ra2[0, 2, p])
        u = up[p, y, x] + ((ra2[1, 0, p] + ra2[1, 1, p]) + ra2[1, 2, p])
        keys = keys + v / (1.0 + jnp.exp(-v)) * u
    keys = keys * 0.5
    keys_half = keys.astype(BF16)
    piece[0] = 4.0 / math.sqrt(FF) * keys
    top, low = pl.ds(0, 88), pl.ds(88, 80)

    def gather_start(field, own):
        field[x, y] = piece[own]
        at, ab = field.at[x, y, top], field.at[x, y, low]
        first = [cp(at, at, dev_x(d)) for d in (1, 3, 2)] + [cp(ab, ab, dev_y(d)) for d in (1, 3, 2)]
        return first, [cp(ab, ab, dev_x(d)) for d in (1, 3, 2)] + [cp(at, at, dev_y(d)) for d in (1, 3, 2)]

    def gather_next(copies, field):
        first, rest = copies
        rest = list(rest)
        for i, d in enumerate((3, 1, 2)):
            first[i].wait_recv()
            at = field.at[(x + d) % 4, y, top]
            rest += to_three(lambda e: at, lambda e: at, dev_y)
            first[i + 3].wait_recv()
            ab = field.at[x, (y + d) % 4, low]
            rest += to_three(lambda e: ab, lambda e: ab, dev_x)
        return rest

    def split_field(field, target):
        def body(i, carry):
            rows = pl.ds(pl.multiple_of(i * 336, 16), 336)
            high, rest = halves(field[i // 2, pl.ds((i % 2) * 2, 2)].reshape(336, E))
            target[rows, :E] = high
            target[rows, E:] = rest
            return carry

        lax.fori_loop(0, 8, body, 0)

    def gram(left, right):
        def body(i, total):
            rows = pl.ds(pl.multiple_of(i * 336, 16), 336)
            return total + dot_tb(left[rows, :], right[rows, :])

        total = lax.fori_loop(0, 8, body, jnp.zeros((2 * E, 2 * E), F32))
        return (total[:E, :E] + total[E:, E:]) + (total[:E, E:] + total[E:, :E])

    def cov_times(i, target):
        rows = pl.ds(pl.multiple_of(i * 336, 16), 336)
        both = dot_b(chi[rows, :], target[...])
        return both[:, :E] + (both[:, E:] + dot_b(clo[rows, :], target[:, :E]))

    bg = gather_start(bc, 0)

    loads[3].wait()
    tp[...] = jnp.zeros_like(tp)
    tp[0:42, :] = tgt[...]
    first = (a * 8 + b) * 42
    t_high, t_rest = tp[...].astype(BF16), tp[...] - tp[...].astype(BF16).astype(F32)
    t_mid, t_low = halves(t_rest)
    t_all = jnp.concatenate([t_high, t_mid, t_low], axis=0)
    minus = -keys_half

    def current(j, carry):
        at = pl.multiple_of(j * 384, 128)
        place = lax.broadcasted_iota(jnp.int32, (48, 384), 1) + j * 384 - first
        mark = jnp.where(place == lax.broadcasted_iota(jnp.int32, (48, 384), 0), 1.0, 0.0).astype(BF16)
        value = dot_tb(minus, dw[:, pl.ds(at, 384)]) + dot_tb(t_all, jnp.concatenate([mark, mark, mark], axis=0))
        for i in range(3):
            part[j * 3 + i] = value[:, i * E : (i + 1) * E]
        return carry

    lax.fori_loop(0, 14, current, 0)
    for i in range(42, 48):
        part[i] = jnp.zeros((E, E), F32)
    real = pl.ds(0, 42)

    def half_of(kk):
        return pl.ds(pl.multiple_of(kk * 64, 8), 64)

    def rows_h(h):
        return pl.ds(pl.multiple_of(k * 64 + h * 32, 8), 32)

    def rows_z(h):
        return pl.ds(pl.multiple_of(k * 64 + h * 32 + z * 8, 8), 8)

    def rows_to(h, d):
        return pl.ds(pl.multiple_of(k * 64 + h * 32 + ((z + d) % 4) * 8, 8), 8)

    def twelve(t):
        return pl.ds(t * 12, 12)

    def three(t, u):
        return pl.ds(t * 12 + u * 3, 3)

    ways = ((0, x, dev_x, y, dev_y), (1, y, dev_y, x, dev_x))

    p1 = cp(part.at[real, half_of(1 - k)], rk, dev_k)
    bg = gather_next(bg, bc)
    p1.wait_recv()

    def add_half(i, carry):
        part[i, half_of(k), :] += rk[i]
        return carry

    lax.fori_loop(0, 42, add_half, 0)
    px = []
    for h, u, dev_u, _, _ in ways:
        px += to_three(lambda d: part.at[twelve((u + d) % 4), rows_h(h)], lambda d: xr.at[h, d - 1], dev_u)
    wait_all(bg)
    split_field(bc, bhl)

    def halve(ref, i, value):
        ref[i, 0] = value[:64]
        ref[i, 1] = value[64:]

    def cores_start(ref, n, got):
        return cp(ref.at[pl.ds(0, n), 1 - k], got.at[pl.ds(0, n)], dev_k)

    def cores_end(copy, ref, n, got):
        copy.wait_recv()
        ref[pl.ds(0, n), k] += got[pl.ds(0, n)]

    def axis_start(ref, n, got, dev):
        return to_three(lambda d: ref.at[pl.ds(0, n), k], lambda d: got.at[d - 1, pl.ds(0, n)], dev)

    def axis_end(copies, ref, n, got, target):
        wait_all(copies)
        target[pl.ds(0, n), k] = ref[pl.ds(0, n), k] + ((got[0, pl.ds(0, n)] + got[1, pl.ds(0, n)]) + got[2, pl.ds(0, n)])

    def cores_share(ref):
        return cp(ref.at[:, k], ref.at[:, k], dev_k)

    def first_image(i, carry):
        value = cov_times(i, bhl)
        vv[i, 0] = value[:PIECE]
        vv[i, 1] = value[PIECE:]
        return carry

    lax.fori_loop(0, 4, first_image, 0)
    v1 = cp(vv.at[:, 1 - k], vk, dev_k)
    v1.wait_recv()
    vv[:, k] += vk[...]
    vz = to_three(lambda d: vv.at[(z + d) % 4, k], lambda d: va.at[d - 1], dev_z)
    wait_all(px)
    py = []
    for h, u, _, w, dev_w in ways:
        part[twelve(u), rows_h(h)] += (xr[h, 0] + xr[h, 1]) + xr[h, 2]
        py += to_three(lambda d: part.at[three(u, (w + d) % 4), rows_h(h)], lambda d: yr.at[h, d - 1], dev_w)
    halve(m0, 0, gram(bhl, bhl))
    mk = cores_start(m0, 1, mc)
    wait_all(vz)
    piece[1] = vv[z, k] + ((va[0] + va[1]) + va[2])
    wg = gather_start(wc, 1)
    wr[z, k] = piece[1]
    wz = to_three(lambda d: wr.at[z, k], lambda d: wr.at[z, k], dev_z)
    wait_all(py)
    pz = []
    for h, u, _, w, _ in ways:
        part[three(u, w), rows_h(h)] += (yr[h, 0] + yr[h, 1]) + yr[h, 2]
        pz += to_three(lambda d: part.at[three(u, w), rows_to(h, d)], lambda d: zr.at[h, d - 1], dev_z)
    cores_end(mk, m0, 1, mc)
    mz = axis_start(m0, 1, mzr, dev_z)
    wg = gather_next(wg, wc)
    wait_all(pz)
    rz = []
    for h, u, _, w, _ in ways:
        res[three(u, w), rows_z(h)] = part[three(u, w), rows_z(h)] + ((zr[h, 0] + zr[h, 1]) + zr[h, 2])
        mine = res.at[three(u, w), rows_z(h)]
        rz += to_three(lambda d: mine, lambda d: mine, dev_z)
    wait_all(wz)
    wk = cp(wr.at[:, k], wr.at[:, k], dev_k)
    axis_end(mz, m0, 1, mzr, gsum)
    wait_all(rz)
    ry = []
    for h, u, _, w, dev_w in ways:
        block = res.at[three(u, w), rows_h(h)]
        ry += to_three(lambda d: block, lambda d: block, dev_w)
    wait_all(wg)
    split_field(wc, whl)
    halve(n12, 0, gram(bhl, whl))
    first_n = n12.at[pl.ds(0, 1)]
    nk = cores_start(first_n, 1, nc.at[pl.ds(0, 1)])
    wait_all(ry)
    rx = []
    for h, u, dev_u, _, _ in ways:
        lines = res.at[twelve(u), rows_h(h)]
        rx += to_three(lambda d: lines, lambda d: lines, dev_u)
    wk.wait_recv()

    def second_image(i, total):
        value = cov_times(i, whl)
        return total + dot_t(wr[i].reshape(336, E), value)

    total = lax.fori_loop(0, 2, second_image, jnp.zeros((E, E), F32))
    cores_end(nk, first_n, 1, nc.at[pl.ds(0, 1)])
    nz = axis_start(first_n, 1, nzr.at[0], dev_z)
    total = lax.fori_loop(2, 4, second_image, total)
    halve(n3, 0, total)
    n3k = cores_start(n3, 1, mc2)
    cores_end(n3k, n3, 1, mc2)
    n3z = axis_start(n3, 1, n3r.at[0], dev_z)
    axis_end(nz, first_n, 1, nzr.at[0], gsum.at[pl.ds(1, 1)])
    gs = cores_share(gsum.at[pl.ds(0, 2)])
    halve(n12, 1, gram(whl, whl))
    second_n = n12.at[pl.ds(1, 1)]
    nk = cores_start(second_n, 1, nc.at[pl.ds(1, 1)])
    gs.wait_recv()

    def whole(ref, i):
        return jnp.concatenate([ref[i, 0], ref[i, 1]], axis=0)

    gram0, n1 = sym(whole(gsum, 0)), sym(whole(gsum, 1))
    g11 = sym(n1 + dot(gram0, gram0))
    (inv1,) = sweep_some(2, g11)
    axis_end(n3z, n3, 1, n3r.at[0], n3.at[pl.ds(1, 1)])
    n3y = axis_start(n3.at[pl.ds(1, 1)], 1, n3r.at[1], dev_y)
    cores_end(nk, second_n, 1, nc.at[pl.ds(1, 1)])
    nz = axis_start(second_n, 1, nzr.at[1], dev_z)
    (inv1,) = sweep_some(6, inv1)
    axis_end(n3y, n3.at[pl.ds(1, 1)], 1, n3r.at[1], n3.at[pl.ds(2, 1)])
    n3x = axis_start(n3.at[pl.ds(2, 1)], 1, n3r.at[2], dev_x)
    axis_end(nz, second_n, 1, nzr.at[1], gsum.at[pl.ds(2, 1)])
    gs = cores_share(gsum.at[pl.ds(2, 1)])
    wait_all(rx)
    half = res.at[real, half_of(k)]
    rkk = cp(half, half, dev_k)
    (inv1,) = sweep_some(8, inv1)
    axis_end(n3x, n3.at[pl.ds(2, 1)], 1, n3r.at[2], n3.at[pl.ds(3, 1)])
    n3s = cores_share(n3.at[pl.ds(3, 1)])
    gs.wait_recv()
    g12 = sym(whole(gsum, 2)) + dot(gram0, n1)
    solved = dot(inv1, jnp.concatenate([g12, gram0], axis=1))
    taken = dot_t(g12, solved)
    g22 = dot(n1, n1)
    n3s.wait_recv()
    schur = sym(sym(whole(n3, 3)) + g22 - taken[:, :E])
    right2 = n1 - taken[:, E:]
    (inv2,) = sweep_some(16, schur)
    on_w = dot(inv2, right2)
    tmp[0] = dot(solved[:, :E], on_w)
    on_b = solved[:, E:] - tmp[0]
    fh, fl = halves(jnp.concatenate([piece[0], piece[1]], axis=1))
    ch, cl = halves(jnp.concatenate([on_b, on_w], axis=0))
    found = dot_b(fh, ch) + (dot_b(fh, cl) + dot_b(fl, ch))
    xh, xl = halves(found)
    xhh = jnp.concatenate([xh, xh], axis=1)
    rkk.wait_recv()

    def update(j, carry):
        right = jnp.concatenate([res[j * 2], res[j * 2 + 1]], axis=1)
        rh, rl = halves(right)
        value = dot_b(xhh, jnp.concatenate([rh, rl], axis=0)) + dot_b(xl, rh)
        out[:, pl.ds(pl.multiple_of(j * 256, 128), 256)] = value.astype(BF16)
        return carry

    lax.fori_loop(0, 21, update, 0, unroll=3)
    for copy in sent:
        copy.wait_send()


def body(states, subject_pos, gate_weight, up_weight, down_weight, covariance, targets):
    vmem = pl.BlockSpec(memory_space=pltpu.VMEM)
    anyw = pl.BlockSpec(memory_space=pl.ANY)
    small = lambda *dims: pltpu.VMEM(dims, F32)
    update = pl.pallas_call(
        kernel,
        out_shape=jax.ShapeDtypeStruct((PIECE, D), BF16),
        in_specs=[anyw, vmem, anyw, anyw, anyw, anyw, vmem],
        out_specs=vmem,
        scratch_shapes=[
            pltpu.VMEM((2, 8, 336, E), BF16),
            pltpu.VMEM((336, 2688), BF16),
            pltpu.VMEM((336, 2688), BF16),
            pltpu.VMEM((PIECE, D), BF16),
            small(2, LINES, E),
            small(2, 4, 4, PIECE, E),
            small(2, 4, 4, PIECE, E),
            small(2, 2, 4, PIECE, E),
            small(2, 2, 4, PIECE, E),
            small(2, 2, 4, PIECE, E),
            small(2, 3, 2, PIECE, E),
            pltpu.VMEM((1344, 2688), BF16),
            pltpu.VMEM((1344, 2688), BF16),
            small(2, PIECE, E),
            small(4, 4, PIECE, E),
            small(4, 4, PIECE, E),
            pltpu.VMEM((2688, 2 * E), BF16),
            pltpu.VMEM((2688, 2 * E), BF16),
            small(4, 2, PIECE, E),
            small(4, PIECE, E),
            small(3, PIECE, E),
            small(4, 2, PIECE, E),
            small(48, E, E),
            small(42, 64, E),
            small(2, 3, 12, 32, E),
            small(2, 3, 3, 32, E),
            small(2, 3, 3, 8, E),
            small(48, E, E),
            small(48, E),
            small(1, 2, 64, E),
            small(2, 2, 64, E),
            small(4, 2, 64, E),
            small(1, 64, E),
            small(2, 64, E),
            small(1, 64, E),
            small(3, 1, 64, E),
            small(2, 3, 1, 64, E),
            small(3, 3, 1, 64, E),
            small(3, 2, 64, E),
            small(1, E, E),
            pltpu.SemaphoreType.DMA((N_SEM,)),
            pltpu.SemaphoreType.DMA((N_SEM,)),
            pltpu.SemaphoreType.DMA((6,)),
        ],
        compiler_params=pltpu.CompilerParams(
            collective_id=0, has_side_effects=True, vmem_limit_bytes=60 * 1024 * 1024
        ),
        name="edit",
    )(
        jnp.transpose(states, (1, 2, 3, 0)),
        subject_pos.T,
        gate_weight.reshape(336, 2688),
        up_weight.reshape(336, 2688),
        down_weight.reshape(PIECE, D),
        covariance.reshape(1344 * 21, E),
        targets,
    )
    return update.reshape(1, 1, PIECE, D)


def solution(mesh):
    return jax.shard_map(
        body,
        mesh=mesh,
        in_specs=(
            P(None, None, None, "row"),
            P(),
            P("row", "col", None),
            P("row", "col", None),
            P("row", "col", None, None),
            P("row", "col", None),
            P(("row", "col"), None),
        ),
        out_specs=P("row", "col", None, None),
        check_vma=False,
    )
```

```python
import math

import jax
import jax.numpy as jnp
from jax import lax
from jax.experimental import pallas as pl
from jax.experimental.pallas import tpu as pltpu
from jax.sharding import PartitionSpec as P

FF = 21504
D = 5376
PIECE = 168
E = 128
F32 = jnp.float32
BF16 = jnp.bfloat16
HI = lax.Precision.HIGHEST
N_SEM = 220
COV_ROWS = 112
COV_STEPS = 1344 // COV_ROWS
LINES = COV_ROWS * 21


def dot(left, right):
    return lax.dot_general(left, right, (((1,), (0,)), ((), ())), precision=HI, preferred_element_type=F32)


def dot_t(left, right):
    return lax.dot_general(left, right, (((0,), (0,)), ((), ())), precision=HI, preferred_element_type=F32)


def dot_b(left, right):
    return lax.dot_general(left, right, (((1,), (0,)), ((), ())), preferred_element_type=F32)


def dot_tb(left, right):
    return lax.dot_general(left, right, (((0,), (0,)), ((), ())), preferred_element_type=F32)


def halves(value):
    high = value.astype(BF16)
    return high, (value - high.astype(F32)).astype(BF16)


def sym(matrix):
    return 0.5 * (matrix + matrix.T)


def sweep_panel(matrix):
    lane8 = lax.broadcasted_iota(jnp.int32, (8, E), 1)
    sub8 = lax.broadcasted_iota(jnp.int32, (8, E), 0)
    lane = lax.broadcasted_iota(jnp.int32, (E - 8, E), 1)
    lane1 = lax.broadcasted_iota(jnp.int32, (1, E), 1)
    top, rest = matrix[:8], matrix[8:]
    for base in (0, 4):
        tops = [jnp.broadcast_to(top[:, base + j : base + j + 1], (8, E)) for j in range(4)]
        rests = [jnp.broadcast_to(rest[:, base + j : base + j + 1], (E - 8, E)) for j in range(4)]
        for j in range(4):
            r = base + j
            inv = 1.0 / tops[j][r : r + 1, :]
            row = jnp.where(lane1 == r, inv, top[r : r + 1, :] * inv)
            rest = jnp.where(lane == r, 0.0, rest) - rests[j] * row
            top = jnp.where(sub8 == r, row, jnp.where(lane8 == r, 0.0, top) - tops[j] * row)
            for m in range(j + 1, 4):
                factor = tops[m][r : r + 1, :] * inv
                rests[m] = rests[m] - rests[j] * factor
                tops[m] = jnp.where(sub8 == r, factor, tops[m] - tops[j] * factor)
    return pltpu.roll(jnp.concatenate([rest, top], axis=0), E - 8, 1)


def sweep_some(count, *matrices):
    return lax.fori_loop(0, count, lambda _, ms: tuple(sweep_panel(m) for m in ms), matrices)


def kernel(
    states_h, pos, gw_h, uw_h, dw_h, cov_h, tgt,
    out,
    states, gw, uw, dw, cbuf, gate, up, ra1, rb1, rc1, ra2,
    chi, clo, piece, bc, wc, bhl, whl, vv, vk, va, wr,
    part, rk, xr, yr, zr, res, tp, m0, n12, n3, mc, nc, mc2, mzr, nzr, n3r, gsum, tmp, send, recv, local,
):
    a = lax.axis_index("row")
    b = lax.axis_index("col")
    x, y = a // 4, a % 4
    z, k = b // 2, b % 2

    def dev_x(d):
        return {"row": ((x + d) % 4) * 4 + y}

    def dev_y(d):
        return {"row": x * 4 + (y + d) % 4}

    def dev_z(d):
        return {"col": ((z + d) % 4) * 2 + k}

    dev_k = {"col": z * 2 + 1 - k}
    sent = []

    def cp(src, dst, dev):
        sem = len(sent)
        copy = pltpu.make_async_remote_copy(
            src_ref=src, dst_ref=dst, send_sem=send.at[sem], recv_sem=recv.at[sem],
            device_id=dev, device_id_type=pl.DeviceIdType.MESH,
        )
        copy.start()
        sent.append(copy)
        return copy

    loads = [
        pltpu.make_async_copy(src, dst, local.at[i])
        for i, (src, dst) in enumerate(((states_h, states), (gw_h, gw), (uw_h, uw), (dw_h, dw)))
    ]
    for load in loads:
        load.start()

    def cov_load(step, slot):
        return pltpu.make_async_copy(
            cov_h.at[pl.ds(pl.multiple_of(step * LINES, 8), LINES)], cbuf.at[slot], local.at[4 + slot]
        )

    cov_load(0, 0).start()

    barrier = pltpu.get_barrier_semaphore()
    peers = [dev(d) for dev in (dev_x, dev_y, dev_z) for d in (1, 2, 3)] + [dev_k]
    for peer in peers:
        pl.semaphore_signal(barrier, inc=1, device_id=peer, device_id_type=pl.DeviceIdType.MESH)

    def ring_far(data, ra, me, dev):
        m2 = (me + 2) % 4
        return [cp(data(0, m2), ra(0), dev(1)), cp(data(1, m2), ra(1), dev(3))]

    def ring_near(data, rb, me, dev):
        return [cp(data(0, (me + 3) % 4), rb(0), dev(3)), cp(data(1, (me + 1) % 4), rb(1), dev(1))]

    def ring_middle(copies, data, ra, rc, me, dev):
        m1, m3 = (me + 1) % 4, (me + 3) % 4
        copies[0].wait_recv()
        data(0, m1)[...] += ra(0)[...]
        c0 = cp(data(0, m1), rc(0), dev(1))
        copies[1].wait_recv()
        data(1, m3)[...] += ra(1)[...]
        c1 = cp(data(1, m3), rc(1), dev(3))
        return [c0, c1]

    def ring_end(copies, data, rb, rc, me):
        for copy in copies:
            copy.wait_recv()
        for h in (0, 1):
            data(h, me)[...] += rb(h)[...] + rc(h)[...]

    def to_three(src, dst, dev):
        return [cp(src(d), dst(d), dev(d)) for d in (1, 2, 3)]

    def wait_all(copies):
        for copy in copies:
            copy.wait_recv()

    loads[0].wait()
    tokens = []
    for p in (0, 1):
        where = pos[p : p + 1, :]
        chosen = jnp.zeros((336, E), F32)
        for s in range(8):
            chosen = jnp.where(where == s, states[p, s].astype(F32), chosen)
        tokens.append(chosen.astype(BF16))
    tokens = jnp.concatenate(tokens, axis=1)

    def project(weight, target, by_y):
        for j in range(7):
            value = dot_tb(weight[:, j * 384 : (j + 1) * 384], tokens)
            row = j * 384
            while row < (j + 1) * 384:
                block, off = row // PIECE, row % PIECE
                size = min(PIECE - off, (j + 1) * 384 - row)
                first, second = (block % 4, block // 4) if by_y else (block // 4, block % 4)
                lines = value[row - j * 384 : row - j * 384 + size]
                target[0, first, second, off : off + size] = lines[:, :E]
                target[1, first, second, off : off + size] = lines[:, E:]
                row += size

    cuts = (pl.ds(0, 88), pl.ds(88, 80))

    def gate_data(q):
        return lambda h, t: gate.at[h, t, :, cuts[q]]

    def up_data(q):
        return lambda h, t: up.at[h, t, :, cuts[q]]

    def buf(ref, which, q):
        return lambda h: ref.at[which, h, :, cuts[q]]

    def cov_step(step, carry):
        slot = step % 2

        @pl.when(step + 1 < COV_STEPS)
        def _():
            cov_load(step + 1, 1 - slot).start()

        cov_load(step, slot).wait()
        rows = pl.ds(pl.multiple_of(step * COV_ROWS, 16), COV_ROWS)
        for t in range(21):
            high, low = halves(cbuf[slot, pl.ds(t, COV_ROWS, stride=21), :])
            chi[rows, t * E : (t + 1) * E] = high
            clo[rows, t * E : (t + 1) * E] = low
        return carry

    loads[1].wait()
    project(gw, gate, False)
    pl.semaphore_wait(barrier, len(peers))
    g_far = [ring_far(gate_data(q), buf(ra1, 0, q), x, dev_x) for q in (0, 1)]
    loads[2].wait()
    project(uw, up, True)
    u_far = [ring_far(up_data(q), buf(ra1, 1, q), y, dev_y) for q in (0, 1)]

    def near(q):
        g = ring_near(gate_data(q), buf(rb1, 0, q), x, dev_x)
        return g, ring_near(up_data(q), buf(rb1, 1, q), y, dev_y)

    def middle(q):
        g = ring_middle(g_far[q], gate_data(q), buf(ra1, 0, q), buf(rc1, 0, q), x, dev_x)
        return g, ring_middle(u_far[q], up_data(q), buf(ra1, 1, q), buf(rc1, 1, q), y, dev_y)

    def second(q, g, u):
        ring_end(g, gate_data(q), buf(rb1, 0, q), buf(rc1, 0, q), x)
        g2 = to_three(
            lambda d: gate.at[:, x, (y + d) % 4, cuts[q]], lambda d: ra2.at[0, d - 1, :, cuts[q]], dev_y
        )
        ring_end(u, up_data(q), buf(rb1, 1, q), buf(rc1, 1, q), y)
        return g2 + to_three(
            lambda d: up.at[:, y, (x + d) % 4, cuts[q]], lambda d: ra2.at[1, d - 1, :, cuts[q]], dev_x
        )

    lax.fori_loop(0, 5, cov_step, 0)
    gn0, un0 = near(0)
    lax.fori_loop(5, 8, cov_step, 0)
    gc0, uc0 = middle(0)
    gn1, un1 = near(1)
    gc1, uc1 = middle(1)
    lax.fori_loop(8, COV_STEPS, cov_step, 0)
    parts = second(0, gn0 + gc0, un0 + uc0)
    parts += second(1, gn1 + gc1, un1 + uc1)
    wait_all(parts)

    keys = jnp.zeros((PIECE, E), F32)
    for p in (0, 1):
        v = gate[p, x, y] + ((ra2[0, 0, p] + ra2[0, 1, p]) + ra2[0, 2, p])
        u = up[p, y, x] + ((ra2[1, 0, p] + ra2[1, 1, p]) + ra2[1, 2, p])
        keys = keys + v / (1.0 + jnp.exp(-v)) * u
    keys = keys * 0.5
    keys_half = keys.astype(BF16)
    piece[0] = 4.0 / math.sqrt(FF) * keys
    top, low = pl.ds(0, 88), pl.ds(88, 80)

    def gather_start(field, own):
        field[x, y] = piece[own]
        at, ab = field.at[x, y, top], field.at[x, y, low]
        first = [cp(at, at, dev_x(d)) for d in (1, 3, 2)] + [cp(ab, ab, dev_y(d)) for d in (1, 3, 2)]
        return first, [cp(ab, ab, dev_x(d)) for d in (1, 3, 2)] + [cp(at, at, dev_y(d)) for d in (1, 3, 2)]

    def gather_next(copies, field):
        first, rest = copies
        rest = list(rest)
        for i, d in enumerate((3, 1, 2)):
            first[i].wait_recv()
            at = field.at[(x + d) % 4, y, top]
            rest += to_three(lambda e: at, lambda e: at, dev_y)
            first[i + 3].wait_recv()
            ab = field.at[x, (y + d) % 4, low]
            rest += to_three(lambda e: ab, lambda e: ab, dev_x)
        return rest

    def split_field(field, target):
        def body(i, carry):
            rows = pl.ds(pl.multiple_of(i * 336, 16), 336)
            high, rest = halves(field[i // 2, pl.ds((i % 2) * 2, 2)].reshape(336, E))
            target[rows, :E] = high
            target[rows, E:] = rest
            return carry

        lax.fori_loop(0, 8, body, 0)

    def gram(left, right):
        def body(i, total):
            rows = pl.ds(pl.multiple_of(i * 336, 16), 336)
            return total + dot_tb(left[rows, :], right[rows, :])

        total = lax.fori_loop(0, 8, body, jnp.zeros((2 * E, 2 * E), F32), unroll=2)
        return (total[:E, :E] + total[E:, E:]) + (total[:E, E:] + total[E:, :E])

    def cov_times(i, target):
        rows = pl.ds(pl.multiple_of(i * 336, 16), 336)
        both = dot_b(chi[rows, :], target[...])
        return both[:, :E] + (both[:, E:] + dot_b(clo[rows, :], target[:, :E]))

    bg = gather_start(bc, 0)

    loads[3].wait()
    tp[...] = jnp.zeros_like(tp)
    tp[0:42, :] = tgt[...]
    first = (a * 8 + b) * 42
    t_high, t_rest = tp[...].astype(BF16), tp[...] - tp[...].astype(BF16).astype(F32)
    t_mid, t_low = halves(t_rest)
    t_all = jnp.concatenate([t_high, t_mid, t_low], axis=0)
    minus = -keys_half

    def current(j, carry):
        at = pl.multiple_of(j * 384, 128)
        place = lax.broadcasted_iota(jnp.int32, (48, 384), 1) + j * 384 - first
        mark = jnp.where(place == lax.broadcasted_iota(jnp.int32, (48, 384), 0), 1.0, 0.0).astype(BF16)
        value = dot_tb(minus, dw[:, pl.ds(at, 384)]) + dot_tb(t_all, jnp.concatenate([mark, mark, mark], axis=0))
        for i in range(3):
            part[j * 3 + i] = value[:, i * E : (i + 1) * E]
        return carry

    lax.fori_loop(0, 14, current, 0)
    for i in range(42, 48):
        part[i] = jnp.zeros((E, E), F32)
    real = pl.ds(0, 42)

    def half_of(kk):
        return pl.ds(pl.multiple_of(kk * 64, 8), 64)

    def rows_h(h):
        return pl.ds(pl.multiple_of(k * 64 + h * 32, 8), 32)

    def rows_z(h):
        return pl.ds(pl.multiple_of(k * 64 + h * 32 + z * 8, 8), 8)

    def rows_to(h, d):
        return pl.ds(pl.multiple_of(k * 64 + h * 32 + ((z + d) % 4) * 8, 8), 8)

    def twelve(t):
        return pl.ds(t * 12, 12)

    def three(t, u):
        return pl.ds(t * 12 + u * 3, 3)

    ways = ((0, x, dev_x, y, dev_y), (1, y, dev_y, x, dev_x))

    p1 = cp(part.at[real, half_of(1 - k)], rk, dev_k)
    bg = gather_next(bg, bc)
    p1.wait_recv()

    def add_half(i, carry):
        part[i, half_of(k), :] += rk[i]
        return carry

    lax.fori_loop(0, 42, add_half, 0)
    px = []
    for h, u, dev_u, _, _ in ways:
        px += to_three(lambda d: part.at[twelve((u + d) % 4), rows_h(h)], lambda d: xr.at[h, d - 1], dev_u)
    wait_all(bg)
    split_field(bc, bhl)

    def halve(ref, i, value):
        ref[i, 0] = value[:64]
        ref[i, 1] = value[64:]

    def cores_start(ref, n, got):
        return cp(ref.at[pl.ds(0, n), 1 - k], got.at[pl.ds(0, n)], dev_k)

    def cores_end(copy, ref, n, got):
        copy.wait_recv()
        ref[pl.ds(0, n), k] += got[pl.ds(0, n)]

    def axis_start(ref, n, got, dev):
        return to_three(lambda d: ref.at[pl.ds(0, n), k], lambda d: got.at[d - 1, pl.ds(0, n)], dev)

    def axis_end(copies, ref, n, got, target):
        wait_all(copies)
        target[pl.ds(0, n), k] = ref[pl.ds(0, n), k] + ((got[0, pl.ds(0, n)] + got[1, pl.ds(0, n)]) + got[2, pl.ds(0, n)])

    def cores_share(ref):
        return cp(ref.at[:, k], ref.at[:, k], dev_k)

    def first_image(i, carry):
        value = cov_times(i, bhl)
        vv[i, 0] = value[:PIECE]
        vv[i, 1] = value[PIECE:]
        return carry

    lax.fori_loop(0, 4, first_image, 0, unroll=2)
    v1 = cp(vv.at[:, 1 - k], vk, dev_k)
    v1.wait_recv()
    vv[:, k] += vk[...]
    vz = to_three(lambda d: vv.at[(z + d) % 4, k], lambda d: va.at[d - 1], dev_z)
    wait_all(px)
    py = []
    for h, u, _, w, dev_w in ways:
        part[twelve(u), rows_h(h)] += (xr[h, 0] + xr[h, 1]) + xr[h, 2]
        py += to_three(lambda d: part.at[three(u, (w + d) % 4), rows_h(h)], lambda d: yr.at[h, d - 1], dev_w)
    halve(m0, 0, gram(bhl, bhl))
    mk = cores_start(m0, 1, mc)
    wait_all(vz)
    piece[1] = vv[z, k] + ((va[0] + va[1]) + va[2])
    wg = gather_start(wc, 1)
    wr[z, k] = piece[1]
    wz = to_three(lambda d: wr.at[z, k], lambda d: wr.at[z, k], dev_z)
    wait_all(py)
    pz = []
    for h, u, _, w, _ in ways:
        part[three(u, w), rows_h(h)] += (yr[h, 0] + yr[h, 1]) + yr[h, 2]
        pz += to_three(lambda d: part.at[three(u, w), rows_to(h, d)], lambda d: zr.at[h, d - 1], dev_z)
    cores_end(mk, m0, 1, mc)
    mz = axis_start(m0, 1, mzr, dev_z)
    wg = gather_next(wg, wc)
    wait_all(pz)
    rz = []
    for h, u, _, w, _ in ways:
        res[three(u, w), rows_z(h)] = part[three(u, w), rows_z(h)] + ((zr[h, 0] + zr[h, 1]) + zr[h, 2])
        mine = res.at[three(u, w), rows_z(h)]
        rz += to_three(lambda d: mine, lambda d: mine, dev_z)
    wait_all(wz)
    wk = cp(wr.at[:, k], wr.at[:, k], dev_k)
    axis_end(mz, m0, 1, mzr, gsum)
    wait_all(rz)
    ry = []
    for h, u, _, w, dev_w in ways:
        block = res.at[three(u, w), rows_h(h)]
        ry += to_three(lambda d: block, lambda d: block, dev_w)
    wait_all(wg)
    split_field(wc, whl)
    halve(n12, 0, gram(bhl, whl))
    first_n = n12.at[pl.ds(0, 1)]
    nk = cores_start(first_n, 1, nc.at[pl.ds(0, 1)])
    wait_all(ry)
    rx = []
    for h, u, dev_u, _, _ in ways:
        lines = res.at[twelve(u), rows_h(h)]
        rx += to_three(lambda d: lines, lambda d: lines, dev_u)
    wk.wait_recv()

    def second_image(i, total):
        value = cov_times(i, whl)
        return total + dot_t(wr[i].reshape(336, E), value)

    total = lax.fori_loop(0, 2, second_image, jnp.zeros((E, E), F32), unroll=2)
    cores_end(nk, first_n, 1, nc.at[pl.ds(0, 1)])
    nz = axis_start(first_n, 1, nzr.at[0], dev_z)
    total = lax.fori_loop(2, 4, second_image, total, unroll=2)
    halve(n3, 0, total)
    n3k = cores_start(n3, 1, mc2)
    cores_end(n3k, n3, 1, mc2)
    n3z = axis_start(n3, 1, n3r.at[0], dev_z)
    axis_end(nz, first_n, 1, nzr.at[0], gsum.at[pl.ds(1, 1)])
    gs = cores_share(gsum.at[pl.ds(0, 2)])
    halve(n12, 1, gram(whl, whl))
    second_n = n12.at[pl.ds(1, 1)]
    nk = cores_start(second_n, 1, nc.at[pl.ds(1, 1)])
    gs.wait_recv()

    def whole(ref, i):
        return jnp.concatenate([ref[i, 0], ref[i, 1]], axis=0)

    gram0, n1 = sym(whole(gsum, 0)), sym(whole(gsum, 1))
    g11 = sym(n1 + dot(gram0, gram0))
    (inv1,) = sweep_some(2, g11)
    axis_end(n3z, n3, 1, n3r.at[0], n3.at[pl.ds(1, 1)])
    n3y = axis_start(n3.at[pl.ds(1, 1)], 1, n3r.at[1], dev_y)
    cores_end(nk, second_n, 1, nc.at[pl.ds(1, 1)])
    nz = axis_start(second_n, 1, nzr.at[1], dev_z)
    (inv1,) = sweep_some(6, inv1)
    axis_end(n3y, n3.at[pl.ds(1, 1)], 1, n3r.at[1], n3.at[pl.ds(2, 1)])
    n3x = axis_start(n3.at[pl.ds(2, 1)], 1, n3r.at[2], dev_x)
    axis_end(nz, second_n, 1, nzr.at[1], gsum.at[pl.ds(2, 1)])
    gs = cores_share(gsum.at[pl.ds(2, 1)])
    wait_all(rx)
    half = res.at[real, half_of(k)]
    rkk = cp(half, half, dev_k)
    (inv1,) = sweep_some(8, inv1)
    axis_end(n3x, n3.at[pl.ds(2, 1)], 1, n3r.at[2], n3.at[pl.ds(3, 1)])
    n3s = cores_share(n3.at[pl.ds(3, 1)])
    gs.wait_recv()
    g12 = sym(whole(gsum, 2)) + dot(gram0, n1)
    solved = dot(inv1, jnp.concatenate([g12, gram0], axis=1))
    taken = dot_t(g12, solved)
    g22 = dot(n1, n1)
    n3s.wait_recv()
    schur = sym(sym(whole(n3, 3)) + g22 - taken[:, :E])
    right2 = n1 - taken[:, E:]
    (inv2,) = sweep_some(16, schur)
    on_w = dot(inv2, right2)
    tmp[0] = dot(solved[:, :E], on_w)
    on_b = solved[:, E:] - tmp[0]
    fh, fl = halves(jnp.concatenate([piece[0], piece[1]], axis=1))
    ch, cl = halves(jnp.concatenate([on_b, on_w], axis=0))
    found = dot_b(fh, ch) + (dot_b(fh, cl) + dot_b(fl, ch))
    xh, xl = halves(found)
    xhh = jnp.concatenate([xh, xh], axis=1)
    rkk.wait_recv()

    def update(j, carry):
        right = jnp.concatenate([res[j * 2], res[j * 2 + 1]], axis=1)
        rh, rl = halves(right)
        value = dot_b(xhh, jnp.concatenate([rh, rl], axis=0)) + dot_b(xl, rh)
        out[:, pl.ds(pl.multiple_of(j * 256, 128), 256)] = value.astype(BF16)
        return carry

    lax.fori_loop(0, 21, update, 0, unroll=3)
    for copy in sent:
        copy.wait_send()


def body(states, subject_pos, gate_weight, up_weight, down_weight, covariance, targets):
    vmem = pl.BlockSpec(memory_space=pltpu.VMEM)
    anyw = pl.BlockSpec(memory_space=pl.ANY)
    small = lambda *dims: pltpu.VMEM(dims, F32)
    update = pl.pallas_call(
        kernel,
        out_shape=jax.ShapeDtypeStruct((PIECE, D), BF16),
        in_specs=[anyw, vmem, anyw, anyw, anyw, anyw, vmem],
        out_specs=vmem,
        scratch_shapes=[
            pltpu.VMEM((2, 8, 336, E), BF16),
            pltpu.VMEM((336, 2688), BF16),
            pltpu.VMEM((336, 2688), BF16),
            pltpu.VMEM((PIECE, D), BF16),
            small(2, LINES, E),
            small(2, 4, 4, PIECE, E),
            small(2, 4, 4, PIECE, E),
            small(2, 2, 4, PIECE, E),
            small(2, 2, 4, PIECE, E),
            small(2, 2, 4, PIECE, E),
            small(2, 3, 2, PIECE, E),
            pltpu.VMEM((1344, 2688), BF16),
            pltpu.VMEM((1344, 2688), BF16),
            small(2, PIECE, E),
            small(4, 4, PIECE, E),
            small(4, 4, PIECE, E),
            pltpu.VMEM((2688, 2 * E), BF16),
            pltpu.VMEM((2688, 2 * E), BF16),
            small(4, 2, PIECE, E),
            small(4, PIECE, E),
            small(3, PIECE, E),
            small(4, 2, PIECE, E),
            small(48, E, E),
            small(42, 64, E),
            small(2, 3, 12, 32, E),
            small(2, 3, 3, 32, E),
            small(2, 3, 3, 8, E),
            small(48, E, E),
            small(48, E),
            small(1, 2, 64, E),
            small(2, 2, 64, E),
            small(4, 2, 64, E),
            small(1, 64, E),
            small(2, 64, E),
            small(1, 64, E),
            small(3, 1, 64, E),
            small(2, 3, 1, 64, E),
            small(3, 3, 1, 64, E),
            small(3, 2, 64, E),
            small(1, E, E),
            pltpu.SemaphoreType.DMA((N_SEM,)),
            pltpu.SemaphoreType.DMA((N_SEM,)),
            pltpu.SemaphoreType.DMA((6,)),
        ],
        compiler_params=pltpu.CompilerParams(
            collective_id=0, has_side_effects=True, vmem_limit_bytes=60 * 1024 * 1024
        ),
        name="edit",
    )(
        jnp.transpose(states, (1, 2, 3, 0)),
        subject_pos.T,
        gate_weight.reshape(336, 2688),
        up_weight.reshape(336, 2688),
        down_weight.reshape(PIECE, D),
        covariance.reshape(1344 * 21, E),
        targets,
    )
    return update.reshape(1, 1, PIECE, D)


def solution(mesh):
    return jax.shard_map(
        body,
        mesh=mesh,
        in_specs=(
            P(None, None, None, "row"),
            P(),
            P("row", "col", None),
            P("row", "col", None),
            P("row", "col", None, None),
            P("row", "col", None),
            P(("row", "col"), None),
        ),
        out_specs=P("row", "col", None, None),
        check_vma=False,
    )
```
